128 devices in a mesh: seq: 16 (over y, z), store: 8 (over x, core).
Axes of the slice: x: 4, y: 4, z: 4, core: 2. Of those that a mesh axis runs over, the one named last changes fastest.
Arguments:
- hidden: bfloat16 [16384, 4096], P('seq'), may hold values from -6 to 6
- nbr_table: bfloat16 [64, 128, 896], P('store'), may hold values from -6 to 6
- nbr_ids: int32 [256, 2], P('seq'), may hold values from 0 to 63, as said below
- w_query: bfloat16 [4096, 4096], P(None, 'store'), may hold values from -0.09375 to 0.09375
- w_key: bfloat16 [896, 4096], P(None, 'store'), may hold values from -0.1875 to 0.1875
- w_value: bfloat16 [896, 4096], P(None, 'store'), may hold values from -0.1875 to 0.1875
- w_out: bfloat16 [4096, 4096], P('store'), may hold values from -0.125 to 0.125
- enc_query: bfloat16 [896, 896], replicated, may hold values from -0.1875 to 0.1875
- enc_key: bfloat16 [4096, 896], P('seq'), may hold values from -0.09375 to 0.09375
- enc_value: bfloat16 [4096, 896], P('seq'), may hold values from -0.09375 to 0.09375
- enc_out: bfloat16 [896, 896], replicated, may hold values from -0.1875 to 0.1875
Outputs:
- cross_out: bfloat16 [16384, 4096], P('seq', 'store')
The draws below stay inside these ranges and needn't reach their ends.
Inputs may be any that keep to these rules, and one draw needn't show every extreme that they name: `nbr_ids`: among the spans of one index of seq (16 consecutive spans), the ids fall in each owner's range k * 8 to k * 8 + 7 exactly 4 times.
All inputs are finite; a program needn't handle non-finite values.
Results may differ from the reference program's by a relative error of at most 0.03.
Values may be sent and summed in bfloat16 or wider, within the bound.
No kernel may reach another device: no remote copies, remote signals or barrier semaphores. Data moves between devices by JAX's collectives and lax.ppermute only.
A program may use at most 128 MiB of HBM per device.

```python
import math
import jax
import jax.numpy as jnp
from jax import lax

D = 4096
HEADS = 32
HD = 128
E = 896
EHEADS = 14
EHD = 64
CH = 64
NLEN = 128
KNB = 2
TOKENS = 16384
CPR = 16
SPANS = 256
ROW_REQ = 32
REQ = 4
BLK_DEV = 8
BLOCKS = 64
HG = 4
N_STORE = 8


def draw_nbr_ids(key, part):

    def one_shard(shard):
        shard_key = jax.random.fold_in(key, shard)
        order = jax.random.permutation(jax.random.fold_in(shard_key, 1), ROW_REQ)
        owners = order // REQ
        within = jax.random.randint(jax.random.fold_in(shard_key, 2), (ROW_REQ,), 0, BLK_DEV)
        within = jnp.where(order == 0, 0, jnp.where(order == ROW_REQ - 1, BLK_DEV - 1, within))
        return (owners * BLK_DEV + within).reshape(CPR, KNB)
    shards = jax.vmap(one_shard)(jnp.arange(SPANS // CPR, dtype=jnp.int32))
    return shards.reshape(SPANS, KNB).astype(jnp.int32)


def raised(array, own_key, source, target, parts, factor):
    owner, partner = [(jnp.arange(array.shape[axis_at]) // (array.shape[axis_at] // parts)).reshape([-1 if axis == axis_at else 1 for axis in range(array.ndim)]) for axis_at in (source, target)]
    chosen = jax.random.permutation(own_key, parts)[partner]
    strong = (owner == chosen) | (owner == (partner + parts // 2) % parts)
    return jnp.where(strong, factor * array, array)


def shard_levels(key, extent, split, least, largest):
    factor_of = 1.0
    for axis_at, blocks in split:
        draws = jax.random.uniform(jax.random.fold_in(jax.random.fold_in(key, 6), axis_at), (blocks,), jnp.float32, least / len(split), largest / len(split))
        factor_of = factor_of * jnp.repeat(jnp.exp(draws), extent[axis_at] // blocks).reshape((-1,) + (1,) * (len(extent) - 1 - axis_at))
    return factor_of


def centred(own_key, shape, width, limit, pieces=(), kind=jnp.bfloat16):
    result = jax.random.normal(own_key, shape, jnp.float32) * width
    if len(pieces) > 0:
        result = shard_levels(own_key, shape, pieces, -0.22, 0.18) * result
    return jnp.clip(result, min=-limit, max=limit).astype(kind)


def bell_draw_with(own_key, dims, width, most, cuts, heavy, kind=jnp.bfloat16):
    values = width * jax.random.normal(own_key, dims, jnp.float32)
    if cuts:
        values = values * shard_levels(own_key, dims, cuts, -0.22, 0.18)
    return jnp.clip(raised(values, jax.random.fold_in(own_key, 3), *heavy), -most, most).astype(kind)


def setup_inputs(seed: int = 0) -> dict:
    key_list = jax.random.split(jax.random.key(seed), 12)
    return {
        "hidden": centred(key_list[0], (TOKENS, D), 1.0, 6.0, ((0, 16),)),
        "nbr_table": centred(key_list[1], (BLOCKS, NLEN, E), 1.0, 6.0, ((0, 8),)),
        "nbr_ids": draw_nbr_ids(jax.random.fold_in(key_list[11], 71), 0),
        "w_query": centred(key_list[3], (D, D), D ** -0.5, 0.09375, ((1, 8),)),
        "w_key": centred(key_list[4], (E, D), E ** -0.5, 0.1875, ((1, 8),)),
        "w_value": centred(key_list[5], (E, D), E ** -0.5, 0.1875, ((1, 8),)),
        "w_out": bell_draw_with(key_list[6], (D, D), D ** -0.5, 0.125, ((0, 8),), (0, 1, 8, 2.0)),
        "enc_query": centred(key_list[7], (E, E), E ** -0.5, 0.1875),
        "enc_key": centred(key_list[8], (D, E), D ** -0.5, 0.09375, ((0, 16),)),
        "enc_value": centred(key_list[9], (D, E), D ** -0.5, 0.09375, ((0, 16),)),
        "enc_out": centred(key_list[10], (E, E), E ** -0.5, 0.1875),
    }


EPSILON = 1e-06

def encoder_block(sources, cond_keys, cond_values, enc_query, enc_out):
    count = sources.shape[0]
    source_f = sources.astype(jnp.float32)
    normed = (source_f * lax.rsqrt(lax.optimization_barrier(jnp.mean(source_f * source_f, axis=-1, keepdims=True)) + EPSILON)).astype(jnp.bfloat16)
    queries = jnp.dot(normed.reshape(count * NLEN, E), enc_query, preferred_element_type=jnp.float32).astype(jnp.bfloat16)
    queries = queries.reshape(count, NLEN, EHEADS, EHD)
    key_heads = cond_keys.reshape(count, CH, EHEADS, EHD)
    value_heads = cond_values.reshape(count, CH, EHEADS, EHD)
    scores = jnp.einsum('nqhd,nkhd->nhqk', queries.astype(jnp.float32), key_heads.astype(jnp.float32)) / math.sqrt(EHD)
    weights = jax.nn.softmax(scores, axis=-1).astype(jnp.bfloat16)
    mixed_heads = jnp.einsum('nhqk,nkhd->nqhd', weights.astype(jnp.float32), value_heads.astype(jnp.float32)).astype(jnp.bfloat16)
    branch = jnp.dot(mixed_heads.reshape(count * NLEN, E), enc_out, preferred_element_type=jnp.float32)
    return (source_f + branch.reshape(count, NLEN, E)).astype(jnp.bfloat16)

def reference(hidden, nbr_table, nbr_ids, w_query, w_key, w_value, w_out, enc_query, enc_key, enc_value, enc_out):
    cond_keys = jnp.dot(hidden, enc_key, preferred_element_type=jnp.float32).astype(jnp.bfloat16).reshape(SPANS, CH, E)
    cond_values = jnp.dot(hidden, enc_value, preferred_element_type=jnp.float32).astype(jnp.bfloat16).reshape(SPANS, CH, E)
    flat_ids = nbr_ids.reshape(-1).astype(jnp.int32)
    span_of = jnp.arange(SPANS * KNB, dtype=jnp.int32) // KNB
    encoded = encoder_block(nbr_table[flat_ids], cond_keys[span_of], cond_values[span_of], enc_query, enc_out)
    encoded = encoded.reshape(SPANS, KNB * NLEN, E)
    previous = jnp.concatenate([jnp.zeros((1, KNB * NLEN, E), jnp.bfloat16), encoded[:-1]], axis=0)
    queries = jnp.dot(hidden, w_query, preferred_element_type=jnp.float32).astype(jnp.bfloat16)
    queries = queries.reshape(SPANS, CH, HEADS, HD)

    def one_span(pair):
        query_heads, before = pair
        dec_keys = jnp.dot(before, w_key, preferred_element_type=jnp.float32).astype(jnp.bfloat16)
        dec_values = jnp.dot(before, w_value, preferred_element_type=jnp.float32).astype(jnp.bfloat16)
        key_heads = dec_keys.reshape(KNB * NLEN, HEADS, HD).astype(jnp.float32)
        value_heads = dec_values.reshape(KNB * NLEN, HEADS, HD).astype(jnp.float32)
        scores = jnp.einsum('qhd,khd->hqk', query_heads.astype(jnp.float32), key_heads) / math.sqrt(HD)
        weights = jax.nn.softmax(scores, axis=-1).astype(jnp.bfloat16)
        mixed_heads = jnp.einsum('hqk,khd->qhd', weights.astype(jnp.float32), value_heads)
        return mixed_heads.astype(jnp.bfloat16).reshape(CH, D)
    attended = lax.map(one_span, (queries, previous)).reshape(TOKENS, D)
    groups = attended.reshape(TOKENS, N_STORE, HG * HD)
    out_rows = w_out.reshape(N_STORE, HG * HD, D)
    running = jnp.zeros((TOKENS, D), jnp.float32)
    for group in range(N_STORE):
        term = jnp.dot(groups[:, group], out_rows[group], preferred_element_type=jnp.float32)
        running = running + term.astype(jnp.bfloat16).astype(jnp.float32)
    return running.astype(jnp.bfloat16)
```

```python
import math

import jax
import jax.numpy as jnp
from jax import lax
from jax.experimental import pallas as pl
from jax.experimental.pallas import tpu as pltpu
from jax.sharding import PartitionSpec as P

D = 4096
HD = 128
E = 896
EHEADS = 14
EHD = 64
CH = 64
NLEN = 128
KNB = 2
PAIRS = E // 128

EPSILON = 1e-06
F32 = jnp.float32
BF16 = jnp.bfloat16
REL = (0, -1, 1, 2)


def dot(a, b):
    return jnp.dot(a, b, preferred_element_type=F32)


def grid_route(side, dy, dz):
    return [
        (side * y + z, side * ((y + dy) % side) + (z + dz) % side)
        for y in range(side)
        for z in range(side)
    ]


def around(block, side, along_y):
    got = [block]
    for rel in REL[1:]:
        route = grid_route(side, -rel, 0) if along_y else grid_route(side, 0, -rel)
        got.append(lax.ppermute(block, "seq", route))
    return got


def cond_kernel(src_ref, span_ref, hidden_ref, *refs):
    a_refs, b_refs = refs[:4], refs[4:8]
    out_ref, held = refs[8], refs[9]
    step = pl.program_id(0)
    rows = hidden_ref.shape[0]
    total = None
    for i in range(4):
        for j in range(4):
            at = pl.multiple_of(src_ref[4 * i + j] * 256, 256)
            weight = jnp.concatenate([a_refs[i][j], b_refs[j][i]], axis=0)
            term = dot(hidden_ref[:, pl.ds(at, 256)], weight)
            total = term if total is None else total + term
    held[pl.ds(pl.multiple_of(step * rows, rows), rows), :] = total.astype(BF16)

    @pl.when(step == pl.num_programs(0) - 1)
    def _():
        for r in range(out_ref.shape[0]):
            at = pl.multiple_of(span_ref[r] * CH, CH)
            out_ref[r] = held[pl.ds(at, CH), :]


def cond_rows(hidden, a_parts, b_parts, sources, spans):
    tokens = hidden.shape[0]
    tile = 256
    requests = spans.shape[0]
    part = pl.BlockSpec((4, 128, 256), lambda i, s, p: (0, 0, 0), pipeline_mode=pl.Buffered(1))
    return pl.pallas_call(
        cond_kernel,
        out_shape=jax.ShapeDtypeStruct((requests, CH, 256), BF16),
        grid_spec=pltpu.PrefetchScalarGridSpec(
            num_scalar_prefetch=2,
            grid=(tokens // tile,),
            in_specs=[pl.BlockSpec((tile, D), lambda i, s, p: (i, 0))] + [part] * 8,
            out_specs=pl.BlockSpec((requests, CH, 256), lambda i, s, p: (0, 0, 0)),
            scratch_shapes=[pltpu.VMEM((tokens, 256), BF16)],
        ),
        compiler_params=pltpu.CompilerParams(
            dimension_semantics=("arbitrary",), vmem_limit_bytes=40 << 20
        ),
        cost_estimate=pl.CostEstimate(
            flops=2 * tokens * D * 256, bytes_accessed=12 << 20, transcendentals=0
        ),
        name="cond_rows",
    )(sources, spans, hidden, *a_parts, *b_parts)


def encode_kernel(query_ref, source_ref, cond_ref, out_w_ref, out_ref, mixed):
    row_head = lax.broadcasted_iota(jnp.int32, (128, 128), 0) // EHD
    col_head = lax.broadcasted_iota(jnp.int32, (128, 128), 1) // EHD
    same = row_head == col_head
    zero = jnp.zeros((128, 128), BF16)
    for p in range(PAIRS):
        keys = cond_ref[p, 0, :, :128]
        values = cond_ref[p, 0, :, 128:]
        key_pair = jnp.where(same, jnp.concatenate([keys, keys], axis=0), zero)
        value_pair = jnp.where(same, jnp.concatenate([values, values], axis=0), zero)
        query = query_ref[0, :, p * 128 : (p + 1) * 128]
        scores = lax.dot_general(
            key_pair, query, (((1,), (1,)), ((), ())), preferred_element_type=F32
        ) * (1.0 / math.sqrt(EHD))
        halves = []
        for h in range(2):
            part = scores[h * EHD : (h + 1) * EHD]
            grown = jnp.exp(part - jnp.max(part, axis=0, keepdims=True))
            halves.append((grown / jnp.sum(grown, axis=0, keepdims=True)).astype(BF16))
        weights = jnp.concatenate(halves, axis=0)
        got = lax.dot_general(
            weights, value_pair, (((0,), (0,)), ((), ())), preferred_element_type=F32
        )
        mixed[:, p * 128 : (p + 1) * 128] = got.astype(BF16)
    branch = dot(mixed[...], out_w_ref[...])
    out_ref[0] = (source_ref[0].astype(F32) + branch).astype(BF16)


def encode(enc_q, sources, cond, enc_out):
    count = sources.shape[0]
    return pl.pallas_call(
        encode_kernel,
        out_shape=jax.ShapeDtypeStruct((count, NLEN, E), BF16),
        grid=(count,),
        in_specs=[
            pl.BlockSpec((1, NLEN, E), lambda i: (i, 0, 0)),
            pl.BlockSpec((1, NLEN, E), lambda i: (i, 0, 0)),
            pl.BlockSpec((cond.shape[0], 1, CH, 256), lambda i: (0, i, 0, 0)),
            pl.BlockSpec((E, E), lambda i: (0, 0), pipeline_mode=pl.Buffered(1)),
        ],
        out_specs=pl.BlockSpec((1, NLEN, E), lambda i: (i, 0, 0)),
        scratch_shapes=[pltpu.VMEM((NLEN, E), BF16)],
        compiler_params=pltpu.CompilerParams(
            dimension_semantics=("arbitrary",), vmem_limit_bytes=24 << 20
        ),
        cost_estimate=pl.CostEstimate(
            flops=count * NLEN * E * E * 2, bytes_accessed=5 << 20, transcendentals=count << 17
        ),
        name="encode",
    )(enc_q, sources, cond, enc_out)


SPANS_STEP = 4


def decode_kernel(pos_ref, *refs):
    del pos_ref
    blocks = SPANS_STEP * KNB
    enc_refs = refs[:blocks]
    carried_ref, q_ref, wk_ref, wv_ref, wo_ref, out_ref, rows, att = refs[blocks:]
    step = pl.program_id(0)
    for m in range(blocks):
        if m < KNB:

            @pl.when(step == 0)
            def _():
                rows[m * NLEN : (m + 1) * NLEN, :] = carried_ref[m]

            @pl.when(step > 0)
            def _():
                rows[m * NLEN : (m + 1) * NLEN, :] = enc_refs[m][0]

        else:
            rows[m * NLEN : (m + 1) * NLEN, :] = enc_refs[m][0]
    width = q_ref.shape[1]
    length = KNB * NLEN
    for s in range(SPANS_STEP):
        block = rows[s * length : (s + 1) * length, :]
        keys = dot(block, wk_ref[...]).astype(BF16)
        values = dot(block, wv_ref[...]).astype(BF16)
        for h in range(width // HD):
            at = slice(h * HD, (h + 1) * HD)
            scores = lax.dot_general(
                q_ref[s * CH : (s + 1) * CH, at],
                keys[:, at],
                (((1,), (1,)), ((), ())),
                preferred_element_type=F32,
            ) * (1.0 / math.sqrt(HD))
            grown = jnp.exp(scores - jnp.max(scores, axis=-1, keepdims=True))
            weights = (grown / jnp.sum(grown, axis=-1, keepdims=True)).astype(BF16)
            att[s * CH : (s + 1) * CH, at] = dot(weights, values[:, at]).astype(BF16)
    chunk = 512
    for n in range(wo_ref.shape[1] // chunk):
        at = slice(n * chunk, (n + 1) * chunk)
        out_ref[:, at] = dot(att[...], wo_ref[:, at]).astype(BF16)


def decode(pos, encoded, carried, queries, w_key, w_value, w_out):
    tokens, width = queries.shape
    spans = tokens // CH
    steps = spans // SPANS_STEP
    blocks = SPANS_STEP * KNB
    tile = SPANS_STEP * CH

    def enc_spec(m):
        return pl.BlockSpec(
            (1, NLEN, E),
            lambda i, pos: (pos[jnp.maximum(i * blocks + m - KNB, 0)], 0, 0),
        )

    once = pl.Buffered(1)
    return pl.pallas_call(
        decode_kernel,
        out_shape=jax.ShapeDtypeStruct((tokens, D), BF16),
        grid_spec=pltpu.PrefetchScalarGridSpec(
            num_scalar_prefetch=1,
            grid=(steps,),
            in_specs=[enc_spec(m) for m in range(blocks)]
            + [
                pl.BlockSpec((KNB, NLEN, E), lambda i, pos: (0, 0, 0), pipeline_mode=once),
                pl.BlockSpec((tile, width), lambda i, pos: (i, 0)),
                pl.BlockSpec((E, width), lambda i, pos: (0, 0), pipeline_mode=once),
                pl.BlockSpec((E, width), lambda i, pos: (0, 0), pipeline_mode=once),
                pl.BlockSpec((width, D), lambda i, pos: (0, 0), pipeline_mode=once),
            ],
            out_specs=pl.BlockSpec((tile, D), lambda i, pos: (i, 0)),
            scratch_shapes=[
                pltpu.VMEM((blocks * NLEN, E), BF16),
                pltpu.VMEM((tile, width), BF16),
            ],
        ),
        compiler_params=pltpu.CompilerParams(
            dimension_semantics=("arbitrary",), vmem_limit_bytes=48 << 20
        ),
        cost_estimate=pl.CostEstimate(
            flops=2 * spans * KNB * NLEN * E * width * 2 + 2 * tokens * width * D,
            bytes_accessed=24 << 20,
            transcendentals=tokens * KNB * NLEN * (width // HD),
        ),
        name="decode",
    )(pos, *([encoded] * blocks), carried, queries, w_key, w_value, w_out)


def body(
    hidden,
    nbr_table,
    nbr_ids,
    w_query,
    w_key,
    w_value,
    w_out,
    enc_query,
    enc_key,
    enc_value,
    enc_out,
):
    store_count = lax.axis_size("store")
    store_rank = lax.axis_index("store")
    seq_count = lax.axis_size("seq")
    seq_rank = lax.axis_index("seq")
    side = math.isqrt(seq_count)
    span_count = nbr_ids.shape[0]
    row_requests = span_count * KNB
    per_owner = row_requests // store_count
    blocks_here = nbr_table.shape[0]

    pair_at = jnp.minimum(store_rank, PAIRS - 1) * 128
    weight = jnp.concatenate(
        [
            lax.dynamic_slice_in_dim(enc_key, pair_at, 128, axis=1),
            lax.dynamic_slice_in_dim(enc_value, pair_at, 128, axis=1),
        ],
        axis=1,
    )
    half = weight.shape[0] // 2
    a_four = jnp.stack(around(weight[:half], side, False))
    b_four = jnp.stack(around(weight[half:], side, True))
    a_parts = around(a_four, side, True)
    b_parts = around(b_four, side, False)
    y_at, z_at = seq_rank // side, seq_rank % side
    rel = jnp.array(REL, jnp.int32)
    from_rank = (
        side * ((y_at + rel + side) % side)[:, None] + ((z_at + rel + side) % side)[None, :]
    ).reshape(-1)

    flat_ids = nbr_ids.reshape(-1)
    slot = jnp.arange(row_requests, dtype=jnp.int32)
    rank_key = (flat_ids // blocks_here) * row_requests + slot
    pos = jnp.sum((rank_key[:, None] > rank_key[None, :]).astype(jnp.int32), axis=1)
    by_owner = jnp.sum(jnp.where(pos[None, :] == slot[:, None], slot[None, :], 0), axis=1)
    picked = lax.dynamic_slice_in_dim(by_owner, store_rank * per_owner, per_owner)
    sources = nbr_table[flat_ids[picked] % blocks_here]

    queries = dot(hidden, w_query).astype(BF16)
    source_f = sources.astype(F32)
    normed = (
        source_f * lax.rsqrt(jnp.mean(source_f * source_f, axis=-1, keepdims=True) + EPSILON)
    ).astype(BF16)
    enc_q = dot(normed.reshape(per_owner * NLEN, E), enc_query).astype(BF16)
    enc_q = enc_q.reshape(per_owner, NLEN, E)

    asked = cond_rows(hidden, a_parts, b_parts, from_rank, by_owner // KNB)
    asked = asked.reshape(store_count, per_owner, CH, 256)
    cond = lax.all_to_all(asked, "store", 0, 0, tiled=True)
    encoded = encode(enc_q, sources, cond, enc_out)
    gathered = lax.all_gather(encoded, "store", axis=0, tiled=True)
    last = gathered[lax.dynamic_slice_in_dim(pos, row_requests - KNB, KNB)]
    carried = lax.ppermute(last, "seq", [(i, i + 1) for i in range(seq_count - 1)])
    terms = decode(pos, gathered, carried, queries, w_key, w_value, w_out)
    return lax.psum_scatter(terms, "store", scatter_dimension=1, tiled=True)


def solution(mesh):
    in_specs = (
        P("seq", None),
        P("store", None, None),
        P("seq", None),
        P(None, "store"),
        P(None, "store"),
        P(None, "store"),
        P("store", None),
        P(),
        P("seq", None),
        P("seq", None),
        P(),
    )
    out_specs = P("seq", "store")
    return jax.shard_map(body, mesh=mesh, in_specs=in_specs, out_specs=out_specs, check_vma=False)
```

```python
import math

import jax
import jax.numpy as jnp
from jax import lax
from jax.experimental import pallas as pl
from jax.experimental.pallas import tpu as pltpu
from jax.sharding import PartitionSpec as P

D = 4096
HD = 128
E = 896
EHEADS = 14
EHD = 64
CH = 64
NLEN = 128
KNB = 2
PAIRS = E // 128

EPSILON = 1e-06
F32 = jnp.float32
BF16 = jnp.bfloat16
REL = (0, -1, 1, 2)
FIRST = 7


def dot(a, b):
    return jnp.dot(a, b, preferred_element_type=F32)


def grid_route(side, dy, dz):
    return [
        (side * y + z, side * ((y + dy) % side) + (z + dz) % side)
        for y in range(side)
        for z in range(side)
    ]


def around(block, side, along_y):
    got = [block]
    for rel in REL[1:]:
        route = grid_route(side, -rel, 0) if along_y else grid_route(side, 0, -rel)
        got.append(lax.ppermute(block, "seq", route))
    return got


def around_x(block, chips):
    got = [block]
    for rel in REL[1:]:
        route = [
            (2 * x + core, 2 * ((x - rel) % chips) + core) for x in range(chips) for core in range(2)
        ]
        got.append(lax.ppermute(block, "store", route))
    return got


def swap_cores(block):
    count = lax.axis_size("store")
    return lax.ppermute(block, "store", [(i, i ^ 1) for i in range(count)])


def once(shape):
    return pl.BlockSpec(shape, lambda *_: (0,) * len(shape), pipeline_mode=pl.Buffered(1))


def cond_kernel(src_ref, hidden_ref, *refs):
    a_refs, b_refs = refs[:4], refs[4:8]
    out_ref, held = refs[8], refs[9]
    step = pl.program_id(0)
    rows = hidden_ref.shape[0]
    total = None
    for i in range(4):
        for j in range(4):
            at = pl.multiple_of(src_ref[4 * i + j] * 256, 256)
            weight = jnp.concatenate([a_refs[i][j], b_refs[j][i]], axis=0)
            term = dot(hidden_ref[:, pl.ds(at, 256)], weight)
            total = term if total is None else total + term
    held[pl.ds(pl.multiple_of(step * rows, rows), rows), :] = total.astype(BF16)

    @pl.when(step == pl.num_programs(0) - 1)
    def _():
        tokens = held.shape[0]
        first = FIRST * CH
        out_ref[: tokens - first, :] = held[first:, :]
        out_ref[tokens - first :, :] = held[:first, :]


def cond_rows(hidden, a_parts, b_parts, ranks):
    tokens = hidden.shape[0]
    tile = 512
    return pl.pallas_call(
        cond_kernel,
        out_shape=jax.ShapeDtypeStruct((tokens, 256), BF16),
        grid_spec=pltpu.PrefetchScalarGridSpec(
            num_scalar_prefetch=1,
            grid=(tokens // tile,),
            in_specs=[pl.BlockSpec((tile, D), lambda i, s: (i, 0))] + [once((4, 128, 256))] * 8,
            out_specs=pl.BlockSpec((tokens, 256), lambda i, s: (0, 0)),
            scratch_shapes=[pltpu.VMEM((tokens, 256), BF16)],
        ),
        compiler_params=pltpu.CompilerParams(
            dimension_semantics=("arbitrary",), vmem_limit_bytes=32 << 20
        ),
        cost_estimate=pl.CostEstimate(
            flops=2 * tokens * D * 256, bytes_accessed=12 << 20, transcendentals=0
        ),
        name="cond_rows",
    )(ranks, hidden, *a_parts, *b_parts)


def enc_query_kernel(pos_ref, *refs):
    del pos_ref
    sources, (w_ref, out_ref) = refs[:4], refs[4:]
    rows = []
    for source in sources:
        block = source[0].astype(F32)
        scale = lax.rsqrt(jnp.mean(block * block, axis=-1, keepdims=True) + EPSILON)
        rows.append((block * scale).astype(BF16))
    got = dot(jnp.concatenate(rows, axis=0), w_ref[...]).astype(BF16)
    for n in range(4):
        out_ref[n] = got[n * NLEN : (n + 1) * NLEN]


def enc_queries(pos, gathered, weight):
    count = pos.shape[0]

    def source(n):
        return pl.BlockSpec((1, NLEN, E), lambda i, pos: (pos[4 * i + n], 0, 0))

    return pl.pallas_call(
        enc_query_kernel,
        out_shape=jax.ShapeDtypeStruct((count, NLEN, E), BF16),
        grid_spec=pltpu.PrefetchScalarGridSpec(
            num_scalar_prefetch=1,
            grid=(count // 4,),
            in_specs=[source(n) for n in range(4)] + [once((E, E))],
            out_specs=pl.BlockSpec((4, NLEN, E), lambda i, pos: (i, 0, 0)),
        ),
        compiler_params=pltpu.CompilerParams(
            dimension_semantics=("arbitrary",), vmem_limit_bytes=24 << 20
        ),
        cost_estimate=pl.CostEstimate(
            flops=2 * count * NLEN * E * E, bytes_accessed=10 << 20, transcendentals=0
        ),
        name="enc_queries",
    )(pos, *([gathered] * 4), weight)


def encode_kernel(pos_ref, pair_ref, *refs):
    del pos_ref
    sources, conds = refs[:4], refs[4:12]
    query_ref, out_w_ref, out_ref, mixed = refs[12:]
    row_head = lax.broadcasted_iota(jnp.int32, (128, 128), 0) // EHD
    col_head = lax.broadcasted_iota(jnp.int32, (128, 128), 1) // EHD
    same = row_head == col_head
    zero = jnp.zeros((128, 128), BF16)
    units = [(n, j) for n in range(4) for j in range(8)]

    def two_heads(block):
        return jnp.where(same, jnp.concatenate([block, block], axis=0), zero)

    def score(n, j):
        at = pl.multiple_of(jnp.minimum(pair_ref[j], PAIRS - 1) * 128, 128)
        return lax.dot_general(
            two_heads(conds[j][n, :, :128]),
            query_ref[n, :, pl.ds(at, 128)],
            (((1,), (1,)), ((), ())),
            preferred_element_type=F32,
        ) * (1.0 / math.sqrt(EHD))

    def soften(scores):
        halves = []
        for h in range(2):
            part = scores[h * EHD : (h + 1) * EHD]
            grown = jnp.exp(part - jnp.max(part, axis=0, keepdims=True))
            halves.append((grown * (1.0 / jnp.sum(grown, axis=0, keepdims=True))).astype(BF16))
        return jnp.concatenate(halves, axis=0)

    scores = [score(n, j) for n, j in units]
    weights = [soften(x) for x in scores]
    for weight, (n, j) in zip(weights, units):
        got = lax.dot_general(
            weight,
            two_heads(conds[j][n, :, 128:]),
            (((0,), (0,)), ((), ())),
            preferred_element_type=F32,
        )
        at = pl.multiple_of(pair_ref[j] * 128, 128)
        mixed[n * NLEN : (n + 1) * NLEN, pl.ds(at, 128)] = got.astype(BF16)
    branch = dot(mixed[:, :E], out_w_ref[...])
    for n in range(4):
        rows = branch[n * NLEN : (n + 1) * NLEN]
        out_ref[n] = (sources[n][0].astype(F32) + rows).astype(BF16)


def encode(base, count, pos, pairs, queries, gathered, conds, enc_out):
    first = base // 4

    def source(n):
        return pl.BlockSpec((1, NLEN, E), lambda i, pos, pairs: (pos[base + 4 * i + n], 0, 0))

    cond = pl.BlockSpec((4, CH, 256), lambda i, pos, pairs: (first + i, 0, 0))
    return pl.pallas_call(
        encode_kernel,
        out_shape=jax.ShapeDtypeStruct((count, NLEN, E), BF16),
        grid_spec=pltpu.PrefetchScalarGridSpec(
            num_scalar_prefetch=2,
            grid=(count // 4,),
            in_specs=[source(n) for n in range(4)]
            + [cond] * 8
            + [
                pl.BlockSpec((4, NLEN, E), lambda i, pos, pairs: (first + i, 0, 0)),
                once((E, E)),
            ],
            out_specs=pl.BlockSpec((4, NLEN, E), lambda i, pos, pairs: (i, 0, 0)),
            scratch_shapes=[pltpu.VMEM((4 * NLEN, 1024), BF16)],
        ),
        compiler_params=pltpu.CompilerParams(
            dimension_semantics=("arbitrary",), vmem_limit_bytes=32 << 20
        ),
        cost_estimate=pl.CostEstimate(
            flops=count * NLEN * E * E * 3, bytes_accessed=8 << 20, transcendentals=count << 17
        ),
        name="encode",
    )(pos, pairs, *([gathered] * 4), *conds, queries, enc_out)


SPANS_STEP = 4


def decode_kernel(carries, *refs):
    own_ref, other_ref, q_ref, wk_ref, wv_ref, wo_ref = refs[:6]
    out_ref, rows, att, ks, vs = refs[-5:]
    for j in range(SPANS_STEP):
        for n, ref in enumerate((own_ref, other_ref)):
            at = slice((KNB * j + n) * NLEN, (KNB * j + n + 1) * NLEN)
            rows[at, :] = ref[j]
    if carries:

        @pl.when(pl.program_id(0) == 0)
        def _():
            rows[:NLEN, :] = refs[6][0]
            rows[NLEN : 2 * NLEN, :] = refs[7][0]

    length = KNB * NLEN
    block = rows[...]
    ks[...] = dot(block, wk_ref[...]).astype(BF16)
    units = [(s, p) for s in range(SPANS_STEP) for p in range(q_ref.shape[1] // 256)]
    empty = jnp.zeros((CH, HD), BF16)
    weights = []
    scores = []
    for s, p in units:
        pair = q_ref[s * CH : (s + 1) * CH, p * 256 : (p + 1) * 256]
        both = jnp.concatenate(
            [
                jnp.concatenate([pair[:, :HD], empty], axis=1),
                jnp.concatenate([empty, pair[:, HD:]], axis=1),
            ],
            axis=0,
        )
        scores.append(
            lax.dot_general(
                ks[s * length : (s + 1) * length, p * 256 : (p + 1) * 256],
                both,
                (((1,), (1,)), ((), ())),
                preferred_element_type=F32,
            )
            * (1.0 / math.sqrt(HD))
        )
    for score in scores:
        grown = jnp.exp(score - jnp.max(score, axis=0, keepdims=True))
        weights.append((grown * (1.0 / jnp.sum(grown, axis=0, keepdims=True))).astype(BF16))
    vs[...] = dot(block, wv_ref[...]).astype(BF16)
    for weight, (s, p) in zip(weights, units):
        got = lax.dot_general(
            weight,
            vs[s * length : (s + 1) * length, p * 256 : (p + 1) * 256],
            (((0,), (0,)), ((), ())),
            preferred_element_type=F32,
        ).astype(BF16)
        att[s * CH : (s + 1) * CH, p * 256 : p * 256 + HD] = got[:CH, :HD]
        att[s * CH : (s + 1) * CH, p * 256 + HD : (p + 1) * 256] = got[CH:, HD:]
    chunk = 512
    for n in range(wo_ref.shape[1] // chunk):
        at = slice(n * chunk, (n + 1) * chunk)
        out_ref[:, at] = dot(att[...], wo_ref[:, at]).astype(BF16)


def decode(first_span, own, other, carried, terms, queries, w_key, w_value, w_out):
    tokens, width = queries.shape
    count = own.shape[0]
    tile = SPANS_STEP * CH
    first = first_span // SPANS_STEP
    rows = SPANS_STEP * KNB * NLEN
    block = pl.BlockSpec((SPANS_STEP, NLEN, E), lambda i: (i, 0, 0))
    operands = [own, other, queries, w_key, w_value, w_out, *carried]
    specs = [
        block,
        block,
        pl.BlockSpec((tile, width), lambda i: (first + i, 0)),
        once((E, width)),
        once((E, width)),
        once((width, D)),
    ] + [once((1, NLEN, E))] * len(carried)
    aliases = {}
    if terms is not None:
        aliases = {len(operands): 0}
        operands.append(terms)
        specs.append(pl.BlockSpec(memory_space=pl.ANY))
    return pl.pallas_call(
        lambda *refs: decode_kernel(len(carried) > 0, *refs),
        out_shape=jax.ShapeDtypeStruct((tokens, D), BF16),
        grid=(count // SPANS_STEP,),
        in_specs=specs,
        out_specs=pl.BlockSpec((tile, D), lambda i: (first + i, 0)),
        scratch_shapes=[
            pltpu.VMEM((rows, E), BF16),
            pltpu.VMEM((tile, width), BF16),
            pltpu.VMEM((rows, width), BF16),
            pltpu.VMEM((rows, width), BF16),
        ],
        input_output_aliases=aliases,
        compiler_params=pltpu.CompilerParams(
            dimension_semantics=("arbitrary",), vmem_limit_bytes=40 << 20
        ),
        cost_estimate=pl.CostEstimate(
            flops=4 * count * KNB * NLEN * E * width + 2 * count * CH * width * D,
            bytes_accessed=12 << 20,
            transcendentals=count * CH * KNB * NLEN * (width // HD),
        ),
        name="decode",
    )(*operands)


def body(
    hidden,
    nbr_table,
    nbr_ids,
    w_query,
    w_key,
    w_value,
    w_out,
    enc_query,
    enc_key,
    enc_value,
    enc_out,
):
    store_count = lax.axis_size("store")
    store_rank = lax.axis_index("store")
    seq_count = lax.axis_size("seq")
    seq_rank = lax.axis_index("seq")
    side = math.isqrt(seq_count)
    chips = store_count // 2
    span_count = nbr_ids.shape[0]
    row_requests = span_count * KNB
    per_owner = row_requests // store_count
    blocks_here = nbr_table.shape[0]

    flat_ids = nbr_ids.reshape(-1)
    slot = jnp.arange(row_requests, dtype=jnp.int32)
    rank_key = (flat_ids // blocks_here) * row_requests + slot
    pos = jnp.sum((rank_key[:, None] > rank_key[None, :]).astype(jnp.int32), axis=1)
    by_owner = jnp.sum(jnp.where(pos[None, :] == slot[:, None], slot[None, :], 0), axis=1)
    picked = lax.dynamic_slice_in_dim(by_owner, store_rank * per_owner, per_owner)
    sources = nbr_table[flat_ids[picked] % blocks_here]
    gathered = lax.all_gather(sources, "store", axis=0, tiled=True)

    pair_at = jnp.minimum(store_rank, PAIRS - 1) * 128
    weight = jnp.concatenate(
        [
            lax.dynamic_slice_in_dim(enc_key, pair_at, 128, axis=1),
            lax.dynamic_slice_in_dim(enc_value, pair_at, 128, axis=1),
        ],
        axis=1,
    )
    half = weight.shape[0] // 2
    a_four = jnp.stack(around(weight[:half], side, False))
    b_four = jnp.stack(around(weight[half:], side, True))
    a_parts = around(a_four, side, True)
    b_parts = around(b_four, side, False)
    y_at, z_at = seq_rank // side, seq_rank % side
    rel = jnp.array(REL, jnp.int32)
    from_rank = (
        side * ((y_at + rel + side) % side)[:, None] + ((z_at + rel + side) % side)[None, :]
    ).reshape(-1)
    cond = cond_rows(hidden, a_parts, b_parts, from_rank).reshape(span_count, CH, 256)
    own_lane = around_x(cond, chips)
    conds = own_lane + [swap_cores(block) for block in own_lane]
    chip, core = store_rank // 2, store_rank % 2
    lane = 2 * ((chip + rel + chips) % chips)
    pairs = jnp.concatenate([lane + core, lane + 1 - core])

    spans = (jnp.arange(span_count, dtype=jnp.int32) + FIRST) % span_count
    mine = jnp.sum(
        jnp.where(slot[None, :] == (KNB * spans + core)[:, None], pos[None, :], 0), axis=1
    )
    enc_q = enc_queries(mine, gathered, enc_query)
    queries = dot(hidden, w_query).astype(BF16)
    part = span_count // 2
    high = encode(0, part, mine, pairs, enc_q, gathered, conds, enc_out)
    low = encode(part, part, mine, pairs, enc_q, gathered, conds, enc_out)
    high_other = swap_cores(high)
    low_other = swap_cores(low)
    carried = lax.ppermute(low[:1], "seq", [(i, i + 1) for i in range(seq_count - 1)])
    carried_other = swap_cores(carried)
    terms = decode(part, high, high_other, (), None, queries, w_key, w_value, w_out)
    terms = decode(
        0, low, low_other, (carried, carried_other), terms, queries, w_key, w_value, w_out
    )
    return lax.psum_scatter(terms, "store", scatter_dimension=1, tiled=True)


def solution(mesh):
    in_specs = (
        P("seq", None),
        P("store", None, None),
        P("seq", None),
        P(None, "store"),
        P(None, "store"),
        P(None, "store"),
        P("store", None),
        P(),
        P("seq", None),
        P("seq", None),
        P(),
    )
    out_specs = P("seq", "store")
    return jax.shard_map(body, mesh=mesh, in_specs=in_specs, out_specs=out_specs, check_vma=False)
```

```python
import math

import jax
import jax.numpy as jnp
from jax import lax
from jax.experimental import pallas as pl
from jax.experimental.pallas import tpu as pltpu
from jax.sharding import PartitionSpec as P

D = 4096
HD = 128
E = 896
EHEADS = 14
EHD = 64
CH = 64
NLEN = 128
KNB = 2
PAIRS = E // 128

EPSILON = 1e-06
VMEM_LIMIT = 36 << 20
F32 = jnp.float32
BF16 = jnp.bfloat16
REL = (0, -1, 1, 2)
FIRST = 15


def dot(a, b):
    return jnp.dot(a, b, preferred_element_type=F32)


def grid_route(side, dy, dz):
    return [
        (side * y + z, side * ((y + dy) % side) + (z + dz) % side)
        for y in range(side)
        for z in range(side)
    ]


def around(block, side, along_y):
    got = [block]
    for rel in REL[1:]:
        route = grid_route(side, -rel, 0) if along_y else grid_route(side, 0, -rel)
        got.append(lax.ppermute(block, "seq", route))
    return got


def around_x(block, chips):
    got = [block]
    for rel in REL[1:]:
        route = [
            (2 * x + core, 2 * ((x - rel) % chips) + core) for x in range(chips) for core in range(2)
        ]
        got.append(lax.ppermute(block, "store", route))
    return got


def swap_cores(block):
    count = lax.axis_size("store")
    return lax.ppermute(block, "store", [(i, i ^ 1) for i in range(count)])


def once(shape):
    return pl.BlockSpec(shape, lambda *_: (0,) * len(shape), pipeline_mode=pl.Buffered(1))


def cond_kernel(src_ref, hidden_ref, *refs):
    a_refs, (b_ref, out_ref, held) = refs[:4], refs[4:]
    step = pl.program_id(0)
    rows = hidden_ref.shape[0]
    total = None
    for i in range(4):
        for j in range(4):
            rank = src_ref[4 * i + j]
            at = pl.multiple_of(rank * 256, 256)
            weight = jnp.concatenate([a_refs[i][j], b_ref[rank]], axis=0)
            term = dot(hidden_ref[:, pl.ds(at, 256)], weight)
            total = term if total is None else total + term
    held[pl.ds(pl.multiple_of(step * rows, rows), rows), :] = total.astype(BF16)

    @pl.when(step == pl.num_programs(0) - 1)
    def _():
        tokens = held.shape[0]
        first = FIRST * CH
        out_ref[: tokens - first, :] = held[first:, :]
        out_ref[tokens - first :, :] = held[:first, :]


def cond_rows(hidden, a_parts, b_all, ranks):
    tokens = hidden.shape[0]
    tile = 512
    return pl.pallas_call(
        cond_kernel,
        out_shape=jax.ShapeDtypeStruct((tokens, 256), BF16),
        grid_spec=pltpu.PrefetchScalarGridSpec(
            num_scalar_prefetch=1,
            grid=(tokens // tile,),
            in_specs=[pl.BlockSpec((tile, D), lambda i, s: (i, 0))] + [once((4, 128, 256))] * 4
            + [once(b_all.shape)],
            out_specs=pl.BlockSpec((tokens, 256), lambda i, s: (0, 0)),
            scratch_shapes=[pltpu.VMEM((tokens, 256), BF16)],
        ),
        compiler_params=pltpu.CompilerParams(
            dimension_semantics=("arbitrary",), vmem_limit_bytes=VMEM_LIMIT
        ),
        cost_estimate=pl.CostEstimate(
            flops=2 * tokens * D * 256, bytes_accessed=12 << 20, transcendentals=0
        ),
        name="cond_rows",
    )(ranks, hidden, *a_parts, b_all)


def enc_query_kernel(pos_ref, *refs):
    del pos_ref
    sources, w_ref, out_ref = refs[:4], refs[4], refs[-1]
    rows = []
    for source in sources:
        block = source[0].astype(F32)
        scale = lax.rsqrt(jnp.mean(block * block, axis=-1, keepdims=True) + EPSILON)
        rows.append((block * scale).astype(BF16))
    got = dot(jnp.concatenate(rows, axis=0), w_ref[...]).astype(BF16)
    for n in range(4):
        out_ref[n] = got[n * NLEN : (n + 1) * NLEN]


def enc_queries(pos, gathered, weight, after):
    count = pos.shape[0]

    def source(n):
        return pl.BlockSpec((1, NLEN, E), lambda i, pos: (pos[4 * i + n], 0, 0))

    return pl.pallas_call(
        enc_query_kernel,
        out_shape=jax.ShapeDtypeStruct((count, NLEN, E), BF16),
        grid_spec=pltpu.PrefetchScalarGridSpec(
            num_scalar_prefetch=1,
            grid=(count // 4,),
            in_specs=[source(n) for n in range(4)]
            + [once((E, E)), pl.BlockSpec(memory_space=pl.ANY)],
            out_specs=pl.BlockSpec((4, NLEN, E), lambda i, pos: (i, 0, 0)),
        ),
        compiler_params=pltpu.CompilerParams(
            dimension_semantics=("arbitrary",), vmem_limit_bytes=VMEM_LIMIT
        ),
        cost_estimate=pl.CostEstimate(
            flops=2 * count * NLEN * E * E, bytes_accessed=10 << 20, transcendentals=0
        ),
        name="enc_queries",
    )(pos, *([gathered] * 4), weight, after)


def encode_kernel(pos_ref, pair_ref, *refs):
    del pos_ref
    sources, conds = refs[:4], refs[4:12]
    query_ref, out_w_ref = refs[12:14]
    out_ref, mixed = refs[-2:]
    row_head = lax.broadcasted_iota(jnp.int32, (128, 128), 0) // EHD
    col_head = lax.broadcasted_iota(jnp.int32, (128, 128), 1) // EHD
    same = row_head == col_head
    zero = jnp.zeros((128, 128), BF16)
    units = [(n, j) for n in range(4) for j in range(8)]

    def two_heads(block):
        return jnp.where(same, jnp.concatenate([block, block], axis=0), zero)

    def score(n, j):
        at = pl.multiple_of(jnp.minimum(pair_ref[j], PAIRS - 1) * 128, 128)
        return lax.dot_general(
            two_heads(conds[j][n, :, :128]),
            query_ref[n, :, pl.ds(at, 128)],
            (((1,), (1,)), ((), ())),
            preferred_element_type=F32,
        ) * (1.0 / math.sqrt(EHD))

    def soften(scores):
        halves = []
        for h in range(2):
            part = scores[h * EHD : (h + 1) * EHD]
            grown = jnp.exp(part - jnp.max(part, axis=0, keepdims=True))
            halves.append((grown * (1.0 / jnp.sum(grown, axis=0, keepdims=True))).astype(BF16))
        return jnp.concatenate(halves, axis=0)

    scores = [score(n, j) for n, j in units]
    weights = [soften(x) for x in scores]
    for weight, (n, j) in zip(weights, units):
        got = lax.dot_general(
            weight,
            two_heads(conds[j][n, :, 128:]),
            (((0,), (0,)), ((), ())),
            preferred_element_type=F32,
        )
        at = pl.multiple_of(pair_ref[j] * 128, 128)
        mixed[n * NLEN : (n + 1) * NLEN, pl.ds(at, 128)] = got.astype(BF16)
    branch = dot(mixed[:, :E], out_w_ref[...])
    for n in range(4):
        rows = branch[n * NLEN : (n + 1) * NLEN]
        out_ref[n] = (sources[n][0].astype(F32) + rows).astype(BF16)


def encode(base, count, pos, pairs, queries, gathered, conds, enc_out, after=()):
    first = base // 4

    def source(n):
        return pl.BlockSpec((1, NLEN, E), lambda i, pos, pairs: (pos[base + 4 * i + n], 0, 0))

    cond = pl.BlockSpec((4, CH, 256), lambda i, pos, pairs: (first + i, 0, 0))
    return pl.pallas_call(
        encode_kernel,
        out_shape=(pltpu.HBM if after else jax.ShapeDtypeStruct)((count, NLEN, E), BF16),
        grid_spec=pltpu.PrefetchScalarGridSpec(
            num_scalar_prefetch=2,
            grid=(count // 4,),
            in_specs=[source(n) for n in range(4)]
            + [cond] * 8
            + [
                pl.BlockSpec((4, NLEN, E), lambda i, pos, pairs: (first + i, 0, 0)),
                once((E, E)),
            ]
            + [pl.BlockSpec(memory_space=pl.ANY)] * len(after),
            out_specs=pl.BlockSpec((4, NLEN, E), lambda i, pos, pairs: (i, 0, 0)),
            scratch_shapes=[pltpu.VMEM((4 * NLEN, 1024), BF16)],
        ),
        compiler_params=pltpu.CompilerParams(
            dimension_semantics=("arbitrary",), vmem_limit_bytes=VMEM_LIMIT
        ),
        cost_estimate=pl.CostEstimate(
            flops=count * NLEN * E * E * 3, bytes_accessed=8 << 20, transcendentals=count << 17
        ),
        name="encode",
    )(pos, pairs, *([gathered] * 4), *conds, queries, enc_out, *after)


SPANS_STEP = 4


def decode_kernel(carries, split, *refs):
    if split:
        block_ref, refs = refs[0], refs[1:]
    own_ref, other_ref, q_ref, wk_ref, wv_ref, wo_ref = refs[:6]
    rows, att, ks, vs = refs[-4:]
    for j in range(SPANS_STEP):
        for n, ref in enumerate((own_ref, other_ref)):
            at = slice((KNB * j + n) * NLEN, (KNB * j + n + 1) * NLEN)
            rows[at, :] = ref[j]
    if carries:

        @pl.when(pl.program_id(0) == 0)
        def _():
            rows[:NLEN, :] = refs[6][0]
            rows[NLEN : 2 * NLEN, :] = refs[7][0]

    length = KNB * NLEN
    block = rows[...]
    ks[...] = dot(block, wk_ref[...]).astype(BF16)
    units = [(s, p) for s in range(SPANS_STEP) for p in range(q_ref.shape[1] // 256)]
    empty = jnp.zeros((CH, HD), BF16)
    weights = []
    scores = []
    for s, p in units:
        pair = q_ref[s * CH : (s + 1) * CH, p * 256 : (p + 1) * 256]
        both = jnp.concatenate(
            [
                jnp.concatenate([pair[:, :HD], empty], axis=1),
                jnp.concatenate([empty, pair[:, HD:]], axis=1),
            ],
            axis=0,
        )
        scores.append(
            lax.dot_general(
                ks[s * length : (s + 1) * length, p * 256 : (p + 1) * 256],
                both,
                (((1,), (1,)), ((), ())),
                preferred_element_type=F32,
            )
            * (1.0 / math.sqrt(HD))
        )
    for score in scores:
        grown = jnp.exp(score - jnp.max(score, axis=0, keepdims=True))
        weights.append((grown * (1.0 / jnp.sum(grown, axis=0, keepdims=True))).astype(BF16))
    vs[...] = dot(block, wv_ref[...]).astype(BF16)
    for weight, (s, p) in zip(weights, units):
        got = lax.dot_general(
            weight,
            vs[s * length : (s + 1) * length, p * 256 : (p + 1) * 256],
            (((0,), (0,)), ((), ())),
            preferred_element_type=F32,
        ).astype(BF16)
        att[s * CH : (s + 1) * CH, p * 256 : p * 256 + HD] = got[:CH, :HD]
        att[s * CH : (s + 1) * CH, p * 256 + HD : (p + 1) * 256] = got[CH:, HD:]
    done = att[...]
    chunk = q_ref.shape[1]
    if split:
        for out_ref, first in ((refs[-6], 0), (refs[-5], 4)):
            for j in range(4):
                at = pl.multiple_of(block_ref[first + j] * chunk, chunk)
                out_ref[j] = dot(done, wo_ref[:, pl.ds(at, chunk)]).astype(BF16)
    else:
        for n in range(wo_ref.shape[1] // chunk):
            at = slice(n * chunk, (n + 1) * chunk)
            refs[-5][:, at] = dot(done, wo_ref[:, at]).astype(BF16)


def decode(first_span, own, other, queries, w_key, w_value, w_out, carried=(), blocks=None, after=()):
    split = blocks is not None
    width = queries.shape[1]
    count = own.shape[0]
    tokens = count * CH
    tile = SPANS_STEP * CH
    first = first_span // SPANS_STEP
    rows = SPANS_STEP * KNB * NLEN
    block = pl.BlockSpec((SPANS_STEP, NLEN, E), lambda i, *_: (i, 0, 0))
    if split:
        out_shape = [jax.ShapeDtypeStruct((4, tokens, width), BF16)] * 2
        out_specs = [pl.BlockSpec((4, tile, width), lambda i, *_: (0, i, 0))] * 2
    else:
        out_shape = pltpu.HBM((tokens, D), BF16)
        out_specs = pl.BlockSpec((tile, D), lambda i, *_: (i, 0))
    return pl.pallas_call(
        lambda *refs: decode_kernel(len(carried) > 0, split, *refs),
        out_shape=out_shape,
        grid_spec=pltpu.PrefetchScalarGridSpec(
            num_scalar_prefetch=int(split),
            grid=(count // SPANS_STEP,),
            in_specs=[
                block,
                block,
                pl.BlockSpec((tile, width), lambda i, *_: (first + i, 0)),
                once((E, width)),
                once((E, width)),
                once((width, D)),
            ]
            + [once((1, NLEN, E))] * len(carried)
            + [pl.BlockSpec(memory_space=pl.ANY)] * len(after),
            out_specs=out_specs,
            scratch_shapes=[
                pltpu.VMEM((rows, E), BF16),
                pltpu.VMEM((tile, width), BF16),
                pltpu.VMEM((rows, width), BF16),
                pltpu.VMEM((rows, width), BF16),
            ],
        ),
        compiler_params=pltpu.CompilerParams(
            dimension_semantics=("arbitrary",), vmem_limit_bytes=(60 << 20) if split else VMEM_LIMIT
        ),
        cost_estimate=pl.CostEstimate(
            flops=4 * count * KNB * NLEN * E * width + 2 * count * CH * width * D,
            bytes_accessed=12 << 20,
            transcendentals=count * CH * KNB * NLEN * (width // HD),
        ),
        name="decode",
    )(*([blocks] if split else []), own, other, queries, w_key, w_value, w_out, *carried, *after)


def body(
    hidden,
    nbr_table,
    nbr_ids,
    w_query,
    w_key,
    w_value,
    w_out,
    enc_query,
    enc_key,
    enc_value,
    enc_out,
):
    store_count = lax.axis_size("store")
    store_rank = lax.axis_index("store")
    seq_count = lax.axis_size("seq")
    seq_rank = lax.axis_index("seq")
    side = math.isqrt(seq_count)
    chips = store_count // 2
    span_count = nbr_ids.shape[0]
    row_requests = span_count * KNB
    per_owner = row_requests // store_count
    blocks_here = nbr_table.shape[0]

    flat_ids = nbr_ids.reshape(-1)
    slot = jnp.arange(row_requests, dtype=jnp.int32)
    rank_key = (flat_ids // blocks_here) * row_requests + slot
    pos = jnp.sum((rank_key[:, None] > rank_key[None, :]).astype(jnp.int32), axis=1)
    by_owner = jnp.sum(jnp.where(pos[None, :] == slot[:, None], slot[None, :], 0), axis=1)
    picked = lax.dynamic_slice_in_dim(by_owner, store_rank * per_owner, per_owner)
    sources = nbr_table[flat_ids[picked] % blocks_here]
    gathered = lax.all_gather(sources, "store", axis=0, tiled=True)
    gathered = pltpu.with_memory_space_constraint(gathered, pltpu.HBM)

    pair_at = jnp.minimum(store_rank, PAIRS - 1) * 128
    weight = jnp.concatenate(
        [
            lax.dynamic_slice_in_dim(enc_key, pair_at, 128, axis=1),
            lax.dynamic_slice_in_dim(enc_value, pair_at, 128, axis=1),
        ],
        axis=1,
    )
    half = weight.shape[0] // 2
    a_four = jnp.stack(around(weight[:half], side, False))
    a_parts = around(a_four, side, True)
    b_rows = jnp.broadcast_to(weight[half:][None], (seq_count, half, 256))
    b_all = lax.all_to_all(b_rows, "seq", 0, 0, tiled=True)
    y_at, z_at = seq_rank // side, seq_rank % side
    rel = jnp.array(REL, jnp.int32)
    from_rank = (
        side * ((y_at + rel + side) % side)[:, None] + ((z_at + rel + side) % side)[None, :]
    ).reshape(-1)
    cond = cond_rows(hidden, a_parts, b_all, from_rank).reshape(span_count, CH, 256)
    own_lane = around_x(cond, chips)
    conds = own_lane + [swap_cores(block) for block in own_lane]
    chip, core = store_rank // 2, store_rank % 2
    lane = 2 * ((chip + rel + chips) % chips)
    pairs = jnp.concatenate([lane + core, lane + 1 - core])

    spans = (jnp.arange(span_count, dtype=jnp.int32) + FIRST) % span_count
    mine = jnp.sum(
        jnp.where(slot[None, :] == (KNB * spans + core)[:, None], pos[None, :], 0), axis=1
    )
    queries = dot(hidden, w_query).astype(BF16)
    enc_q = enc_queries(mine, gathered, enc_query, queries)
    part = span_count // 2
    low = encode(0, part, mine, pairs, enc_q, gathered, conds, enc_out)
    low_other = swap_cores(low)
    carried, carried_other = (
        lax.ppermute(
            low[:1],
            ("seq", "store"),
            [
                (i * store_count + k, (i + 1) * store_count + (k ^ flip))
                for i in range(seq_count - 1)
                for k in range(store_count)
            ],
        )
        for flip in range(2)
    )
    high = encode(part, part, mine, pairs, enc_q, gathered, conds, enc_out, after=(low,))
    high_other = swap_cores(high)
    terms = decode(
        0,
        low,
        low_other,
        queries,
        w_key,
        w_value,
        w_out,
        carried=(carried, carried_other),
        after=(high,),
    )
    low_out = lax.psum_scatter(terms, "store", scatter_dimension=1, tiled=True)
    kept, given = decode(
        part, high, high_other, queries, w_key, w_value, w_out, blocks=pairs, after=(terms,)
    )
    taken = swap_cores(given)
    sums = [kept[j].astype(F32) + taken[j].astype(F32) for j in range(4)]
    high_out = sums[0]
    for j in range(1, 4):
        route = [
            (2 * x + k, 2 * ((x + REL[j]) % chips) + k) for x in range(chips) for k in range(2)
        ]
        high_out = high_out + lax.ppermute(sums[j].astype(BF16), "store", route).astype(F32)
    return jnp.concatenate([low_out, high_out.astype(BF16)], axis=0)


def solution(mesh):
    in_specs = (
        P("seq", None),
        P("store", None, None),
        P("seq", None),
        P(None, "store"),
        P(None, "store"),
        P(None, "store"),
        P("store", None),
        P(),
        P("seq", None),
        P("seq", None),
        P(),
    )
    out_specs = P("seq", "store")
    return jax.shard_map(body, mesh=mesh, in_specs=in_specs, out_specs=out_specs, check_vma=False)
```

```python
import math

import jax
import jax.numpy as jnp
from jax import lax
from jax.experimental import pallas as pl
from jax.experimental.pallas import tpu as pltpu
from jax.sharding import PartitionSpec as P

D = 4096
HD = 128
E = 896
EHEADS = 14
EHD = 64
CH = 64
NLEN = 128
KNB = 2
PAIRS = E // 128

EPSILON = 1e-06
VMEM_LIMIT = 36 << 20
F32 = jnp.float32
BF16 = jnp.bfloat16
REL = (0, -1, 1, 2)
FIRST = 15


def dot(a, b):
    return jnp.dot(a, b, preferred_element_type=F32)


def grid_route(side, dy, dz):
    return [
        (side * y + z, side * ((y + dy) % side) + (z + dz) % side)
        for y in range(side)
        for z in range(side)
    ]


def around(block, side, along_y):
    got = [block]
    for rel in REL[1:]:
        route = grid_route(side, -rel, 0) if along_y else grid_route(side, 0, -rel)
        got.append(lax.ppermute(block, "seq", route))
    return got


def around_x(block, chips):
    got = [block]
    for rel in REL[1:]:
        route = [
            (2 * x + core, 2 * ((x - rel) % chips) + core) for x in range(chips) for core in range(2)
        ]
        got.append(lax.ppermute(block, "store", route))
    return got


def swap_cores(block):
    count = lax.axis_size("store")
    return lax.ppermute(block, "store", [(i, i ^ 1) for i in range(count)])


def once(shape):
    return pl.BlockSpec(shape, lambda *_: (0,) * len(shape), pipeline_mode=pl.Buffered(1))


def cond_kernel(src_ref, hidden_ref, *refs):
    parts, (out_ref, total) = refs[:4], refs[-2:]
    step = pl.program_id(0)
    for i in range(4):

        @pl.when(step == i)
        def _():
            terms = None if i == 0 else total[...]
            for j in range(4):
                at = pl.multiple_of(src_ref[4 + j] * 256, 256)
                term = dot(hidden_ref[:, pl.ds(at, 256)], parts[i][j])
                terms = term if terms is None else terms + term
            if i == 3:
                last = terms.shape[0] - CH
                out_ref[:CH, :] = terms[last:].astype(BF16)
                out_ref[CH:, :] = terms[:last].astype(BF16)
            else:
                total[...] = terms


def cond_rows(hidden, parts, sources, after):
    tokens = hidden.shape[0]
    return pl.pallas_call(
        cond_kernel,
        out_shape=jax.ShapeDtypeStruct((tokens, 256), BF16),
        grid_spec=pltpu.PrefetchScalarGridSpec(
            num_scalar_prefetch=1,
            grid=(4,),
            in_specs=[pl.BlockSpec((tokens, D // 4), lambda i, s: (0, s[i]))]
            + [once((4, 256, 256))] * 4
            + [pl.BlockSpec(memory_space=pl.ANY)],
            out_specs=pl.BlockSpec((tokens, 256), lambda i, s: (0, 0)),
            scratch_shapes=[pltpu.VMEM((tokens, 256), F32)],
        ),
        compiler_params=pltpu.CompilerParams(
            dimension_semantics=("arbitrary",), vmem_limit_bytes=VMEM_LIMIT
        ),
        cost_estimate=pl.CostEstimate(
            flops=2 * tokens * D * 256, bytes_accessed=12 << 20, transcendentals=0
        ),
        name="cond_rows",
    )(sources, hidden, *parts, after)


def hold_kernel(block_ref, after_ref, out_ref):
    del after_ref
    out_ref[...] = block_ref[...]


def hold(block, after):
    return pl.pallas_call(
        hold_kernel,
        out_shape=jax.ShapeDtypeStruct(block.shape, BF16),
        in_specs=[
            pl.BlockSpec(memory_space=pltpu.VMEM),
            pl.BlockSpec(memory_space=pl.ANY),
        ],
        out_specs=pl.BlockSpec(memory_space=pltpu.VMEM),
        compiler_params=pltpu.CompilerParams(vmem_limit_bytes=4 << 20),
        cost_estimate=pl.CostEstimate(flops=0, bytes_accessed=1 << 20, transcendentals=0),
        name="hold",
    )(block, after)


def enc_query_kernel(pos_ref, *refs):
    del pos_ref
    sources, w_ref, out_ref = refs[:4], refs[4], refs[-1]
    rows = []
    for source in sources:
        block = source[0].astype(F32)
        scale = lax.rsqrt(jnp.mean(block * block, axis=-1, keepdims=True) + EPSILON)
        rows.append((block * scale).astype(BF16))
    got = dot(jnp.concatenate(rows, axis=0), w_ref[...]).astype(BF16)
    for n in range(4):
        out_ref[n] = got[n * NLEN : (n + 1) * NLEN]


def enc_queries(pos, gathered, weight):
    count = pos.shape[0]

    def source(n):
        return pl.BlockSpec((1, NLEN, E), lambda i, pos: (pos[4 * i + n], 0, 0))

    return pl.pallas_call(
        enc_query_kernel,
        out_shape=jax.ShapeDtypeStruct((count, NLEN, E), BF16),
        grid_spec=pltpu.PrefetchScalarGridSpec(
            num_scalar_prefetch=1,
            grid=(count // 4,),
            in_specs=[source(n) for n in range(4)] + [once((E, E))],
            out_specs=pl.BlockSpec((4, NLEN, E), lambda i, pos: (i, 0, 0)),
        ),
        compiler_params=pltpu.CompilerParams(
            dimension_semantics=("arbitrary",), vmem_limit_bytes=VMEM_LIMIT
        ),
        cost_estimate=pl.CostEstimate(
            flops=2 * count * NLEN * E * E, bytes_accessed=10 << 20, transcendentals=0
        ),
        name="enc_queries",
    )(pos, *([gathered] * 4), weight)


def encode_kernel(pos_ref, pair_ref, *refs):
    del pos_ref
    sources, conds = refs[:4], refs[4:12]
    query_ref, out_w_ref = refs[12:14]
    out_ref, mixed = refs[-2:]
    row_head = lax.broadcasted_iota(jnp.int32, (128, 128), 0) // EHD
    col_head = lax.broadcasted_iota(jnp.int32, (128, 128), 1) // EHD
    same = row_head == col_head
    zero = jnp.zeros((128, 128), BF16)
    units = [(n, j) for n in range(4) for j in range(8)]

    def two_heads(block):
        return jnp.where(same, jnp.concatenate([block, block], axis=0), zero)

    def score(n, j):
        at = pl.multiple_of(jnp.minimum(pair_ref[j], PAIRS - 1) * 128, 128)
        return lax.dot_general(
            two_heads(conds[j][n, :, :128]),
            query_ref[n, :, pl.ds(at, 128)],
            (((1,), (1,)), ((), ())),
            preferred_element_type=F32,
        ) * (1.0 / math.sqrt(EHD))

    def soften(scores):
        halves = []
        for h in range(2):
            part = scores[h * EHD : (h + 1) * EHD]
            grown = jnp.exp(part - jnp.max(part, axis=0, keepdims=True))
            halves.append((grown * (1.0 / jnp.sum(grown, axis=0, keepdims=True))).astype(BF16))
        return jnp.concatenate(halves, axis=0)

    scores = [score(n, j) for n, j in units]
    weights = [soften(x) for x in scores]
    for weight, (n, j) in zip(weights, units):
        got = lax.dot_general(
            weight,
            two_heads(conds[j][n, :, 128:]),
            (((0,), (0,)), ((), ())),
            preferred_element_type=F32,
        )
        at = pl.multiple_of(pair_ref[j] * 128, 128)
        mixed[n * NLEN : (n + 1) * NLEN, pl.ds(at, 128)] = got.astype(BF16)
    branch = dot(mixed[:, :E], out_w_ref[...])
    for n in range(4):
        rows = branch[n * NLEN : (n + 1) * NLEN]
        out_ref[n] = (sources[n][0].astype(F32) + rows).astype(BF16)


def encode(base, count, pos, pairs, queries, gathered, conds, enc_out, after):
    first = base // 4

    def source(n):
        return pl.BlockSpec((1, NLEN, E), lambda i, pos, pairs: (pos[base + 4 * i + n], 0, 0))

    cond = pl.BlockSpec((4, CH, 256), lambda i, pos, pairs: (first + i, 0, 0))
    return pl.pallas_call(
        encode_kernel,
        out_shape=(pltpu.HBM if base > 0 else jax.ShapeDtypeStruct)((count, NLEN, E), BF16),
        grid_spec=pltpu.PrefetchScalarGridSpec(
            num_scalar_prefetch=2,
            grid=(count // 4,),
            in_specs=[source(n) for n in range(4)]
            + [cond] * 8
            + [
                pl.BlockSpec((4, NLEN, E), lambda i, pos, pairs: (first + i, 0, 0)),
                once((E, E)),
            ]
            + [pl.BlockSpec(memory_space=pl.ANY)] * len(after),
            out_specs=pl.BlockSpec((4, NLEN, E), lambda i, pos, pairs: (i, 0, 0)),
            scratch_shapes=[pltpu.VMEM((4 * NLEN, 1024), BF16)],
        ),
        compiler_params=pltpu.CompilerParams(
            dimension_semantics=("arbitrary",), vmem_limit_bytes=VMEM_LIMIT
        ),
        cost_estimate=pl.CostEstimate(
            flops=count * NLEN * E * E * 3, bytes_accessed=8 << 20, transcendentals=count << 17
        ),
        name="encode",
    )(pos, pairs, *([gathered] * 4), *conds, queries, enc_out, *after)


SPANS_STEP = 4


def decode_kernel(carries, split, *refs):
    if split:
        block_ref, refs = refs[0], refs[1:]
    own_ref, other_ref, q_ref, wk_ref, wv_ref, wo_ref = refs[:6]
    rows, att, ks, vs = refs[-4:]
    for j in range(SPANS_STEP):
        for n, ref in enumerate((own_ref, other_ref)):
            at = slice((KNB * j + n) * NLEN, (KNB * j + n + 1) * NLEN)
            rows[at, :] = ref[j]
    if carries:

        @pl.when(pl.program_id(0) == 0)
        def _():
            rows[:NLEN, :] = refs[6][0]
            rows[NLEN : 2 * NLEN, :] = refs[7][0]

    length = KNB * NLEN
    block = rows[...]
    ks[...] = dot(block, wk_ref[...]).astype(BF16)
    units = [(s, p) for s in range(SPANS_STEP) for p in range(q_ref.shape[1] // 256)]
    empty = jnp.zeros((CH, HD), BF16)
    weights = []
    scores = []
    for s, p in units:
        pair = q_ref[s * CH : (s + 1) * CH, p * 256 : (p + 1) * 256]
        both = jnp.concatenate(
            [
                jnp.concatenate([pair[:, :HD], empty], axis=1),
                jnp.concatenate([empty, pair[:, HD:]], axis=1),
            ],
            axis=0,
        )
        scores.append(
            lax.dot_general(
                ks[s * length : (s + 1) * length, p * 256 : (p + 1) * 256],
                both,
                (((1,), (1,)), ((), ())),
                preferred_element_type=F32,
            )
            * (1.0 / math.sqrt(HD))
        )
    for score in scores:
        grown = jnp.exp(score - jnp.max(score, axis=0, keepdims=True))
        weights.append((grown * (1.0 / jnp.sum(grown, axis=0, keepdims=True))).astype(BF16))
    vs[...] = dot(block, wv_ref[...]).astype(BF16)
    for weight, (s, p) in zip(weights, units):
        got = lax.dot_general(
            weight,
            vs[s * length : (s + 1) * length, p * 256 : (p + 1) * 256],
            (((0,), (0,)), ((), ())),
            preferred_element_type=F32,
        ).astype(BF16)
        att[s * CH : (s + 1) * CH, p * 256 : p * 256 + HD] = got[:CH, :HD]
        att[s * CH : (s + 1) * CH, p * 256 + HD : (p + 1) * 256] = got[CH:, HD:]
    done = att[...]
    chunk = q_ref.shape[1]
    if split:
        for out_ref, first in ((refs[-6], 0), (refs[-5], 4)):
            for j in range(4):
                at = pl.multiple_of(block_ref[first + j] * chunk, chunk)
                out_ref[j] = dot(done, wo_ref[:, pl.ds(at, chunk)]).astype(BF16)
    else:
        for n in range(wo_ref.shape[1] // chunk):
            at = slice(n * chunk, (n + 1) * chunk)
            refs[-5][:, at] = dot(done, wo_ref[:, at]).astype(BF16)


def decode(first_span, own, other, queries, w_key, w_value, w_out, carried=(), blocks=None, after=()):
    split = blocks is not None
    width = queries.shape[1]
    count = own.shape[0]
    tokens = count * CH
    tile = SPANS_STEP * CH
    first = first_span // SPANS_STEP
    rows = SPANS_STEP * KNB * NLEN
    block = pl.BlockSpec((SPANS_STEP, NLEN, E), lambda i, *_: (i, 0, 0))
    if split:
        out_shape = [jax.ShapeDtypeStruct((4, tokens, width), BF16)] * 2
        out_specs = [pl.BlockSpec((4, tile, width), lambda i, *_: (0, i, 0))] * 2
    else:
        out_shape = pltpu.HBM((tokens, D), BF16)
        out_specs = pl.BlockSpec((tile, D), lambda i, *_: (i, 0))
    return pl.pallas_call(
        lambda *refs: decode_kernel(len(carried) > 0, split, *refs),
        out_shape=out_shape,
        grid_spec=pltpu.PrefetchScalarGridSpec(
            num_scalar_prefetch=int(split),
            grid=(count // SPANS_STEP,),
            in_specs=[
                block,
                block,
                pl.BlockSpec((tile, width), lambda i, *_: (first + i, 0)),
                once((E, width)),
                once((E, width)),
                once((width, D)),
            ]
            + [once((1, NLEN, E))] * len(carried)
            + [pl.BlockSpec(memory_space=pl.ANY)] * len(after),
            out_specs=out_specs,
            scratch_shapes=[
                pltpu.VMEM((rows, E), BF16),
                pltpu.VMEM((tile, width), BF16),
                pltpu.VMEM((rows, width), BF16),
                pltpu.VMEM((rows, width), BF16),
            ],
        ),
        compiler_params=pltpu.CompilerParams(
            dimension_semantics=("arbitrary",), vmem_limit_bytes=(60 << 20) if split else VMEM_LIMIT
        ),
        cost_estimate=pl.CostEstimate(
            flops=4 * count * KNB * NLEN * E * width + 2 * count * CH * width * D,
            bytes_accessed=12 << 20,
            transcendentals=count * CH * KNB * NLEN * (width // HD),
        ),
        name="decode",
    )(*([blocks] if split else []), own, other, queries, w_key, w_value, w_out, *carried, *after)


def body(
    hidden,
    nbr_table,
    nbr_ids,
    w_query,
    w_key,
    w_value,
    w_out,
    enc_query,
    enc_key,
    enc_value,
    enc_out,
):
    store_count = lax.axis_size("store")
    store_rank = lax.axis_index("store")
    seq_count = lax.axis_size("seq")
    seq_rank = lax.axis_index("seq")
    side = math.isqrt(seq_count)
    chips = store_count // 2
    span_count = nbr_ids.shape[0]
    row_requests = span_count * KNB
    per_owner = row_requests // store_count
    blocks_here = nbr_table.shape[0]

    flat_ids = nbr_ids.reshape(-1)
    slot = jnp.arange(row_requests, dtype=jnp.int32)
    rank_key = (flat_ids // blocks_here) * row_requests + slot
    pos = jnp.sum((rank_key[:, None] > rank_key[None, :]).astype(jnp.int32), axis=1)
    by_owner = jnp.sum(jnp.where(pos[None, :] == slot[:, None], slot[None, :], 0), axis=1)
    picked = lax.dynamic_slice_in_dim(by_owner, store_rank * per_owner, per_owner)
    sources = nbr_table[flat_ids[picked] % blocks_here]
    gathered = lax.all_gather(sources, "store", axis=0, tiled=True)
    gathered = pltpu.with_memory_space_constraint(gathered, pltpu.HBM)

    pair_at = jnp.minimum(store_rank, PAIRS - 1) * 128
    weight = jnp.concatenate(
        [
            lax.dynamic_slice_in_dim(enc_key, pair_at, 128, axis=1),
            lax.dynamic_slice_in_dim(enc_value, pair_at, 128, axis=1),
        ],
        axis=1,
    )
    row = jnp.stack(around(weight, side, False))
    parts = around(row, side, True)
    rel = jnp.array(REL, jnp.int32)
    y_at, z_at = seq_rank // side, seq_rank % side
    from_rank = jnp.concatenate([(y_at + rel + side) % side, (z_at + rel + side) % side])
    hidden_far = pltpu.with_memory_space_constraint(hidden, pltpu.HBM)
    queries = dot(hidden, w_query).astype(BF16)
    queries = pltpu.with_memory_space_constraint(queries, pltpu.HBM)
    cond = cond_rows(hidden_far, parts, from_rank, queries).reshape(-1, CH, 256)
    own_lane = around_x(cond, chips)
    chip, core = store_rank // 2, store_rank % 2
    lane = 2 * ((chip + rel + chips) % chips)
    pairs = jnp.concatenate([lane + core, lane + 1 - core])

    spans = (jnp.arange(span_count, dtype=jnp.int32) + FIRST) % span_count
    mine = jnp.sum(
        jnp.where(slot[None, :] == (KNB * spans + core)[:, None], pos[None, :], 0), axis=1
    )
    enc_query = pltpu.with_memory_space_constraint(enc_query, pltpu.HBM)
    enc_q = enc_queries(mine, gathered, enc_query)
    own_lane[1] = hold(own_lane[1], enc_q)
    conds = own_lane + [swap_cores(block) for block in own_lane]
    part = span_count // 2
    low = encode(0, part, mine, pairs, enc_q, gathered, conds, enc_out, ())
    low_other = swap_cores(low)
    carried, carried_other = (
        lax.ppermute(
            low[:1],
            ("seq", "store"),
            [
                (i * store_count + k, (i + 1) * store_count + (k ^ flip))
                for i in range(seq_count - 1)
                for k in range(store_count)
            ],
        )
        for flip in range(2)
    )
    high = encode(part, part, mine, pairs, enc_q, gathered, conds, enc_out, (low,))
    high_other = swap_cores(high)
    terms = decode(
        0,
        low,
        low_other,
        queries,
        w_key,
        w_value,
        w_out,
        carried=(carried, carried_other),
        after=(high,),
    )
    low_out = lax.psum_scatter(terms, "store", scatter_dimension=1, tiled=True)
    kept, given = decode(
        part, high, high_other, queries, w_key, w_value, w_out, blocks=pairs, after=(terms,)
    )
    taken = swap_cores(given)
    sums = [kept[j].astype(F32) + taken[j].astype(F32) for j in range(4)]
    high_out = sums[0]
    for j in range(1, 4):
        route = [
            (2 * x + k, 2 * ((x + REL[j]) % chips) + k) for x in range(chips) for k in range(2)
        ]
        high_out = high_out + lax.ppermute(sums[j].astype(BF16), "store", route).astype(F32)
    return jnp.concatenate([low_out, high_out.astype(BF16)], axis=0)


def solution(mesh):
    in_specs = (
        P("seq", None),
        P("store", None, None),
        P("seq", None),
        P(None, "store"),
        P(None, "store"),
        P(None, "store"),
        P("store", None),
        P(),
        P("seq", None),
        P("seq", None),
        P(),
    )
    out_specs = P("seq", "store")
    return jax.shard_map(body, mesh=mesh, in_specs=in_specs, out_specs=out_specs, check_vma=False)
```

```python
import math

import jax
import jax.numpy as jnp
from jax import lax
from jax.experimental import pallas as pl
from jax.experimental.pallas import tpu as pltpu
from jax.sharding import PartitionSpec as P

D = 4096
HD = 128
E = 896
EHEADS = 14
EHD = 64
CH = 64
NLEN = 128
KNB = 2
PAIRS = E // 128

EPSILON = 1e-06
VMEM_LIMIT = 36 << 20
F32 = jnp.float32
BF16 = jnp.bfloat16
REL = (0, -1, 1, 2)
FIRST = 15


def dot(a, b):
    return jnp.dot(a, b, preferred_element_type=F32)


def grid_route(side, dy, dz):
    return [
        (side * y + z, side * ((y + dy) % side) + (z + dz) % side)
        for y in range(side)
        for z in range(side)
    ]


def around(block, side, along_y):
    got = [block]
    for rel in REL[1:]:
        route = grid_route(side, -rel, 0) if along_y else grid_route(side, 0, -rel)
        got.append(lax.ppermute(block, "seq", route))
    return got


def around_x(block, chips):
    got = [block]
    for rel in REL[1:]:
        route = [
            (2 * x + core, 2 * ((x - rel) % chips) + core) for x in range(chips) for core in range(2)
        ]
        got.append(lax.ppermute(block, "store", route))
    return got


def swap_cores(block):
    count = lax.axis_size("store")
    return lax.ppermute(block, "store", [(i, i ^ 1) for i in range(count)])


def core_sums(kept, given):
    taken = swap_cores(given)
    sums = [kept[j].astype(F32) + taken[j].astype(F32) for j in range(4)]
    return sums[:1] + [block.astype(BF16) for block in sums[1:]]


def sum_over_x(sums, chips):
    total = sums[0]
    for j in range(1, 4):
        route = [
            (2 * x + core, 2 * ((x + REL[j]) % chips) + core) for x in range(chips) for core in range(2)
        ]
        total = total + lax.ppermute(sums[j], "store", route).astype(F32)
    return total


def once(shape):
    return pl.BlockSpec(shape, lambda *_: (0,) * len(shape), pipeline_mode=pl.Buffered(1))


def cond_kernel(src_ref, hidden_ref, *refs):
    a_refs, b_refs, (out_ref, total) = refs[:4], refs[4:8], refs[-2:]
    step = pl.program_id(0)
    for i in range(4):

        @pl.when(step == i)
        def _():
            terms = None if i == 0 else total[...]
            for j in range(4):
                at = pl.multiple_of(src_ref[4 + j] * 256, 256)
                weight = jnp.concatenate([a_refs[i][j], b_refs[j][i]], axis=0)
                term = dot(hidden_ref[:, pl.ds(at, 256)], weight)
                terms = term if terms is None else terms + term
            if i == 3:
                last = terms.shape[0] - CH
                out_ref[:CH, :] = terms[last:].astype(BF16)
                out_ref[CH:, :] = terms[:last].astype(BF16)
            else:
                total[...] = terms


def cond_rows(hidden, parts, sources, after):
    tokens = hidden.shape[0]
    return pl.pallas_call(
        cond_kernel,
        out_shape=jax.ShapeDtypeStruct((tokens, 256), BF16),
        grid_spec=pltpu.PrefetchScalarGridSpec(
            num_scalar_prefetch=1,
            grid=(4,),
            in_specs=[pl.BlockSpec((tokens, D // 4), lambda i, s: (0, s[i]))]
            + [once((4, 128, 256))] * 8
            + [pl.BlockSpec(memory_space=pl.ANY)],
            out_specs=pl.BlockSpec((tokens, 256), lambda i, s: (0, 0)),
            scratch_shapes=[pltpu.VMEM((tokens, 256), F32)],
        ),
        compiler_params=pltpu.CompilerParams(
            dimension_semantics=("arbitrary",), vmem_limit_bytes=VMEM_LIMIT
        ),
        cost_estimate=pl.CostEstimate(
            flops=2 * tokens * D * 256, bytes_accessed=12 << 20, transcendentals=0
        ),
        name="cond_rows",
    )(sources, hidden, *parts, after)


def hold_kernel(*refs):
    count = len(refs) // 2
    for source, target in zip(refs[:count], refs[count + 1 :]):
        target[...] = source[...]


def hold(blocks, after):
    count = len(blocks)
    vmem = pl.BlockSpec(memory_space=pltpu.VMEM)
    return pl.pallas_call(
        hold_kernel,
        out_shape=[jax.ShapeDtypeStruct(block.shape, BF16) for block in blocks],
        in_specs=[vmem] * count + [pl.BlockSpec(memory_space=pl.ANY)],
        out_specs=[vmem] * count,
        compiler_params=pltpu.CompilerParams(vmem_limit_bytes=8 << 20),
        cost_estimate=pl.CostEstimate(flops=0, bytes_accessed=1 << 20, transcendentals=0),
        name="hold",
    )(*blocks, after)


def stack_kernel(*refs):
    for j in range(4):
        refs[8][j] = refs[j][...]
        refs[9][j] = refs[4 + j][...]


def stack_fours(a, b):
    vmem = pl.BlockSpec(memory_space=pltpu.VMEM)
    shape = jax.ShapeDtypeStruct((4, *a[0].shape), BF16)
    return pl.pallas_call(
        stack_kernel,
        out_shape=[shape, shape],
        in_specs=[vmem] * 8,
        out_specs=[vmem] * 2,
        compiler_params=pltpu.CompilerParams(vmem_limit_bytes=8 << 20),
        cost_estimate=pl.CostEstimate(flops=0, bytes_accessed=1 << 20, transcendentals=0),
        name="stack_fours",
    )(*a, *b)


def enc_query_kernel(pos_ref, *refs):
    del pos_ref
    sources, w_ref, out_ref = refs[:4], refs[4], refs[-1]
    rows = []
    for source in sources:
        block = source[0].astype(F32)
        scale = lax.rsqrt(jnp.mean(block * block, axis=-1, keepdims=True) + EPSILON)
        rows.append((block * scale).astype(BF16))
    got = dot(jnp.concatenate(rows, axis=0), w_ref[...]).astype(BF16)
    for n in range(4):
        out_ref[n] = got[n * NLEN : (n + 1) * NLEN]


def enc_queries(pos, gathered, weight):
    count = pos.shape[0]

    def source(n):
        return pl.BlockSpec((1, NLEN, E), lambda i, pos: (pos[4 * i + n], 0, 0))

    return pl.pallas_call(
        enc_query_kernel,
        out_shape=jax.ShapeDtypeStruct((count, NLEN, E), BF16),
        grid_spec=pltpu.PrefetchScalarGridSpec(
            num_scalar_prefetch=1,
            grid=(count // 4,),
            in_specs=[source(n) for n in range(4)] + [once((E, E))],
            out_specs=pl.BlockSpec((4, NLEN, E), lambda i, pos: (i, 0, 0)),
        ),
        compiler_params=pltpu.CompilerParams(
            dimension_semantics=("arbitrary",), vmem_limit_bytes=VMEM_LIMIT
        ),
        cost_estimate=pl.CostEstimate(
            flops=2 * count * NLEN * E * E, bytes_accessed=10 << 20, transcendentals=0
        ),
        name="enc_queries",
    )(pos, *([gathered] * 4), weight)


def encode_kernel(pos_ref, pair_ref, *refs):
    del pos_ref
    sources, conds = refs[:4], refs[4:12]
    query_ref, out_w_ref = refs[12:14]
    out_ref, mixed = refs[-2:]
    row_head = lax.broadcasted_iota(jnp.int32, (128, 128), 0) // EHD
    col_head = lax.broadcasted_iota(jnp.int32, (128, 128), 1) // EHD
    same = row_head == col_head
    zero = jnp.zeros((128, 128), BF16)
    units = [(n, j) for n in range(4) for j in range(8)]

    def two_heads(block):
        return jnp.where(same, jnp.concatenate([block, block], axis=0), zero)

    def score(n, j):
        at = pl.multiple_of(jnp.minimum(pair_ref[j], PAIRS - 1) * 128, 128)
        return lax.dot_general(
            two_heads(conds[j][n, :, :128]),
            query_ref[n, :, pl.ds(at, 128)],
            (((1,), (1,)), ((), ())),
            preferred_element_type=F32,
        ) * (1.0 / math.sqrt(EHD))

    def soften(scores):
        halves = []
        for h in range(2):
            part = scores[h * EHD : (h + 1) * EHD]
            grown = jnp.exp(part - jnp.max(part, axis=0, keepdims=True))
            halves.append((grown * (1.0 / jnp.sum(grown, axis=0, keepdims=True))).astype(BF16))
        return jnp.concatenate(halves, axis=0)

    scores = [score(n, j) for n, j in units]
    weights = [soften(x) for x in scores]
    for weight, (n, j) in zip(weights, units):
        got = lax.dot_general(
            weight,
            two_heads(conds[j][n, :, 128:]),
            (((0,), (0,)), ((), ())),
            preferred_element_type=F32,
        )
        at = pl.multiple_of(pair_ref[j] * 128, 128)
        mixed[n * NLEN : (n + 1) * NLEN, pl.ds(at, 128)] = got.astype(BF16)
    branch = dot(mixed[:, :E], out_w_ref[...])
    for n in range(4):
        rows = branch[n * NLEN : (n + 1) * NLEN]
        out_ref[n] = (sources[n][0].astype(F32) + rows).astype(BF16)


def encode(base, count, pos, pairs, queries, gathered, conds, enc_out, after):
    first = base // 4

    def source(n):
        return pl.BlockSpec((1, NLEN, E), lambda i, pos, pairs: (pos[base + 4 * i + n], 0, 0))

    cond = pl.BlockSpec((4, CH, 256), lambda i, pos, pairs: (first + i, 0, 0))
    return pl.pallas_call(
        encode_kernel,
        out_shape=jax.ShapeDtypeStruct((count, NLEN, E), BF16),
        grid_spec=pltpu.PrefetchScalarGridSpec(
            num_scalar_prefetch=2,
            grid=(count // 4,),
            in_specs=[source(n) for n in range(4)]
            + [cond] * 8
            + [
                pl.BlockSpec((4, NLEN, E), lambda i, pos, pairs: (first + i, 0, 0)),
                once((E, E)),
            ]
            + [pl.BlockSpec(memory_space=pl.ANY)] * len(after),
            out_specs=pl.BlockSpec((4, NLEN, E), lambda i, pos, pairs: (i, 0, 0)),
            scratch_shapes=[pltpu.VMEM((4 * NLEN, 1024), BF16)],
        ),
        compiler_params=pltpu.CompilerParams(
            dimension_semantics=("arbitrary",), vmem_limit_bytes=VMEM_LIMIT
        ),
        cost_estimate=pl.CostEstimate(
            flops=count * NLEN * E * E * 3, bytes_accessed=8 << 20, transcendentals=count << 17
        ),
        name="encode",
    )(pos, pairs, *([gathered] * 4), *conds, queries, enc_out, *after)


SPANS_STEP = 4


def decode_kernel(carries, block_ref, *refs):
    own_ref, other_ref, q_ref, wk_ref, wv_ref, wo_ref = refs[:6]
    rows, att, ks, vs = refs[-4:]
    for j in range(SPANS_STEP):
        for n, ref in enumerate((own_ref, other_ref)):
            at = slice((KNB * j + n) * NLEN, (KNB * j + n + 1) * NLEN)
            rows[at, :] = ref[j]
    if carries:

        @pl.when(pl.program_id(0) == 0)
        def _():
            rows[:NLEN, :] = refs[6][0]
            rows[NLEN : 2 * NLEN, :] = refs[7][0]

    length = KNB * NLEN
    block = rows[...]
    ks[...] = dot(block, wk_ref[...]).astype(BF16)
    units = [(s, p) for s in range(SPANS_STEP) for p in range(q_ref.shape[1] // 256)]
    empty = jnp.zeros((CH, HD), BF16)
    weights = []
    scores = []
    for s, p in units:
        pair = q_ref[s * CH : (s + 1) * CH, p * 256 : (p + 1) * 256]
        both = jnp.concatenate(
            [
                jnp.concatenate([pair[:, :HD], empty], axis=1),
                jnp.concatenate([empty, pair[:, HD:]], axis=1),
            ],
            axis=0,
        )
        scores.append(
            lax.dot_general(
                ks[s * length : (s + 1) * length, p * 256 : (p + 1) * 256],
                both,
                (((1,), (1,)), ((), ())),
                preferred_element_type=F32,
            )
            * (1.0 / math.sqrt(HD))
        )
    for score in scores:
        grown = jnp.exp(score - jnp.max(score, axis=0, keepdims=True))
        weights.append((grown * (1.0 / jnp.sum(grown, axis=0, keepdims=True))).astype(BF16))
    vs[...] = dot(block, wv_ref[...]).astype(BF16)
    for weight, (s, p) in zip(weights, units):
        got = lax.dot_general(
            weight,
            vs[s * length : (s + 1) * length, p * 256 : (p + 1) * 256],
            (((0,), (0,)), ((), ())),
            preferred_element_type=F32,
        ).astype(BF16)
        att[s * CH : (s + 1) * CH, p * 256 : p * 256 + HD] = got[:CH, :HD]
        att[s * CH : (s + 1) * CH, p * 256 + HD : (p + 1) * 256] = got[CH:, HD:]
    done = att[...]
    chunk = q_ref.shape[1]
    for out_ref, first in ((refs[-6], 0), (refs[-5], 4)):
        for j in range(4):
            at = pl.multiple_of(block_ref[first + j] * chunk, chunk)
            out_ref[j] = dot(done, wo_ref[:, pl.ds(at, chunk)]).astype(BF16)


def decode(first_span, own, other, queries, w_key, w_value, w_out, blocks, carried=(), after=()):
    width = queries.shape[1]
    count = own.shape[0]
    tokens = count * CH
    tile = SPANS_STEP * CH
    first = first_span // SPANS_STEP
    rows = SPANS_STEP * KNB * NLEN
    block = pl.BlockSpec((SPANS_STEP, NLEN, E), lambda i, *_: (i, 0, 0))
    out_shape = [jax.ShapeDtypeStruct((4, tokens, width), BF16)] * 2
    out_specs = [pl.BlockSpec((4, tile, width), lambda i, *_: (0, i, 0))] * 2
    return pl.pallas_call(
        lambda *refs: decode_kernel(len(carried) > 0, *refs),
        out_shape=out_shape,
        grid_spec=pltpu.PrefetchScalarGridSpec(
            num_scalar_prefetch=1,
            grid=(count // SPANS_STEP,),
            in_specs=[
                block,
                block,
                pl.BlockSpec((tile, width), lambda i, *_: (first + i, 0)),
                once((E, width)),
                once((E, width)),
                once((width, D)),
            ]
            + [once((1, NLEN, E))] * len(carried)
            + [pl.BlockSpec(memory_space=pl.ANY)] * len(after),
            out_specs=out_specs,
            scratch_shapes=[
                pltpu.VMEM((rows, E), BF16),
                pltpu.VMEM((tile, width), BF16),
                pltpu.VMEM((rows, width), BF16),
                pltpu.VMEM((rows, width), BF16),
            ],
        ),
        compiler_params=pltpu.CompilerParams(
            dimension_semantics=("arbitrary",), vmem_limit_bytes=VMEM_LIMIT
        ),
        cost_estimate=pl.CostEstimate(
            flops=4 * count * KNB * NLEN * E * width + 2 * count * CH * width * D,
            bytes_accessed=12 << 20,
            transcendentals=count * CH * KNB * NLEN * (width // HD),
        ),
        name="decode",
    )(blocks, own, other, queries, w_key, w_value, w_out, *carried, *after)


def body(
    hidden,
    nbr_table,
    nbr_ids,
    w_query,
    w_key,
    w_value,
    w_out,
    enc_query,
    enc_key,
    enc_value,
    enc_out,
):
    store_count = lax.axis_size("store")
    store_rank = lax.axis_index("store")
    seq_count = lax.axis_size("seq")
    seq_rank = lax.axis_index("seq")
    side = math.isqrt(seq_count)
    chips = store_count // 2
    span_count = nbr_ids.shape[0]
    row_requests = span_count * KNB
    per_owner = row_requests // store_count
    blocks_here = nbr_table.shape[0]

    flat_ids = nbr_ids.reshape(-1)
    slot = jnp.arange(row_requests, dtype=jnp.int32)
    rank_key = (flat_ids // blocks_here) * row_requests + slot
    pos = jnp.sum((rank_key[:, None] > rank_key[None, :]).astype(jnp.int32), axis=1)
    by_owner = jnp.sum(jnp.where(pos[None, :] == slot[:, None], slot[None, :], 0), axis=1)
    picked = lax.dynamic_slice_in_dim(by_owner, store_rank * per_owner, per_owner)
    sources = nbr_table[flat_ids[picked] % blocks_here]
    gathered = lax.all_gather(sources, "store", axis=0, tiled=True)
    gathered = pltpu.with_memory_space_constraint(gathered, pltpu.HBM)

    pair_at = jnp.minimum(store_rank, PAIRS - 1) * 128
    weight = jnp.concatenate(
        [
            lax.dynamic_slice_in_dim(enc_key, pair_at, 128, axis=1),
            lax.dynamic_slice_in_dim(enc_value, pair_at, 128, axis=1),
        ],
        axis=1,
    )
    half = weight.shape[0] // 2
    a_four, b_four = stack_fours(
        around(weight[:half], side, False), around(weight[half:], side, True)
    )
    parts = around(a_four, side, True) + around(b_four, side, False)
    rel = jnp.array(REL, jnp.int32)
    y_at, z_at = seq_rank // side, seq_rank % side
    from_rank = jnp.concatenate([(y_at + rel + side) % side, (z_at + rel + side) % side])
    hidden_far = pltpu.with_memory_space_constraint(hidden, pltpu.HBM)
    queries = dot(hidden, w_query).astype(BF16)
    queries = pltpu.with_memory_space_constraint(queries, pltpu.HBM)
    cond = cond_rows(hidden_far, parts, from_rank, queries).reshape(-1, CH, 256)
    own_lane = around_x(cond, chips)
    chip, core = store_rank // 2, store_rank % 2
    lane = 2 * ((chip + rel + chips) % chips)
    pairs = jnp.concatenate([lane + core, lane + 1 - core])

    spans = (jnp.arange(span_count, dtype=jnp.int32) + FIRST) % span_count
    mine = jnp.sum(
        jnp.where(slot[None, :] == (KNB * spans + core)[:, None], pos[None, :], 0), axis=1
    )
    enc_query = pltpu.with_memory_space_constraint(enc_query, pltpu.HBM)
    enc_q = enc_queries(mine, gathered, enc_query)
    own_lane[1:] = hold(own_lane[1:], enc_q)
    conds = own_lane + [swap_cores(block) for block in own_lane]
    part = span_count // 2
    low = encode(0, part, mine, pairs, enc_q, gathered, conds, enc_out, ())
    low_other = swap_cores(low)
    carried, carried_other = (
        lax.ppermute(
            low[:1],
            ("seq", "store"),
            [
                (i * store_count + k, (i + 1) * store_count + (k ^ flip))
                for i in range(seq_count - 1)
                for k in range(store_count)
            ],
        )
        for flip in range(2)
    )
    high = encode(part, part, mine, pairs, enc_q, gathered, conds, enc_out, (low,))
    high_other = swap_cores(high)
    low_terms = decode(
        0,
        low,
        low_other,
        queries,
        w_key,
        w_value,
        w_out,
        pairs,
        carried=(carried, carried_other),
        after=(high,),
    )
    low_sums = core_sums(*low_terms)
    low_out = sum_over_x(low_sums, chips)
    high_terms = decode(
        part, high, high_other, queries, w_key, w_value, w_out, pairs, after=low_sums[1:]
    )
    high_out = sum_over_x(core_sums(*high_terms), chips)
    return jnp.concatenate([low_out, high_out], axis=0).astype(BF16)


def solution(mesh):
    in_specs = (
        P("seq", None),
        P("store", None, None),
        P("seq", None),
        P(None, "store"),
        P(None, "store"),
        P(None, "store"),
        P("store", None),
        P(),
        P("seq", None),
        P("seq", None),
        P(),
    )
    out_specs = P("seq", "store")
    return jax.shard_map(body, mesh=mesh, in_specs=in_specs, out_specs=out_specs, check_vma=False)
```

```python
import math

import jax
import jax.numpy as jnp
from jax import lax
from jax.experimental import pallas as pl
from jax.experimental.pallas import tpu as pltpu
from jax.sharding import PartitionSpec as P

D = 4096
HD = 128
E = 896
EHEADS = 14
EHD = 64
CH = 64
NLEN = 128
KNB = 2
PAIRS = E // 128

EPSILON = 1e-06
VMEM_LIMIT = 36 << 20
F32 = jnp.float32
BF16 = jnp.bfloat16
REL = (0, -1, 1, 2)
FIRST = 15


def dot(a, b):
    return jnp.dot(a, b, preferred_element_type=F32)


def grid_route(side, dy, dz):
    return [
        (side * y + z, side * ((y + dy) % side) + (z + dz) % side)
        for y in range(side)
        for z in range(side)
    ]


def around(block, side, along_y):
    got = [block]
    for rel in REL[1:]:
        route = grid_route(side, -rel, 0) if along_y else grid_route(side, 0, -rel)
        got.append(lax.ppermute(block, "seq", route))
    return got


def around_x(block, chips):
    got = [block]
    for rel in REL[1:]:
        route = [
            (2 * x + core, 2 * ((x - rel) % chips) + core) for x in range(chips) for core in range(2)
        ]
        got.append(lax.ppermute(block, "store", route))
    return got


def swap_cores(block):
    count = lax.axis_size("store")
    return lax.ppermute(block, "store", [(i, i ^ 1) for i in range(count)])


def add_kernel(kept_ref, taken_ref, *refs):
    for j, out_ref in enumerate(refs[-4:]):
        total = kept_ref[j].astype(F32) + taken_ref[j].astype(F32)
        out_ref[...] = total.astype(out_ref.dtype)


def core_sums(kept, taken, after):
    vmem = pl.BlockSpec(memory_space=pltpu.VMEM)
    shape = kept.shape[1:]
    return pl.pallas_call(
        add_kernel,
        out_shape=[jax.ShapeDtypeStruct(shape, F32)] + [jax.ShapeDtypeStruct(shape, BF16)] * 3,
        in_specs=[vmem] * 2 + [pl.BlockSpec(memory_space=pl.ANY)] * len(after),
        out_specs=[vmem] * 4,
        compiler_params=pltpu.CompilerParams(vmem_limit_bytes=8 << 20),
        cost_estimate=pl.CostEstimate(flops=1 << 19, bytes_accessed=4 << 20, transcendentals=0),
        name="core_sums",
    )(kept, taken, *after)


def send_over_x(sums, chips):
    got = []
    for j in range(1, 4):
        route = [
            (2 * x + core, 2 * ((x + REL[j]) % chips) + core)
            for x in range(chips)
            for core in range(2)
        ]
        got.append(lax.ppermute(sums[j], "store", route))
    return got


def once(shape):
    return pl.BlockSpec(shape, lambda *_: (0,) * len(shape), pipeline_mode=pl.Buffered(1))


def cond_kernel(src_ref, hidden_ref, *refs):
    a_refs, b_refs, (out_ref, total) = refs[:4], refs[4:8], refs[-2:]
    step = pl.program_id(0)
    for i in range(4):

        @pl.when(step == i)
        def _():
            terms = None if i == 0 else total[...]
            for j in range(4):
                at = pl.multiple_of(src_ref[4 + j] * 256, 256)
                weight = jnp.concatenate([a_refs[i][j], b_refs[j][i]], axis=0)
                term = dot(hidden_ref[:, pl.ds(at, 256)], weight)
                terms = term if terms is None else terms + term
            if i == 3:
                last = terms.shape[0] - CH
                out_ref[:CH, :] = terms[last:].astype(BF16)
                out_ref[CH:, :] = terms[:last].astype(BF16)
            else:
                total[...] = terms


def cond_rows(hidden, parts, sources, after):
    tokens = hidden.shape[0]
    return pl.pallas_call(
        cond_kernel,
        out_shape=jax.ShapeDtypeStruct((tokens, 256), BF16),
        grid_spec=pltpu.PrefetchScalarGridSpec(
            num_scalar_prefetch=1,
            grid=(4,),
            in_specs=[pl.BlockSpec((tokens, D // 4), lambda i, s: (0, s[i]))]
            + [once((4, 128, 256))] * 8
            + [pl.BlockSpec(memory_space=pl.ANY)],
            out_specs=pl.BlockSpec((tokens, 256), lambda i, s: (0, 0)),
            scratch_shapes=[pltpu.VMEM((tokens, 256), F32)],
        ),
        compiler_params=pltpu.CompilerParams(
            dimension_semantics=("arbitrary",), vmem_limit_bytes=VMEM_LIMIT
        ),
        cost_estimate=pl.CostEstimate(
            flops=2 * tokens * D * 256, bytes_accessed=12 << 20, transcendentals=0
        ),
        name="cond_rows",
    )(sources, hidden, *parts, after)


def hold_kernel(*refs):
    count = len(refs) // 2
    for source, target in zip(refs[:count], refs[count + 1 :]):
        target[...] = source[...]


def hold(blocks, after):
    count = len(blocks)
    vmem = pl.BlockSpec(memory_space=pltpu.VMEM)
    return pl.pallas_call(
        hold_kernel,
        out_shape=[jax.ShapeDtypeStruct(block.shape, BF16) for block in blocks],
        in_specs=[vmem] * count + [pl.BlockSpec(memory_space=pl.ANY)],
        out_specs=[vmem] * count,
        compiler_params=pltpu.CompilerParams(vmem_limit_bytes=8 << 20),
        cost_estimate=pl.CostEstimate(flops=0, bytes_accessed=1 << 20, transcendentals=0),
        name="hold",
    )(*blocks, after)


def stack_kernel(*refs):
    for j in range(4):
        refs[8][j] = refs[j][...]
        refs[9][j] = refs[4 + j][...]


def stack_fours(a, b):
    vmem = pl.BlockSpec(memory_space=pltpu.VMEM)
    shape = jax.ShapeDtypeStruct((4, *a[0].shape), BF16)
    return pl.pallas_call(
        stack_kernel,
        out_shape=[shape, shape],
        in_specs=[vmem] * 8,
        out_specs=[vmem] * 2,
        compiler_params=pltpu.CompilerParams(vmem_limit_bytes=8 << 20),
        cost_estimate=pl.CostEstimate(flops=0, bytes_accessed=1 << 20, transcendentals=0),
        name="stack_fours",
    )(*a, *b)


def enc_query_kernel(pos_ref, *refs):
    del pos_ref
    sources, w_ref, out_ref = refs[:4], refs[4], refs[-1]
    rows = []
    for source in sources:
        block = source[0].astype(F32)
        scale = lax.rsqrt(jnp.mean(block * block, axis=-1, keepdims=True) + EPSILON)
        rows.append((block * scale).astype(BF16))
    got = dot(jnp.concatenate(rows, axis=0), w_ref[...]).astype(BF16)
    for n in range(4):
        out_ref[n] = got[n * NLEN : (n + 1) * NLEN]


def enc_queries(pos, gathered, weight):
    count = pos.shape[0]

    def source(n):
        return pl.BlockSpec((1, NLEN, E), lambda i, pos: (pos[4 * i + n], 0, 0))

    return pl.pallas_call(
        enc_query_kernel,
        out_shape=jax.ShapeDtypeStruct((count, NLEN, E), BF16),
        grid_spec=pltpu.PrefetchScalarGridSpec(
            num_scalar_prefetch=1,
            grid=(count // 4,),
            in_specs=[source(n) for n in range(4)] + [once((E, E))],
            out_specs=pl.BlockSpec((4, NLEN, E), lambda i, pos: (i, 0, 0)),
        ),
        compiler_params=pltpu.CompilerParams(
            dimension_semantics=("arbitrary",), vmem_limit_bytes=VMEM_LIMIT
        ),
        cost_estimate=pl.CostEstimate(
            flops=2 * count * NLEN * E * E, bytes_accessed=10 << 20, transcendentals=0
        ),
        name="enc_queries",
    )(pos, *([gathered] * 4), weight)


def encode_kernel(pos_ref, pair_ref, *refs):
    del pos_ref
    sources, conds = refs[:4], refs[4:12]
    query_ref, out_w_ref = refs[12:14]
    out_ref, mixed = refs[-2:]
    row_head = lax.broadcasted_iota(jnp.int32, (128, 128), 0) // EHD
    col_head = lax.broadcasted_iota(jnp.int32, (128, 128), 1) // EHD
    same = row_head == col_head
    zero = jnp.zeros((128, 128), BF16)
    units = [(n, j) for n in range(4) for j in range(8)]

    def two_heads(block):
        return jnp.where(same, jnp.concatenate([block, block], axis=0), zero)

    def score(n, j):
        at = pl.multiple_of(jnp.minimum(pair_ref[j], PAIRS - 1) * 128, 128)
        return lax.dot_general(
            two_heads(conds[j][n, :, :128]),
            query_ref[n, :, pl.ds(at, 128)],
            (((1,), (1,)), ((), ())),
            preferred_element_type=F32,
        ) * (1.0 / math.sqrt(EHD))

    def soften(scores):
        halves = []
        for h in range(2):
            part = scores[h * EHD : (h + 1) * EHD]
            grown = jnp.exp(part - jnp.max(part, axis=0, keepdims=True))
            halves.append((grown * (1.0 / jnp.sum(grown, axis=0, keepdims=True))).astype(BF16))
        return jnp.concatenate(halves, axis=0)

    scores = [score(n, j) for n, j in units]
    weights = [soften(x) for x in scores]
    for weight, (n, j) in zip(weights, units):
        got = lax.dot_general(
            weight,
            two_heads(conds[j][n, :, 128:]),
            (((0,), (0,)), ((), ())),
            preferred_element_type=F32,
        )
        at = pl.multiple_of(pair_ref[j] * 128, 128)
        mixed[n * NLEN : (n + 1) * NLEN, pl.ds(at, 128)] = got.astype(BF16)
    branch = dot(mixed[:, :E], out_w_ref[...])
    for n in range(4):
        rows = branch[n * NLEN : (n + 1) * NLEN]
        out_ref[n] = (sources[n][0].astype(F32) + rows).astype(BF16)


def encode(base, count, pos, pairs, queries, gathered, conds, enc_out, after):
    first = base // 4

    def source(n):
        return pl.BlockSpec((1, NLEN, E), lambda i, pos, pairs: (pos[base + 4 * i + n], 0, 0))

    cond = pl.BlockSpec((4, CH, 256), lambda i, pos, pairs: (first + i, 0, 0))
    return pl.pallas_call(
        encode_kernel,
        out_shape=jax.ShapeDtypeStruct((count, NLEN, E), BF16),
        grid_spec=pltpu.PrefetchScalarGridSpec(
            num_scalar_prefetch=2,
            grid=(count // 4,),
            in_specs=[source(n) for n in range(4)]
            + [cond] * 8
            + [
                pl.BlockSpec((4, NLEN, E), lambda i, pos, pairs: (first + i, 0, 0)),
                once((E, E)),
            ]
            + [pl.BlockSpec(memory_space=pl.ANY)] * len(after),
            out_specs=pl.BlockSpec((4, NLEN, E), lambda i, pos, pairs: (i, 0, 0)),
            scratch_shapes=[pltpu.VMEM((4 * NLEN, 1024), BF16)],
        ),
        compiler_params=pltpu.CompilerParams(
            dimension_semantics=("arbitrary",), vmem_limit_bytes=VMEM_LIMIT
        ),
        cost_estimate=pl.CostEstimate(
            flops=count * NLEN * E * E * 3, bytes_accessed=8 << 20, transcendentals=count << 17
        ),
        name="encode",
    )(pos, pairs, *([gathered] * 4), *conds, queries, enc_out, *after)


SPANS_STEP = 4


def decode_kernel(carries, block_ref, *refs):
    own_ref, other_ref, q_ref, wk_ref, wv_ref, wo_ref = refs[:6]
    rows, att, ks, vs = refs[-4:]
    for j in range(SPANS_STEP):
        for n, ref in enumerate((own_ref, other_ref)):
            at = slice((KNB * j + n) * NLEN, (KNB * j + n + 1) * NLEN)
            rows[at, :] = ref[j]
    if carries:

        @pl.when(pl.program_id(0) == 0)
        def _():
            rows[:NLEN, :] = refs[6][0]
            rows[NLEN : 2 * NLEN, :] = refs[7][0]

    length = KNB * NLEN
    block = rows[...]
    ks[...] = dot(block, wk_ref[...]).astype(BF16)
    units = [(s, p) for s in range(SPANS_STEP) for p in range(q_ref.shape[1] // 256)]
    empty = jnp.zeros((CH, HD), BF16)
    weights = []
    scores = []
    for s, p in units:
        pair = q_ref[s * CH : (s + 1) * CH, p * 256 : (p + 1) * 256]
        both = jnp.concatenate(
            [
                jnp.concatenate([pair[:, :HD], empty], axis=1),
                jnp.concatenate([empty, pair[:, HD:]], axis=1),
            ],
            axis=0,
        )
        scores.append(
            lax.dot_general(
                ks[s * length : (s + 1) * length, p * 256 : (p + 1) * 256],
                both,
                (((1,), (1,)), ((), ())),
                preferred_element_type=F32,
            )
            * (1.0 / math.sqrt(HD))
        )
    for score in scores:
        grown = jnp.exp(score - jnp.max(score, axis=0, keepdims=True))
        weights.append((grown * (1.0 / jnp.sum(grown, axis=0, keepdims=True))).astype(BF16))
    vs[...] = dot(block, wv_ref[...]).astype(BF16)
    for weight, (s, p) in zip(weights, units):
        got = lax.dot_general(
            weight,
            vs[s * length : (s + 1) * length, p * 256 : (p + 1) * 256],
            (((0,), (0,)), ((), ())),
            preferred_element_type=F32,
        ).astype(BF16)
        att[s * CH : (s + 1) * CH, p * 256 : p * 256 + HD] = got[:CH, :HD]
        att[s * CH : (s + 1) * CH, p * 256 + HD : (p + 1) * 256] = got[CH:, HD:]
    done = att[...]
    chunk = q_ref.shape[1]

    @pl.loop(0, 4)
    def _(j):
        for out_ref, first in ((refs[-6], 0), (refs[-5], 4)):
            at = pl.multiple_of(block_ref[first + j] * chunk, chunk)
            out_ref[j] = dot(done, wo_ref[:, pl.ds(at, chunk)]).astype(BF16)


def decode(step, own, other, queries, w_key, w_value, w_out, blocks, carried, after):
    width = queries.shape[1]
    tile = SPANS_STEP * CH
    part = step % (own.shape[0] // SPANS_STEP)
    rows = SPANS_STEP * KNB * NLEN
    block = pl.BlockSpec((SPANS_STEP, NLEN, E), lambda i, *_: (part, 0, 0))
    return pl.pallas_call(
        lambda *refs: decode_kernel(len(carried) > 0, *refs),
        out_shape=[jax.ShapeDtypeStruct((4, tile, width), BF16)] * 2,
        grid_spec=pltpu.PrefetchScalarGridSpec(
            num_scalar_prefetch=1,
            grid=(1,),
            in_specs=[
                block,
                block,
                pl.BlockSpec((tile, width), lambda i, *_: (step, 0)),
                once((E, width)),
                once((E, width)),
                once((width, D)),
            ]
            + [once((1, NLEN, E))] * len(carried)
            + [pl.BlockSpec(memory_space=pl.ANY)] * len(after),
            out_specs=[once((4, tile, width))] * 2,
            scratch_shapes=[
                pltpu.VMEM((rows, E), BF16),
                pltpu.VMEM((tile, width), BF16),
                pltpu.VMEM((rows, width), BF16),
                pltpu.VMEM((rows, width), BF16),
            ],
        ),
        compiler_params=pltpu.CompilerParams(
            dimension_semantics=("arbitrary",), vmem_limit_bytes=VMEM_LIMIT
        ),
        cost_estimate=pl.CostEstimate(
            flops=4 * SPANS_STEP * KNB * NLEN * E * width + 2 * tile * width * D,
            bytes_accessed=6 << 20,
            transcendentals=tile * KNB * NLEN * (width // HD),
        ),
        name="decode",
    )(blocks, own, other, queries, w_key, w_value, w_out, *carried, *after)


def body(
    hidden,
    nbr_table,
    nbr_ids,
    w_query,
    w_key,
    w_value,
    w_out,
    enc_query,
    enc_key,
    enc_value,
    enc_out,
):
    store_count = lax.axis_size("store")
    store_rank = lax.axis_index("store")
    seq_count = lax.axis_size("seq")
    seq_rank = lax.axis_index("seq")
    side = math.isqrt(seq_count)
    chips = store_count // 2
    span_count = nbr_ids.shape[0]
    row_requests = span_count * KNB
    per_owner = row_requests // store_count
    blocks_here = nbr_table.shape[0]

    flat_ids = nbr_ids.reshape(-1)
    slot = jnp.arange(row_requests, dtype=jnp.int32)
    rank_key = (flat_ids // blocks_here) * row_requests + slot
    pos = jnp.sum((rank_key[:, None] > rank_key[None, :]).astype(jnp.int32), axis=1)
    by_owner = jnp.sum(jnp.where(pos[None, :] == slot[:, None], slot[None, :], 0), axis=1)
    picked = lax.dynamic_slice_in_dim(by_owner, store_rank * per_owner, per_owner)
    sources = nbr_table[flat_ids[picked] % blocks_here]
    gathered = lax.all_gather(sources, "store", axis=0, tiled=True)
    gathered = pltpu.with_memory_space_constraint(gathered, pltpu.HBM)

    pair_at = jnp.minimum(store_rank, PAIRS - 1) * 128
    weight = jnp.concatenate(
        [
            lax.dynamic_slice_in_dim(enc_key, pair_at, 128, axis=1),
            lax.dynamic_slice_in_dim(enc_value, pair_at, 128, axis=1),
        ],
        axis=1,
    )
    half = weight.shape[0] // 2
    a_four, b_four = stack_fours(
        around(weight[:half], side, False), around(weight[half:], side, True)
    )
    parts = around(a_four, side, True) + around(b_four, side, False)
    rel = jnp.array(REL, jnp.int32)
    y_at, z_at = seq_rank // side, seq_rank % side
    from_rank = jnp.concatenate([(y_at + rel + side) % side, (z_at + rel + side) % side])
    hidden_far = pltpu.with_memory_space_constraint(hidden, pltpu.HBM)
    queries = dot(hidden, w_query).astype(BF16)
    queries = pltpu.with_memory_space_constraint(queries, pltpu.HBM)
    cond = cond_rows(hidden_far, parts, from_rank, queries).reshape(-1, CH, 256)
    own_lane = around_x(cond, chips)
    chip, core = store_rank // 2, store_rank % 2
    lane = 2 * ((chip + rel + chips) % chips)
    pairs = jnp.concatenate([lane + core, lane + 1 - core])

    spans = (jnp.arange(span_count, dtype=jnp.int32) + FIRST) % span_count
    mine = jnp.sum(
        jnp.where(slot[None, :] == (KNB * spans + core)[:, None], pos[None, :], 0), axis=1
    )
    enc_query = pltpu.with_memory_space_constraint(enc_query, pltpu.HBM)
    enc_q = enc_queries(mine, gathered, enc_query)
    own_lane[1:] = hold(own_lane[1:], enc_q)
    conds = own_lane + [swap_cores(block) for block in own_lane]
    part = span_count // 2
    low = encode(0, part, mine, pairs, enc_q, gathered, conds, enc_out, ())
    low_other = swap_cores(low)
    carried, carried_other = (
        lax.ppermute(
            low[:1],
            ("seq", "store"),
            [
                (i * store_count + k, (i + 1) * store_count + (k ^ flip))
                for i in range(seq_count - 1)
                for k in range(store_count)
            ],
        )
        for flip in range(2)
    )
    high = encode(part, part, mine, pairs, enc_q, gathered, conds, enc_out, (low,))
    high_other = swap_cores(high)
    weights = (queries, w_key, w_value, w_out, pairs)
    kept, given, taken, sums, got = ([None] * 4 for _ in range(5))
    kept[0], given[0] = decode(0, low, low_other, *weights, (carried, carried_other), (high,))
    taken[0] = swap_cores(given[0])
    kept[1], given[1] = decode(1, low, low_other, *weights, (), (kept[0],))
    taken[1] = swap_cores(given[1])
    sums[0] = core_sums(kept[0], taken[0], (kept[1],))
    got[0] = send_over_x(sums[0], chips)
    kept[2], given[2] = decode(2, high, high_other, *weights, (), sums[0][1:])
    taken[2] = swap_cores(given[2])
    sums[1] = core_sums(kept[1], taken[1], (kept[2],))
    got[1] = send_over_x(sums[1], chips)
    kept[3], given[3] = decode(3, high, high_other, *weights, (), (*sums[1][1:], *got[0]))
    taken[3] = swap_cores(given[3])
    sums[2] = core_sums(kept[2], taken[2], (kept[3],))
    got[2] = send_over_x(sums[2], chips)
    sums[3] = core_sums(kept[3], taken[3], (*sums[2][1:], *got[1][:1]))
    got[3] = send_over_x(sums[3], chips)
    outs = []
    for k in range(4):
        total = sums[k][0]
        for block in got[k]:
            total = total + block.astype(F32)
        outs.append(total.astype(BF16))
    return jnp.concatenate(outs, axis=0)


def solution(mesh):
    in_specs = (
        P("seq", None),
        P("store", None, None),
        P("seq", None),
        P(None, "store"),
        P(None, "store"),
        P(None, "store"),
        P("store", None),
        P(),
        P("seq", None),
        P("seq", None),
        P(),
    )
    out_specs = P("seq", "store")
    return jax.shard_map(body, mesh=mesh, in_specs=in_specs, out_specs=out_specs, check_vma=False)
```

```python
import math

import jax
import jax.numpy as jnp
from jax import lax
from jax.experimental import pallas as pl
from jax.experimental.pallas import tpu as pltpu
from jax.sharding import PartitionSpec as P

D = 4096
HD = 128
E = 896
EHEADS = 14
EHD = 64
CH = 64
NLEN = 128
KNB = 2
PAIRS = E // 128

EPSILON = 1e-06
VMEM_LIMIT = 36 << 20
F32 = jnp.float32
BF16 = jnp.bfloat16
REL = (0, -1, 1, 2)
FIRST = 7


def dot(a, b):
    return jnp.dot(a, b, preferred_element_type=F32)


def grid_route(side, dy, dz):
    return [
        (side * y + z, side * ((y + dy) % side) + (z + dz) % side)
        for y in range(side)
        for z in range(side)
    ]


def around(block, side, along_y):
    got = [block]
    for rel in REL[1:]:
        route = grid_route(side, -rel, 0) if along_y else grid_route(side, 0, -rel)
        got.append(lax.ppermute(block, "seq", route))
    return got


def around_x(block, chips):
    got = [block]
    for rel in REL[1:]:
        route = [
            (2 * x + core, 2 * ((x - rel) % chips) + core) for x in range(chips) for core in range(2)
        ]
        got.append(lax.ppermute(block, "store", route))
    return got


def swap_cores(block):
    count = lax.axis_size("store")
    return lax.ppermute(block, "store", [(i, i ^ 1) for i in range(count)])


def add_kernel(kept_ref, taken_ref, *refs):
    for j, out_ref in enumerate(refs[-4:]):
        total = kept_ref[j].astype(F32) + taken_ref[j].astype(F32)
        out_ref[...] = total.astype(out_ref.dtype)


def core_sums(kept, taken, after):
    vmem = pl.BlockSpec(memory_space=pltpu.VMEM)
    shape = kept.shape[1:]
    return pl.pallas_call(
        add_kernel,
        out_shape=[jax.ShapeDtypeStruct(shape, F32)] + [jax.ShapeDtypeStruct(shape, BF16)] * 3,
        in_specs=[vmem] * 2 + [pl.BlockSpec(memory_space=pl.ANY)] * len(after),
        out_specs=[vmem] * 4,
        compiler_params=pltpu.CompilerParams(vmem_limit_bytes=8 << 20),
        cost_estimate=pl.CostEstimate(flops=1 << 19, bytes_accessed=4 << 20, transcendentals=0),
        name="core_sums",
    )(kept, taken, *after)


def send_over_x(sums, chips):
    got = []
    for j in range(1, 4):
        route = [
            (2 * x + core, 2 * ((x + REL[j]) % chips) + core)
            for x in range(chips)
            for core in range(2)
        ]
        got.append(lax.ppermute(sums[j], "store", route))
    return got


def once(shape):
    return pl.BlockSpec(shape, lambda *_: (0,) * len(shape), pipeline_mode=pl.Buffered(1))


def cond_kernel(src_ref, hidden_ref, *refs):
    a_refs, b_refs, (out_ref, total) = refs[:4], refs[4:8], refs[-2:]
    step = pl.program_id(0)
    for i in range(4):

        @pl.when(step == i)
        def _():
            terms = None if i == 0 else total[...]
            for j in range(4):
                at = pl.multiple_of(src_ref[4 + j] * 256, 256)
                weight = jnp.concatenate([a_refs[i][j], b_refs[j][i]], axis=0)
                term = dot(hidden_ref[:, pl.ds(at, 256)], weight)
                terms = term if terms is None else terms + term
            if i == 3:
                first = FIRST * CH
                out_ref[: terms.shape[0] - first, :] = terms[first:].astype(BF16)
                out_ref[terms.shape[0] - first :, :] = terms[:first].astype(BF16)
            else:
                total[...] = terms


def cond_rows(hidden, parts, sources, after):
    tokens = hidden.shape[0]
    return pl.pallas_call(
        cond_kernel,
        out_shape=jax.ShapeDtypeStruct((tokens, 256), BF16),
        grid_spec=pltpu.PrefetchScalarGridSpec(
            num_scalar_prefetch=1,
            grid=(4,),
            in_specs=[pl.BlockSpec((tokens, D // 4), lambda i, s: (0, s[i]))]
            + [once((4, 128, 256))] * 8
            + [pl.BlockSpec(memory_space=pl.ANY)],
            out_specs=pl.BlockSpec((tokens, 256), lambda i, s: (0, 0)),
            scratch_shapes=[pltpu.VMEM((tokens, 256), F32)],
        ),
        compiler_params=pltpu.CompilerParams(
            dimension_semantics=("arbitrary",), vmem_limit_bytes=VMEM_LIMIT
        ),
        cost_estimate=pl.CostEstimate(
            flops=2 * tokens * D * 256, bytes_accessed=12 << 20, transcendentals=0
        ),
        name="cond_rows",
    )(sources, hidden, *parts, after)


def hold_kernel(*refs):
    count = len(refs) // 2
    for source, target in zip(refs[:count], refs[count + 1 :]):
        target[...] = source[...]


def hold(blocks, after):
    count = len(blocks)
    vmem = pl.BlockSpec(memory_space=pltpu.VMEM)
    return pl.pallas_call(
        hold_kernel,
        out_shape=[jax.ShapeDtypeStruct(block.shape, BF16) for block in blocks],
        in_specs=[vmem] * count + [pl.BlockSpec(memory_space=pl.ANY)],
        out_specs=[vmem] * count,
        compiler_params=pltpu.CompilerParams(vmem_limit_bytes=8 << 20),
        cost_estimate=pl.CostEstimate(flops=0, bytes_accessed=1 << 20, transcendentals=0),
        name="hold",
    )(*blocks, after)


def stack_kernel(*refs):
    for j in range(4):
        refs[8][j] = refs[j][...]
        refs[9][j] = refs[4 + j][...]


def stack_fours(a, b):
    vmem = pl.BlockSpec(memory_space=pltpu.VMEM)
    shape = jax.ShapeDtypeStruct((4, *a[0].shape), BF16)
    return pl.pallas_call(
        stack_kernel,
        out_shape=[shape, shape],
        in_specs=[vmem] * 8,
        out_specs=[vmem] * 2,
        compiler_params=pltpu.CompilerParams(vmem_limit_bytes=8 << 20),
        cost_estimate=pl.CostEstimate(flops=0, bytes_accessed=1 << 20, transcendentals=0),
        name="stack_fours",
    )(*a, *b)


def enc_query_kernel(pos_ref, *refs):
    del pos_ref
    sources, w_ref, out_ref = refs[:4], refs[4], refs[-1]
    rows = []
    for source in sources:
        block = source[0].astype(F32)
        scale = lax.rsqrt(jnp.mean(block * block, axis=-1, keepdims=True) + EPSILON)
        rows.append((block * scale).astype(BF16))
    got = dot(jnp.concatenate(rows, axis=0), w_ref[...]).astype(BF16)
    for n in range(4):
        out_ref[n] = got[n * NLEN : (n + 1) * NLEN]


def enc_queries(pos, gathered, weight):
    count = pos.shape[0]

    def source(n):
        return pl.BlockSpec((1, NLEN, E), lambda i, pos: (pos[4 * i + n], 0, 0))

    return pl.pallas_call(
        enc_query_kernel,
        out_shape=jax.ShapeDtypeStruct((count, NLEN, E), BF16),
        grid_spec=pltpu.PrefetchScalarGridSpec(
            num_scalar_prefetch=1,
            grid=(count // 4,),
            in_specs=[source(n) for n in range(4)] + [once((E, E))],
            out_specs=pl.BlockSpec((4, NLEN, E), lambda i, pos: (i, 0, 0)),
        ),
        compiler_params=pltpu.CompilerParams(
            dimension_semantics=("arbitrary",), vmem_limit_bytes=VMEM_LIMIT
        ),
        cost_estimate=pl.CostEstimate(
            flops=2 * count * NLEN * E * E, bytes_accessed=10 << 20, transcendentals=0
        ),
        name="enc_queries",
    )(pos, *([gathered] * 4), weight)


def encode_kernel(pos_ref, pair_ref, *refs):
    del pos_ref
    sources, conds = refs[:4], refs[4:12]
    query_ref, out_w_ref = refs[12:14]
    out_ref, mixed = refs[-2:]
    row_head = lax.broadcasted_iota(jnp.int32, (128, 128), 0) // EHD
    col_head = lax.broadcasted_iota(jnp.int32, (128, 128), 1) // EHD
    same = row_head == col_head
    zero = jnp.zeros((128, 128), BF16)
    units = [(n, j) for n in range(4) for j in range(8)]

    def two_heads(block):
        return jnp.where(same, jnp.concatenate([block, block], axis=0), zero)

    def score(n, j):
        at = pl.multiple_of(jnp.minimum(pair_ref[j], PAIRS - 1) * 128, 128)
        return lax.dot_general(
            two_heads(conds[j][n, :, :128]),
            query_ref[n, :, pl.ds(at, 128)],
            (((1,), (1,)), ((), ())),
            preferred_element_type=F32,
        ) * (1.0 / math.sqrt(EHD))

    def soften(scores):
        halves = []
        for h in range(2):
            part = scores[h * EHD : (h + 1) * EHD]
            grown = jnp.exp(part - jnp.max(part, axis=0, keepdims=True))
            halves.append((grown * (1.0 / jnp.sum(grown, axis=0, keepdims=True))).astype(BF16))
        return jnp.concatenate(halves, axis=0)

    scores = [score(n, j) for n, j in units]
    weights = [soften(x) for x in scores]
    for weight, (n, j) in zip(weights, units):
        got = lax.dot_general(
            weight,
            two_heads(conds[j][n, :, 128:]),
            (((0,), (0,)), ((), ())),
            preferred_element_type=F32,
        )
        at = pl.multiple_of(pair_ref[j] * 128, 128)
        mixed[n * NLEN : (n + 1) * NLEN, pl.ds(at, 128)] = got.astype(BF16)
    branch = dot(mixed[:, :E], out_w_ref[...])
    for n in range(4):
        rows = branch[n * NLEN : (n + 1) * NLEN]
        out_ref[n] = (sources[n][0].astype(F32) + rows).astype(BF16)


def encode(base, count, pos, pairs, queries, gathered, conds, enc_out, after):
    first = base // 4

    def source(n):
        return pl.BlockSpec((1, NLEN, E), lambda i, pos, pairs: (pos[base + 4 * i + n], 0, 0))

    cond = pl.BlockSpec((4, CH, 256), lambda i, pos, pairs: (first + i, 0, 0))
    return pl.pallas_call(
        encode_kernel,
        out_shape=jax.ShapeDtypeStruct((count, NLEN, E), BF16),
        grid_spec=pltpu.PrefetchScalarGridSpec(
            num_scalar_prefetch=2,
            grid=(count // 4,),
            in_specs=[source(n) for n in range(4)]
            + [cond] * 8
            + [
                pl.BlockSpec((4, NLEN, E), lambda i, pos, pairs: (first + i, 0, 0)),
                once((E, E)),
            ]
            + [pl.BlockSpec(memory_space=pl.ANY)] * len(after),
            out_specs=pl.BlockSpec((4, NLEN, E), lambda i, pos, pairs: (i, 0, 0)),
            scratch_shapes=[pltpu.VMEM((4 * NLEN, 1024), BF16)],
        ),
        compiler_params=pltpu.CompilerParams(
            dimension_semantics=("arbitrary",), vmem_limit_bytes=VMEM_LIMIT
        ),
        cost_estimate=pl.CostEstimate(
            flops=count * NLEN * E * E * 3, bytes_accessed=8 << 20, transcendentals=count << 17
        ),
        name="encode",
    )(pos, pairs, *([gathered] * 4), *conds, queries, enc_out, *after)


SPANS_STEP = 4


def decode_kernel(carries, split, *refs):
    if split:
        block_ref, refs = refs[0], refs[1:]
    own_ref, other_ref, q_ref, wk_ref, wv_ref, wo_ref = refs[:6]
    rows, att, ks, vs = refs[-4:]
    for j in range(SPANS_STEP):
        for n, ref in enumerate((own_ref, other_ref)):
            at = slice((KNB * j + n) * NLEN, (KNB * j + n + 1) * NLEN)
            rows[at, :] = ref[j]
    if carries:

        @pl.when(pl.program_id(0) == 0)
        def _():
            rows[:NLEN, :] = refs[6][0]
            rows[NLEN : 2 * NLEN, :] = refs[7][0]

    length = KNB * NLEN
    block = rows[...]
    ks[...] = dot(block, wk_ref[...]).astype(BF16)
    units = [(s, p) for s in range(SPANS_STEP) for p in range(q_ref.shape[1] // 256)]
    empty = jnp.zeros((CH, HD), BF16)
    weights = []
    scores = []
    for s, p in units:
        pair = q_ref[s * CH : (s + 1) * CH, p * 256 : (p + 1) * 256]
        both = jnp.concatenate(
            [
                jnp.concatenate([pair[:, :HD], empty], axis=1),
                jnp.concatenate([empty, pair[:, HD:]], axis=1),
            ],
            axis=0,
        )
        scores.append(
            lax.dot_general(
                ks[s * length : (s + 1) * length, p * 256 : (p + 1) * 256],
                both,
                (((1,), (1,)), ((), ())),
                preferred_element_type=F32,
            )
            * (1.0 / math.sqrt(HD))
        )
    for score in scores:
        grown = jnp.exp(score - jnp.max(score, axis=0, keepdims=True))
        weights.append((grown * (1.0 / jnp.sum(grown, axis=0, keepdims=True))).astype(BF16))
    vs[...] = dot(block, wv_ref[...]).astype(BF16)
    for weight, (s, p) in zip(weights, units):
        got = lax.dot_general(
            weight,
            vs[s * length : (s + 1) * length, p * 256 : (p + 1) * 256],
            (((0,), (0,)), ((), ())),
            preferred_element_type=F32,
        ).astype(BF16)
        att[s * CH : (s + 1) * CH, p * 256 : p * 256 + HD] = got[:CH, :HD]
        att[s * CH : (s + 1) * CH, p * 256 + HD : (p + 1) * 256] = got[CH:, HD:]
    done = att[...]
    chunk = q_ref.shape[1]

    if split:

        @pl.loop(0, 4)
        def _(j):
            for out_ref, first in ((refs[-6], 0), (refs[-5], 4)):
                at = pl.multiple_of(block_ref[first + j] * chunk, chunk)
                out_ref[j] = dot(done, wo_ref[:, pl.ds(at, chunk)]).astype(BF16)

    else:

        @pl.loop(0, wo_ref.shape[1] // chunk)
        def _(j):
            at = pl.ds(pl.multiple_of(j * chunk, chunk), chunk)
            refs[-5][:, at] = dot(done, wo_ref[:, at]).astype(BF16)


def decode(first, steps, own, other, queries, w_key, w_value, w_out, blocks, carried, after):
    split = blocks is not None
    width = queries.shape[1]
    tile = SPANS_STEP * CH
    part = first % (own.shape[0] // SPANS_STEP)
    rows = SPANS_STEP * KNB * NLEN
    block = pl.BlockSpec((SPANS_STEP, NLEN, E), lambda i, *_: (part + i, 0, 0))
    if split:
        out_shape = [jax.ShapeDtypeStruct((4, steps * tile, width), BF16)] * 2
        out_specs = [pl.BlockSpec((4, tile, width), lambda i, *_: (0, i, 0))] * 2
    else:
        out_shape = pltpu.HBM((steps * tile, D), BF16)
        out_specs = pl.BlockSpec((tile, D), lambda i, *_: (i, 0))
    return pl.pallas_call(
        lambda *refs: decode_kernel(len(carried) > 0, split, *refs),
        out_shape=out_shape,
        grid_spec=pltpu.PrefetchScalarGridSpec(
            num_scalar_prefetch=int(split),
            grid=(steps,),
            in_specs=[
                block,
                block,
                pl.BlockSpec((tile, width), lambda i, *_: (first + i, 0)),
                once((E, width)),
                once((E, width)),
                once((width, D)),
            ]
            + [once((1, NLEN, E))] * len(carried)
            + [pl.BlockSpec(memory_space=pltpu.HBM if split else pl.ANY)],
            out_specs=out_specs,
            scratch_shapes=[
                pltpu.VMEM((rows, E), BF16),
                pltpu.VMEM((tile, width), BF16),
                pltpu.VMEM((rows, width), BF16),
                pltpu.VMEM((rows, width), BF16),
            ],
        ),
        compiler_params=pltpu.CompilerParams(
            dimension_semantics=("arbitrary",),
            vmem_limit_bytes=(60 << 20) if split else VMEM_LIMIT,
        ),
        cost_estimate=pl.CostEstimate(
            flops=steps * (4 * SPANS_STEP * KNB * NLEN * E * width + 2 * tile * width * D),
            bytes_accessed=6 << 20,
            transcendentals=steps * tile * KNB * NLEN * (width // HD),
        ),
        name="decode",
    )(*([blocks] if split else []), own, other, queries, w_key, w_value, w_out, *carried, after)


def body(
    hidden,
    nbr_table,
    nbr_ids,
    w_query,
    w_key,
    w_value,
    w_out,
    enc_query,
    enc_key,
    enc_value,
    enc_out,
):
    store_count = lax.axis_size("store")
    store_rank = lax.axis_index("store")
    seq_count = lax.axis_size("seq")
    seq_rank = lax.axis_index("seq")
    side = math.isqrt(seq_count)
    chips = store_count // 2
    span_count = nbr_ids.shape[0]
    row_requests = span_count * KNB
    per_owner = row_requests // store_count
    blocks_here = nbr_table.shape[0]

    flat_ids = nbr_ids.reshape(-1)
    slot = jnp.arange(row_requests, dtype=jnp.int32)
    rank_key = (flat_ids // blocks_here) * row_requests + slot
    pos = jnp.sum((rank_key[:, None] > rank_key[None, :]).astype(jnp.int32), axis=1)
    by_owner = jnp.sum(jnp.where(pos[None, :] == slot[:, None], slot[None, :], 0), axis=1)
    picked = lax.dynamic_slice_in_dim(by_owner, store_rank * per_owner, per_owner)
    sources = nbr_table[flat_ids[picked] % blocks_here]
    gathered = lax.all_gather(sources, "store", axis=0, tiled=True)
    gathered = pltpu.with_memory_space_constraint(gathered, pltpu.HBM)

    pair_at = jnp.minimum(store_rank, PAIRS - 1) * 128
    weight = jnp.concatenate(
        [
            lax.dynamic_slice_in_dim(enc_key, pair_at, 128, axis=1),
            lax.dynamic_slice_in_dim(enc_value, pair_at, 128, axis=1),
        ],
        axis=1,
    )
    half = weight.shape[0] // 2
    a_four, b_four = stack_fours(
        around(weight[:half], side, False), around(weight[half:], side, True)
    )
    parts = around(a_four, side, True) + around(b_four, side, False)
    rel = jnp.array(REL, jnp.int32)
    y_at, z_at = seq_rank // side, seq_rank % side
    from_rank = jnp.concatenate([(y_at + rel + side) % side, (z_at + rel + side) % side])
    hidden_far = pltpu.with_memory_space_constraint(hidden, pltpu.HBM)
    queries = dot(hidden, w_query).astype(BF16)
    queries = pltpu.with_memory_space_constraint(queries, pltpu.HBM)
    cond = cond_rows(hidden_far, parts, from_rank, queries).reshape(-1, CH, 256)
    own_lane = around_x(cond, chips)
    chip, core = store_rank // 2, store_rank % 2
    lane = 2 * ((chip + rel + chips) % chips)
    pairs = jnp.concatenate([lane + core, lane + 1 - core])

    spans = (jnp.arange(span_count, dtype=jnp.int32) + FIRST) % span_count
    mine = jnp.sum(
        jnp.where(slot[None, :] == (KNB * spans + core)[:, None], pos[None, :], 0), axis=1
    )
    enc_query = pltpu.with_memory_space_constraint(enc_query, pltpu.HBM)
    enc_q = enc_queries(mine, gathered, enc_query)
    own_lane[1:] = hold(own_lane[1:], enc_q)
    conds = own_lane + [swap_cores(block) for block in own_lane]
    part = span_count // 2
    high = encode(0, part, mine, pairs, enc_q, gathered, conds, enc_out, ())
    high_other = swap_cores(high)
    low = encode(part, part, mine, pairs, enc_q, gathered, conds, enc_out, (high,))
    low_other = swap_cores(low)
    carried = tuple(
        lax.ppermute(
            low[:1],
            ("seq", "store"),
            [
                (i * store_count + k, (i + 1) * store_count + (k ^ flip))
                for i in range(seq_count - 1)
                for k in range(store_count)
            ],
        )
        for flip in range(2)
    )
    weights = (queries, w_key, w_value, w_out)
    terms = decode(2, 2, high, high_other, *weights, None, (), low)
    high_out = lax.psum_scatter(terms, "store", scatter_dimension=1, tiled=True)
    kept_1, given_1 = decode(1, 1, low, low_other, *weights, pairs, (), terms)
    taken_1 = swap_cores(given_1)
    kept_0, given_0 = decode(0, 1, low, low_other, *weights, pairs, carried, kept_1)
    taken_0 = swap_cores(given_0)
    sums_1 = core_sums(kept_1, taken_1, (kept_0,))
    got_1 = send_over_x(sums_1, chips)
    sums_0 = core_sums(kept_0, taken_0, sums_1[1:])
    got_0 = send_over_x(sums_0, chips)
    outs = []
    for sums, got in ((sums_0, got_0), (sums_1, got_1)):
        total = sums[0]
        for block in got:
            total = total + block.astype(F32)
        outs.append(total.astype(BF16))
    return jnp.concatenate([*outs, high_out], axis=0)


def solution(mesh):
    in_specs = (
        P("seq", None),
        P("store", None, None),
        P("seq", None),
        P(None, "store"),
        P(None, "store"),
        P(None, "store"),
        P("store", None),
        P(),
        P("seq", None),
        P("seq", None),
        P(),
    )
    out_specs = P("seq", "store")
    return jax.shard_map(body, mesh=mesh, in_specs=in_specs, out_specs=out_specs, check_vma=False)
```

```python
import math

import jax
import jax.numpy as jnp
from jax import lax
from jax.experimental import pallas as pl
from jax.experimental.pallas import tpu as pltpu
from jax.sharding import PartitionSpec as P

D = 4096
HD = 128
E = 896
EHEADS = 14
EHD = 64
CH = 64
NLEN = 128
KNB = 2
PAIRS = E // 128

EPSILON = 1e-06
VMEM_LIMIT = 36 << 20
F32 = jnp.float32
BF16 = jnp.bfloat16
REL = (0, -1, 1, 2)
FIRST = 7


def dot(a, b):
    return jnp.dot(a, b, preferred_element_type=F32)


def grid_route(side, dy, dz):
    return [
        (side * y + z, side * ((y + dy) % side) + (z + dz) % side)
        for y in range(side)
        for z in range(side)
    ]


def around(block, side, along_y):
    got = [block]
    for rel in REL[1:]:
        route = grid_route(side, -rel, 0) if along_y else grid_route(side, 0, -rel)
        got.append(lax.ppermute(block, "seq", route))
    return got


def around_x(block, chips):
    got = [block]
    for rel in REL[1:]:
        route = [
            (2 * x + core, 2 * ((x - rel) % chips) + core) for x in range(chips) for core in range(2)
        ]
        got.append(lax.ppermute(block, "store", route))
    return got


def swap_cores(block):
    count = lax.axis_size("store")
    return lax.ppermute(block, "store", [(i, i ^ 1) for i in range(count)])


def add_kernel(kept_ref, taken_ref, *refs):
    for j, out_ref in enumerate(refs[-4:]):
        total = kept_ref[j].astype(F32) + taken_ref[j].astype(F32)
        out_ref[...] = total.astype(out_ref.dtype)


def core_sums(kept, taken, after):
    vmem = pl.BlockSpec(memory_space=pltpu.VMEM)
    shape = kept.shape[1:]
    return pl.pallas_call(
        add_kernel,
        out_shape=[jax.ShapeDtypeStruct(shape, F32)] + [jax.ShapeDtypeStruct(shape, BF16)] * 3,
        in_specs=[vmem] * 2 + [pl.BlockSpec(memory_space=pl.ANY)] * len(after),
        out_specs=[vmem] * 4,
        compiler_params=pltpu.CompilerParams(vmem_limit_bytes=8 << 20),
        cost_estimate=pl.CostEstimate(flops=1 << 19, bytes_accessed=4 << 20, transcendentals=0),
        name="core_sums",
    )(kept, taken, *after)


def send_over_x(sums, chips):
    got = []
    for j in range(1, 4):
        route = [
            (2 * x + core, 2 * ((x + REL[j]) % chips) + core)
            for x in range(chips)
            for core in range(2)
        ]
        got.append(lax.ppermute(sums[j], "store", route))
    return got


def once(shape):
    return pl.BlockSpec(shape, lambda *_: (0,) * len(shape), pipeline_mode=pl.Buffered(1))


def cond_kernel(src_ref, hidden_ref, *refs):
    a_refs, b_refs, (out_ref, total) = refs[:4], refs[4:8], refs[-2:]
    step = pl.program_id(0)
    for i in range(4):

        @pl.when(step == i)
        def _():
            terms = None if i == 0 else total[...]
            for j in range(4):
                at = pl.multiple_of(src_ref[4 + j] * 256, 256)
                weight = jnp.concatenate([a_refs[i][j], b_refs[j][i]], axis=0)
                term = dot(hidden_ref[:, pl.ds(at, 256)], weight)
                terms = term if terms is None else terms + term
            if i == 3:
                first = FIRST * CH
                out_ref[: terms.shape[0] - first, :] = terms[first:].astype(BF16)
                out_ref[terms.shape[0] - first :, :] = terms[:first].astype(BF16)
            else:
                total[...] = terms


def cond_rows(hidden, parts, sources, after):
    tokens = hidden.shape[0]
    return pl.pallas_call(
        cond_kernel,
        out_shape=jax.ShapeDtypeStruct((tokens, 256), BF16),
        grid_spec=pltpu.PrefetchScalarGridSpec(
            num_scalar_prefetch=1,
            grid=(4,),
            in_specs=[pl.BlockSpec((tokens, D // 4), lambda i, s: (0, s[i]))]
            + [once((4, 128, 256))] * 8
            + [pl.BlockSpec(memory_space=pl.ANY)],
            out_specs=pl.BlockSpec((tokens, 256), lambda i, s: (0, 0)),
            scratch_shapes=[pltpu.VMEM((tokens, 256), F32)],
        ),
        compiler_params=pltpu.CompilerParams(
            dimension_semantics=("arbitrary",), vmem_limit_bytes=VMEM_LIMIT
        ),
        cost_estimate=pl.CostEstimate(
            flops=2 * tokens * D * 256, bytes_accessed=12 << 20, transcendentals=0
        ),
        name="cond_rows",
    )(sources, hidden, *parts, after)


def hold_kernel(*refs):
    count = len(refs) // 2
    for source, target in zip(refs[:count], refs[count + 1 :]):
        target[...] = source[...]


def hold(blocks, after):
    count = len(blocks)
    vmem = pl.BlockSpec(memory_space=pltpu.VMEM)
    return pl.pallas_call(
        hold_kernel,
        out_shape=[jax.ShapeDtypeStruct(block.shape, BF16) for block in blocks],
        in_specs=[vmem] * count + [pl.BlockSpec(memory_space=pl.ANY)],
        out_specs=[vmem] * count,
        compiler_params=pltpu.CompilerParams(vmem_limit_bytes=8 << 20),
        cost_estimate=pl.CostEstimate(flops=0, bytes_accessed=1 << 20, transcendentals=0),
        name="hold",
    )(*blocks, after)


def stack_kernel(*refs):
    for j in range(4):
        refs[8][j] = refs[j][...]
        refs[9][j] = refs[4 + j][...]


def stack_fours(a, b):
    vmem = pl.BlockSpec(memory_space=pltpu.VMEM)
    shape = jax.ShapeDtypeStruct((4, *a[0].shape), BF16)
    return pl.pallas_call(
        stack_kernel,
        out_shape=[shape, shape],
        in_specs=[vmem] * 8,
        out_specs=[vmem] * 2,
        compiler_params=pltpu.CompilerParams(vmem_limit_bytes=8 << 20),
        cost_estimate=pl.CostEstimate(flops=0, bytes_accessed=1 << 20, transcendentals=0),
        name="stack_fours",
    )(*a, *b)


def enc_query_kernel(pos_ref, *refs):
    del pos_ref
    sources, w_ref, out_ref = refs[:4], refs[4], refs[-1]
    rows = []
    for source in sources:
        block = source[0].astype(F32)
        scale = lax.rsqrt(jnp.mean(block * block, axis=-1, keepdims=True) + EPSILON)
        rows.append((block * scale).astype(BF16))
    got = dot(jnp.concatenate(rows, axis=0), w_ref[...]).astype(BF16)
    for n in range(4):
        out_ref[n] = got[n * NLEN : (n + 1) * NLEN]


def enc_queries(pos, gathered, weight):
    count = pos.shape[0]

    def source(n):
        return pl.BlockSpec((1, NLEN, E), lambda i, pos: (pos[4 * i + n], 0, 0))

    return pl.pallas_call(
        enc_query_kernel,
        out_shape=jax.ShapeDtypeStruct((count, NLEN, E), BF16),
        grid_spec=pltpu.PrefetchScalarGridSpec(
            num_scalar_prefetch=1,
            grid=(count // 4,),
            in_specs=[source(n) for n in range(4)] + [once((E, E))],
            out_specs=pl.BlockSpec((4, NLEN, E), lambda i, pos: (i, 0, 0)),
        ),
        compiler_params=pltpu.CompilerParams(
            dimension_semantics=("arbitrary",), vmem_limit_bytes=VMEM_LIMIT
        ),
        cost_estimate=pl.CostEstimate(
            flops=2 * count * NLEN * E * E, bytes_accessed=10 << 20, transcendentals=0
        ),
        name="enc_queries",
    )(pos, *([gathered] * 4), weight)


def encode_kernel(pos_ref, pair_ref, *refs):
    del pos_ref
    sources, conds = refs[:4], refs[4:12]
    query_ref, out_w_ref = refs[12:14]
    out_ref, mixed = refs[-2:]
    row_head = lax.broadcasted_iota(jnp.int32, (128, 128), 0) // EHD
    col_head = lax.broadcasted_iota(jnp.int32, (128, 128), 1) // EHD
    same = row_head == col_head
    zero = jnp.zeros((128, 128), BF16)
    units = [(n, j) for n in range(4) for j in range(8)]

    def two_heads(block):
        return jnp.where(same, jnp.concatenate([block, block], axis=0), zero)

    def score(n, j):
        at = pl.multiple_of(jnp.minimum(pair_ref[j], PAIRS - 1) * 128, 128)
        return lax.dot_general(
            two_heads(conds[j][n, :, :128]),
            query_ref[n, :, pl.ds(at, 128)],
            (((1,), (1,)), ((), ())),
            preferred_element_type=F32,
        ) * (1.0 / math.sqrt(EHD))

    def soften(scores):
        halves = []
        for h in range(2):
            part = scores[h * EHD : (h + 1) * EHD]
            grown = jnp.exp(part - jnp.max(part, axis=0, keepdims=True))
            halves.append((grown * (1.0 / jnp.sum(grown, axis=0, keepdims=True))).astype(BF16))
        return jnp.concatenate(halves, axis=0)

    scores = [score(n, j) for n, j in units]
    weights = [soften(x) for x in scores]
    for weight, (n, j) in zip(weights, units):
        got = lax.dot_general(
            weight,
            two_heads(conds[j][n, :, 128:]),
            (((0,), (0,)), ((), ())),
            preferred_element_type=F32,
        )
        at = pl.multiple_of(pair_ref[j] * 128, 128)
        mixed[n * NLEN : (n + 1) * NLEN, pl.ds(at, 128)] = got.astype(BF16)
    branch = dot(mixed[:, :E], out_w_ref[...])
    for n in range(4):
        rows = branch[n * NLEN : (n + 1) * NLEN]
        out_ref[n] = (sources[n][0].astype(F32) + rows).astype(BF16)


def encode(base, count, pos, pairs, queries, gathered, conds, enc_out, after):
    first = base // 4

    def source(n):
        return pl.BlockSpec((1, NLEN, E), lambda i, pos, pairs: (pos[base + 4 * i + n], 0, 0))

    cond = pl.BlockSpec((4, CH, 256), lambda i, pos, pairs: (first + i, 0, 0))
    return pl.pallas_call(
        encode_kernel,
        out_shape=jax.ShapeDtypeStruct((count, NLEN, E), BF16),
        grid_spec=pltpu.PrefetchScalarGridSpec(
            num_scalar_prefetch=2,
            grid=(count // 4,),
            in_specs=[source(n) for n in range(4)]
            + [cond] * 8
            + [
                pl.BlockSpec((4, NLEN, E), lambda i, pos, pairs: (first + i, 0, 0)),
                once((E, E)),
            ]
            + [pl.BlockSpec(memory_space=pl.ANY)] * len(after),
            out_specs=pl.BlockSpec((4, NLEN, E), lambda i, pos, pairs: (i, 0, 0)),
            scratch_shapes=[pltpu.VMEM((4 * NLEN, 1024), BF16)],
        ),
        compiler_params=pltpu.CompilerParams(
            dimension_semantics=("arbitrary",), vmem_limit_bytes=VMEM_LIMIT
        ),
        cost_estimate=pl.CostEstimate(
            flops=count * NLEN * E * E * 3, bytes_accessed=8 << 20, transcendentals=count << 17
        ),
        name="encode",
    )(pos, pairs, *([gathered] * 4), *conds, queries, enc_out, *after)


SPANS_STEP = 4


def decode_kernel(carries, split, *refs):
    if split:
        block_ref, refs = refs[0], refs[1:]
    own_ref, other_ref, q_ref, wk_ref, wv_ref, wo_ref = refs[:6]
    if split:
        outs, (rows, att, ks, vs, wv_here, wo_here, sems) = refs[-9:-7], refs[-7:]
        load_value = pltpu.make_async_copy(wv_ref, wv_here, sems.at[0])
        load_out = pltpu.make_async_copy(wo_ref, wo_here, sems.at[1])
        load_value.start()
        load_out.start()
        wv_ref, wo_ref = wv_here, wo_here
    else:
        outs, (rows, att, ks, vs) = refs[-5:-4], refs[-4:]
    for j in range(SPANS_STEP):
        for n, ref in enumerate((own_ref, other_ref)):
            at = slice((KNB * j + n) * NLEN, (KNB * j + n + 1) * NLEN)
            rows[at, :] = ref[j]
    if carries:

        @pl.when(pl.program_id(0) == 0)
        def _():
            rows[:NLEN, :] = refs[6][0]
            rows[NLEN : 2 * NLEN, :] = refs[7][0]

    length = KNB * NLEN
    block = rows[...]
    ks[...] = dot(block, wk_ref[...]).astype(BF16)
    units = [(s, p) for s in range(SPANS_STEP) for p in range(q_ref.shape[1] // 256)]
    empty = jnp.zeros((CH, HD), BF16)
    weights = []
    scores = []
    for s, p in units:
        pair = q_ref[s * CH : (s + 1) * CH, p * 256 : (p + 1) * 256]
        both = jnp.concatenate(
            [
                jnp.concatenate([pair[:, :HD], empty], axis=1),
                jnp.concatenate([empty, pair[:, HD:]], axis=1),
            ],
            axis=0,
        )
        scores.append(
            lax.dot_general(
                ks[s * length : (s + 1) * length, p * 256 : (p + 1) * 256],
                both,
                (((1,), (1,)), ((), ())),
                preferred_element_type=F32,
            )
            * (1.0 / math.sqrt(HD))
        )
    for score in scores:
        grown = jnp.exp(score - jnp.max(score, axis=0, keepdims=True))
        weights.append((grown * (1.0 / jnp.sum(grown, axis=0, keepdims=True))).astype(BF16))
    if split:
        load_value.wait()
    vs[...] = dot(block, wv_ref[...]).astype(BF16)
    for weight, (s, p) in zip(weights, units):
        got = lax.dot_general(
            weight,
            vs[s * length : (s + 1) * length, p * 256 : (p + 1) * 256],
            (((0,), (0,)), ((), ())),
            preferred_element_type=F32,
        ).astype(BF16)
        att[s * CH : (s + 1) * CH, p * 256 : p * 256 + HD] = got[:CH, :HD]
        att[s * CH : (s + 1) * CH, p * 256 + HD : (p + 1) * 256] = got[CH:, HD:]
    done = att[...]
    chunk = q_ref.shape[1]

    if split:
        load_out.wait()
        for out_ref, first in ((outs[0], 0), (outs[1], 4)):
            for j in range(4):
                at = pl.multiple_of(block_ref[first + j] * chunk, chunk)
                out_ref[j] = dot(done, wo_ref[:, pl.ds(at, chunk)]).astype(BF16)
    else:
        for j in range(wo_ref.shape[1] // chunk):
            at = slice(j * chunk, (j + 1) * chunk)
            outs[0][:, at] = dot(done, wo_ref[:, at]).astype(BF16)


def decode(first, steps, own, other, queries, w_key, w_value, w_out, blocks, carried, after):
    split = blocks is not None
    width = queries.shape[1]
    tile = SPANS_STEP * CH
    part = first % (own.shape[0] // SPANS_STEP)
    rows = SPANS_STEP * KNB * NLEN
    block = pl.BlockSpec((SPANS_STEP, NLEN, E), lambda i, *_: (part + i, 0, 0))
    far = pl.BlockSpec(memory_space=pltpu.HBM)
    scratch = []
    if split:
        assert steps == 1
        scratch = [
            pltpu.VMEM((E, width), BF16),
            pltpu.VMEM((width, D), BF16),
            pltpu.SemaphoreType.DMA((2,)),
        ]
        out_shape = [jax.ShapeDtypeStruct((4, steps * tile, width), BF16)] * 2
        out_specs = [pl.BlockSpec((4, tile, width), lambda i, *_: (0, i, 0))] * 2
    else:
        out_shape = pltpu.HBM((steps * tile, D), BF16)
        out_specs = pl.BlockSpec((tile, D), lambda i, *_: (i, 0))
    return pl.pallas_call(
        lambda *refs: decode_kernel(len(carried) > 0, split, *refs),
        out_shape=out_shape,
        grid_spec=pltpu.PrefetchScalarGridSpec(
            num_scalar_prefetch=int(split),
            grid=(steps,),
            in_specs=[
                block,
                block,
                pl.BlockSpec((tile, width), lambda i, *_: (first + i, 0)),
                once((E, width)),
                far if split else once((E, width)),
                far if split else once((width, D)),
            ]
            + [once((1, NLEN, E))] * len(carried)
            + [far if split else pl.BlockSpec(memory_space=pl.ANY)],
            out_specs=out_specs,
            scratch_shapes=[
                pltpu.VMEM((rows, E), BF16),
                pltpu.VMEM((tile, width), BF16),
                pltpu.VMEM((rows, width), BF16),
                pltpu.VMEM((rows, width), BF16),
            ]
            + scratch,
        ),
        compiler_params=pltpu.CompilerParams(
            dimension_semantics=("arbitrary",),
            vmem_limit_bytes=(60 << 20) if split else VMEM_LIMIT,
        ),
        cost_estimate=pl.CostEstimate(
            flops=steps * (4 * SPANS_STEP * KNB * NLEN * E * width + 2 * tile * width * D),
            bytes_accessed=6 << 20,
            transcendentals=steps * tile * KNB * NLEN * (width // HD),
        ),
        name="decode",
    )(*([blocks] if split else []), own, other, queries, w_key, w_value, w_out, *carried, after)


def body(
    hidden,
    nbr_table,
    nbr_ids,
    w_query,
    w_key,
    w_value,
    w_out,
    enc_query,
    enc_key,
    enc_value,
    enc_out,
):
    store_count = lax.axis_size("store")
    store_rank = lax.axis_index("store")
    seq_count = lax.axis_size("seq")
    seq_rank = lax.axis_index("seq")
    side = math.isqrt(seq_count)
    chips = store_count // 2
    span_count = nbr_ids.shape[0]
    row_requests = span_count * KNB
    per_owner = row_requests // store_count
    blocks_here = nbr_table.shape[0]

    flat_ids = nbr_ids.reshape(-1)
    slot = jnp.arange(row_requests, dtype=jnp.int32)
    rank_key = (flat_ids // blocks_here) * row_requests + slot
    pos = jnp.sum((rank_key[:, None] > rank_key[None, :]).astype(jnp.int32), axis=1)
    by_owner = jnp.sum(jnp.where(pos[None, :] == slot[:, None], slot[None, :], 0), axis=1)
    picked = lax.dynamic_slice_in_dim(by_owner, store_rank * per_owner, per_owner)
    sources = nbr_table[flat_ids[picked] % blocks_here]
    gathered = lax.all_gather(sources, "store", axis=0, tiled=True)
    gathered = pltpu.with_memory_space_constraint(gathered, pltpu.HBM)

    pair_at = jnp.minimum(store_rank, PAIRS - 1) * 128
    weight = jnp.concatenate(
        [
            lax.dynamic_slice_in_dim(enc_key, pair_at, 128, axis=1),
            lax.dynamic_slice_in_dim(enc_value, pair_at, 128, axis=1),
        ],
        axis=1,
    )
    half = weight.shape[0] // 2
    a_four, b_four = stack_fours(
        around(weight[:half], side, False), around(weight[half:], side, True)
    )
    parts = around(a_four, side, True) + around(b_four, side, False)
    rel = jnp.array(REL, jnp.int32)
    y_at, z_at = seq_rank // side, seq_rank % side
    from_rank = jnp.concatenate([(y_at + rel + side) % side, (z_at + rel + side) % side])
    hidden_far = pltpu.with_memory_space_constraint(hidden, pltpu.HBM)
    queries = dot(hidden, w_query).astype(BF16)
    queries = pltpu.with_memory_space_constraint(queries, pltpu.HBM)
    cond = cond_rows(hidden_far, parts, from_rank, queries).reshape(-1, CH, 256)
    own_lane = around_x(cond, chips)
    chip, core = store_rank // 2, store_rank % 2
    lane = 2 * ((chip + rel + chips) % chips)
    pairs = jnp.concatenate([lane + core, lane + 1 - core])

    spans = (jnp.arange(span_count, dtype=jnp.int32) + FIRST) % span_count
    mine = jnp.sum(
        jnp.where(slot[None, :] == (KNB * spans + core)[:, None], pos[None, :], 0), axis=1
    )
    enc_query = pltpu.with_memory_space_constraint(enc_query, pltpu.HBM)
    enc_q = enc_queries(mine, gathered, enc_query)
    own_lane[1:] = hold(own_lane[1:], enc_q)
    conds = own_lane + [swap_cores(block) for block in own_lane]
    part = span_count // 2
    high = encode(0, part, mine, pairs, enc_q, gathered, conds, enc_out, ())
    high_other = swap_cores(high)
    low = encode(part, part, mine, pairs, enc_q, gathered, conds, enc_out, (high,))
    low_other = swap_cores(low)
    carried = tuple(
        lax.ppermute(
            low[:1],
            ("seq", "store"),
            [
                (i * store_count + k, (i + 1) * store_count + (k ^ flip))
                for i in range(seq_count - 1)
                for k in range(store_count)
            ],
        )
        for flip in range(2)
    )
    weights = (queries, w_key, w_value, w_out)
    terms = decode(2, 2, high, high_other, *weights, None, (), low)
    high_out = lax.psum_scatter(terms, "store", scatter_dimension=1, tiled=True)
    kept_1, given_1 = decode(1, 1, low, low_other, *weights, pairs, (), terms)
    taken_1 = swap_cores(given_1)
    kept_0, given_0 = decode(0, 1, low, low_other, *weights, pairs, carried, kept_1)
    taken_0 = swap_cores(given_0)
    sums_1 = core_sums(kept_1, taken_1, (kept_0,))
    got_1 = send_over_x(sums_1, chips)
    sums_0 = core_sums(kept_0, taken_0, sums_1[1:])
    got_0 = send_over_x(sums_0, chips)
    outs = []
    for sums, got in ((sums_0, got_0), (sums_1, got_1)):
        total = sums[0]
        for block in got:
            total = total + block.astype(F32)
        outs.append(total.astype(BF16))
    return jnp.concatenate([*outs, high_out], axis=0)


def solution(mesh):
    in_specs = (
        P("seq", None),
        P("store", None, None),
        P("seq", None),
        P(None, "store"),
        P(None, "store"),
        P(None, "store"),
        P("store", None),
        P(),
        P("seq", None),
        P("seq", None),
        P(),
    )
    out_specs = P("seq", "store")
    return jax.shard_map(body, mesh=mesh, in_specs=in_specs, out_specs=out_specs, check_vma=False)
```

```python
import math

import jax
import jax.numpy as jnp
from jax import lax
from jax.experimental import pallas as pl
from jax.experimental.pallas import tpu as pltpu
from jax.sharding import PartitionSpec as P

D = 4096
HD = 128
E = 896
EHEADS = 14
EHD = 64
CH = 64
NLEN = 128
KNB = 2
PAIRS = E // 128

EPSILON = 1e-06
VMEM_LIMIT = 36 << 20
F32 = jnp.float32
BF16 = jnp.bfloat16
REL = (0, -1, 1, 2)
FIRST = 7


def dot(a, b):
    return jnp.dot(a, b, preferred_element_type=F32)


def grid_route(side, dy, dz):
    return [
        (side * y + z, side * ((y + dy) % side) + (z + dz) % side)
        for y in range(side)
        for z in range(side)
    ]


def around(block, side, along_y):
    got = [block]
    for rel in REL[1:]:
        route = grid_route(side, -rel, 0) if along_y else grid_route(side, 0, -rel)
        got.append(lax.ppermute(block, "seq", route))
    return got


def around_x(block, chips):
    got = [block]
    for rel in REL[1:]:
        route = [
            (2 * x + core, 2 * ((x - rel) % chips) + core) for x in range(chips) for core in range(2)
        ]
        got.append(lax.ppermute(block, "store", route))
    return got


def swap_cores(block):
    count = lax.axis_size("store")
    return lax.ppermute(block, "store", [(i, i ^ 1) for i in range(count)])


def add_kernel(kept_ref, taken_ref, *refs):
    for j, out_ref in enumerate(refs[-4:]):
        total = kept_ref[j].astype(F32) + taken_ref[j].astype(F32)
        out_ref[...] = total.astype(out_ref.dtype)


def core_sums(kept, taken, after):
    vmem = pl.BlockSpec(memory_space=pltpu.VMEM)
    shape = kept.shape[1:]
    return pl.pallas_call(
        add_kernel,
        out_shape=[jax.ShapeDtypeStruct(shape, F32)] + [jax.ShapeDtypeStruct(shape, BF16)] * 3,
        in_specs=[vmem] * 2 + [pl.BlockSpec(memory_space=pl.ANY)] * len(after),
        out_specs=[vmem] * 4,
        compiler_params=pltpu.CompilerParams(vmem_limit_bytes=8 << 20),
        cost_estimate=pl.CostEstimate(flops=1 << 19, bytes_accessed=4 << 20, transcendentals=0),
        name="core_sums",
    )(kept, taken, *after)


def send_over_x(sums, chips):
    got = []
    for j in range(1, 4):
        route = [
            (2 * x + core, 2 * ((x + REL[j]) % chips) + core)
            for x in range(chips)
            for core in range(2)
        ]
        got.append(lax.ppermute(sums[j], "store", route))
    return got


def once(shape):
    return pl.BlockSpec(shape, lambda *_: (0,) * len(shape), pipeline_mode=pl.Buffered(1))


def cond_kernel(src_ref, hidden_ref, *refs):
    a_refs, b_refs, (out_ref, total) = refs[:4], refs[4:8], refs[-2:]
    step = pl.program_id(0)
    for i in range(4):

        @pl.when(step == i)
        def _():
            terms = None if i == 0 else total[...]
            for j in range(4):
                at = pl.multiple_of(src_ref[4 + j] * 256, 256)
                weight = jnp.concatenate([a_refs[i][j], b_refs[j][i]], axis=0)
                term = dot(hidden_ref[:, pl.ds(at, 256)], weight)
                terms = term if terms is None else terms + term
            if i == 3:
                first = FIRST * CH
                out_ref[: terms.shape[0] - first, :] = terms[first:].astype(BF16)
                out_ref[terms.shape[0] - first :, :] = terms[:first].astype(BF16)
            else:
                total[...] = terms


def cond_rows(hidden, parts, sources, after):
    tokens = hidden.shape[0]
    return pl.pallas_call(
        cond_kernel,
        out_shape=jax.ShapeDtypeStruct((tokens, 256), BF16),
        grid_spec=pltpu.PrefetchScalarGridSpec(
            num_scalar_prefetch=1,
            grid=(4,),
            in_specs=[pl.BlockSpec((tokens, D // 4), lambda i, s: (0, s[i]))]
            + [once((4, 128, 256))] * 8
            + [pl.BlockSpec(memory_space=pl.ANY)],
            out_specs=pl.BlockSpec((tokens, 256), lambda i, s: (0, 0)),
            scratch_shapes=[pltpu.VMEM((tokens, 256), F32)],
        ),
        compiler_params=pltpu.CompilerParams(
            dimension_semantics=("arbitrary",), vmem_limit_bytes=VMEM_LIMIT
        ),
        cost_estimate=pl.CostEstimate(
            flops=2 * tokens * D * 256, bytes_accessed=12 << 20, transcendentals=0
        ),
        name="cond_rows",
    )(sources, hidden, *parts, after)


def hold_kernel(*refs):
    count = len(refs) // 2
    for source, target in zip(refs[:count], refs[count + 1 :]):
        target[...] = source[...]


def hold(blocks, after):
    count = len(blocks)
    vmem = pl.BlockSpec(memory_space=pltpu.VMEM)
    return pl.pallas_call(
        hold_kernel,
        out_shape=[jax.ShapeDtypeStruct(block.shape, BF16) for block in blocks],
        in_specs=[vmem] * count + [pl.BlockSpec(memory_space=pl.ANY)],
        out_specs=[vmem] * count,
        compiler_params=pltpu.CompilerParams(vmem_limit_bytes=8 << 20),
        cost_estimate=pl.CostEstimate(flops=0, bytes_accessed=1 << 20, transcendentals=0),
        name="hold",
    )(*blocks, after)


def stack_kernel(*refs):
    for j in range(4):
        refs[8][j] = refs[j][...]
        refs[9][j] = refs[4 + j][...]


def stack_fours(a, b):
    vmem = pl.BlockSpec(memory_space=pltpu.VMEM)
    shape = jax.ShapeDtypeStruct((4, *a[0].shape), BF16)
    return pl.pallas_call(
        stack_kernel,
        out_shape=[shape, shape],
        in_specs=[vmem] * 8,
        out_specs=[vmem] * 2,
        compiler_params=pltpu.CompilerParams(vmem_limit_bytes=8 << 20),
        cost_estimate=pl.CostEstimate(flops=0, bytes_accessed=1 << 20, transcendentals=0),
        name="stack_fours",
    )(*a, *b)


def enc_query_kernel(pos_ref, *refs):
    del pos_ref
    sources, w_ref, out_ref = refs[:4], refs[4], refs[-1]
    rows = []
    for source in sources:
        block = source[0].astype(F32)
        scale = lax.rsqrt(jnp.mean(block * block, axis=-1, keepdims=True) + EPSILON)
        rows.append((block * scale).astype(BF16))
    got = dot(jnp.concatenate(rows, axis=0), w_ref[...]).astype(BF16)
    for n in range(4):
        out_ref[n] = got[n * NLEN : (n + 1) * NLEN]


def enc_queries(pos, gathered, weight):
    count = pos.shape[0]

    def source(n):
        return pl.BlockSpec((1, NLEN, E), lambda i, pos: (pos[4 * i + n], 0, 0))

    return pl.pallas_call(
        enc_query_kernel,
        out_shape=jax.ShapeDtypeStruct((count, NLEN, E), BF16),
        grid_spec=pltpu.PrefetchScalarGridSpec(
            num_scalar_prefetch=1,
            grid=(count // 4,),
            in_specs=[source(n) for n in range(4)] + [once((E, E))],
            out_specs=pl.BlockSpec((4, NLEN, E), lambda i, pos: (i, 0, 0)),
        ),
        compiler_params=pltpu.CompilerParams(
            dimension_semantics=("arbitrary",), vmem_limit_bytes=VMEM_LIMIT
        ),
        cost_estimate=pl.CostEstimate(
            flops=2 * count * NLEN * E * E, bytes_accessed=10 << 20, transcendentals=0
        ),
        name="enc_queries",
    )(pos, *([gathered] * 4), weight)


def encode_kernel(pos_ref, pair_ref, *refs):
    del pos_ref
    sources, conds = refs[:4], refs[4:12]
    query_ref, out_w_ref = refs[12:14]
    out_ref, mixed = refs[-2:]
    row_head = lax.broadcasted_iota(jnp.int32, (128, 128), 0) // EHD
    col_head = lax.broadcasted_iota(jnp.int32, (128, 128), 1) // EHD
    same = row_head == col_head
    zero = jnp.zeros((128, 128), BF16)
    units = [(n, j) for n in range(4) for j in range(8)]

    def two_heads(block):
        return jnp.where(same, jnp.concatenate([block, block], axis=0), zero)

    def score(n, j):
        at = pl.multiple_of(jnp.minimum(pair_ref[j], PAIRS - 1) * 128, 128)
        return lax.dot_general(
            two_heads(conds[j][n, :, :128]),
            query_ref[n, :, pl.ds(at, 128)],
            (((1,), (1,)), ((), ())),
            preferred_element_type=F32,
        ) * (1.0 / math.sqrt(EHD))

    def soften(scores):
        halves = []
        for h in range(2):
            part = scores[h * EHD : (h + 1) * EHD]
            grown = jnp.exp(part - jnp.max(part, axis=0, keepdims=True))
            halves.append((grown * (1.0 / jnp.sum(grown, axis=0, keepdims=True))).astype(BF16))
        return jnp.concatenate(halves, axis=0)

    scores = [score(n, j) for n, j in units]
    weights = [soften(x) for x in scores]
    for weight, (n, j) in zip(weights, units):
        got = lax.dot_general(
            weight,
            two_heads(conds[j][n, :, 128:]),
            (((0,), (0,)), ((), ())),
            preferred_element_type=F32,
        )
        at = pl.multiple_of(pair_ref[j] * 128, 128)
        mixed[n * NLEN : (n + 1) * NLEN, pl.ds(at, 128)] = got.astype(BF16)
    branch = dot(mixed[:, :E], out_w_ref[...])
    for n in range(4):
        rows = branch[n * NLEN : (n + 1) * NLEN]
        out_ref[n] = (sources[n][0].astype(F32) + rows).astype(BF16)


def encode(base, count, pos, pairs, queries, gathered, conds, enc_out, after):
    first = base // 4

    def source(n):
        return pl.BlockSpec((1, NLEN, E), lambda i, pos, pairs: (pos[base + 4 * i + n], 0, 0))

    cond = pl.BlockSpec((4, CH, 256), lambda i, pos, pairs: (first + i, 0, 0))
    return pl.pallas_call(
        encode_kernel,
        out_shape=jax.ShapeDtypeStruct((count, NLEN, E), BF16),
        grid_spec=pltpu.PrefetchScalarGridSpec(
            num_scalar_prefetch=2,
            grid=(count // 4,),
            in_specs=[source(n) for n in range(4)]
            + [cond] * 8
            + [
                pl.BlockSpec((4, NLEN, E), lambda i, pos, pairs: (first + i, 0, 0)),
                once((E, E)),
            ]
            + [pl.BlockSpec(memory_space=pl.ANY)] * len(after),
            out_specs=pl.BlockSpec((4, NLEN, E), lambda i, pos, pairs: (i, 0, 0)),
            scratch_shapes=[pltpu.VMEM((4 * NLEN, 1024), BF16)],
        ),
        compiler_params=pltpu.CompilerParams(
            dimension_semantics=("arbitrary",), vmem_limit_bytes=VMEM_LIMIT
        ),
        cost_estimate=pl.CostEstimate(
            flops=count * NLEN * E * E * 3, bytes_accessed=8 << 20, transcendentals=count << 17
        ),
        name="encode",
    )(pos, pairs, *([gathered] * 4), *conds, queries, enc_out, *after)


SPANS_STEP = 4


def decode_kernel(carries, split, *refs):
    if split:
        block_ref, refs = refs[0], refs[1:]
    own_ref, other_ref, q_ref, wk_ref, wv_ref, wo_ref = refs[:6]
    if split:
        outs, (rows, att, ks, vs, wv_here, wo_here, sems) = refs[-9:-7], refs[-7:]
        load_value = pltpu.make_async_copy(wv_ref, wv_here, sems.at[0])
        load_out = pltpu.make_async_copy(wo_ref, wo_here, sems.at[1])
        load_value.start()
        load_out.start()
        wv_ref, wo_ref = wv_here, wo_here
    else:
        outs, (rows, att, ks, vs) = refs[-5:-4], refs[-4:]
    for j in range(SPANS_STEP):
        for n, ref in enumerate((own_ref, other_ref)):
            at = slice((KNB * j + n) * NLEN, (KNB * j + n + 1) * NLEN)
            rows[at, :] = ref[j]
    if carries:

        @pl.when(pl.program_id(0) == 0)
        def _():
            rows[:NLEN, :] = refs[6][0]
            rows[NLEN : 2 * NLEN, :] = refs[7][0]

    length = KNB * NLEN
    block = rows[...]
    ks[...] = dot(block, wk_ref[...]).astype(BF16)
    units = [(s, p) for s in range(SPANS_STEP) for p in range(q_ref.shape[1] // 256)]
    empty = jnp.zeros((CH, HD), BF16)
    weights = []
    scores = []
    for s, p in units:
        pair = q_ref[s * CH : (s + 1) * CH, p * 256 : (p + 1) * 256]
        both = jnp.concatenate(
            [
                jnp.concatenate([pair[:, :HD], empty], axis=1),
                jnp.concatenate([empty, pair[:, HD:]], axis=1),
            ],
            axis=0,
        )
        scores.append(
            lax.dot_general(
                ks[s * length : (s + 1) * length, p * 256 : (p + 1) * 256],
                both,
                (((1,), (1,)), ((), ())),
                preferred_element_type=F32,
            )
            * (1.0 / math.sqrt(HD))
        )
    for score in scores:
        grown = jnp.exp(score - jnp.max(score, axis=0, keepdims=True))
        weights.append((grown * (1.0 / jnp.sum(grown, axis=0, keepdims=True))).astype(BF16))
    if split:
        load_value.wait()
    vs[...] = dot(block, wv_ref[...]).astype(BF16)
    for weight, (s, p) in zip(weights, units):
        got = lax.dot_general(
            weight,
            vs[s * length : (s + 1) * length, p * 256 : (p + 1) * 256],
            (((0,), (0,)), ((), ())),
            preferred_element_type=F32,
        ).astype(BF16)
        att[s * CH : (s + 1) * CH, p * 256 : p * 256 + HD] = got[:CH, :HD]
        att[s * CH : (s + 1) * CH, p * 256 + HD : (p + 1) * 256] = got[CH:, HD:]
    done = att[...]
    chunk = q_ref.shape[1]

    if split:
        load_out.wait()
        for out_ref, first in ((outs[0], 0), (outs[1], 4)):
            for j in range(4):
                at = pl.multiple_of(block_ref[first + j] * chunk, chunk)
                out_ref[j] = dot(done, wo_ref[:, pl.ds(at, chunk)]).astype(BF16)
    else:
        for j in range(wo_ref.shape[1] // chunk):
            at = slice(j * chunk, (j + 1) * chunk)
            outs[0][:, at] = dot(done, wo_ref[:, at]).astype(BF16)


def decode(first, steps, own, other, queries, w_key, w_value, w_out, blocks, carried, after):
    split = blocks is not None
    width = queries.shape[1]
    tile = SPANS_STEP * CH
    part = first % (own.shape[0] // SPANS_STEP)
    rows = SPANS_STEP * KNB * NLEN
    block = pl.BlockSpec((SPANS_STEP, NLEN, E), lambda i, *_: (part + i, 0, 0))
    far = pl.BlockSpec(memory_space=pltpu.HBM)
    scratch = []
    if split:
        assert steps == 1
        scratch = [
            pltpu.VMEM((E, width), BF16),
            pltpu.VMEM((width, D), BF16),
            pltpu.SemaphoreType.DMA((2,)),
        ]
        out_shape = [jax.ShapeDtypeStruct((4, steps * tile, width), BF16)] * 2
        out_specs = [pl.BlockSpec((4, tile, width), lambda i, *_: (0, i, 0))] * 2
    else:
        out_shape = pltpu.HBM((steps * tile, D), BF16)
        out_specs = pl.BlockSpec((tile, D), lambda i, *_: (i, 0))
    return pl.pallas_call(
        lambda *refs: decode_kernel(len(carried) > 0, split, *refs),
        out_shape=out_shape,
        grid_spec=pltpu.PrefetchScalarGridSpec(
            num_scalar_prefetch=int(split),
            grid=(steps,),
            in_specs=[
                block,
                block,
                pl.BlockSpec((tile, width), lambda i, *_: (first + i, 0)),
                once((E, width)),
                far if split else once((E, width)),
                far if split else once((width, D)),
            ]
            + [once((1, NLEN, E))] * len(carried)
            + [far if split else pl.BlockSpec(memory_space=pl.ANY)],
            out_specs=out_specs,
            scratch_shapes=[
                pltpu.VMEM((rows, E), BF16),
                pltpu.VMEM((tile, width), BF16),
                pltpu.VMEM((rows, width), BF16),
                pltpu.VMEM((rows, width), BF16),
            ]
            + scratch,
        ),
        compiler_params=pltpu.CompilerParams(
            dimension_semantics=("arbitrary",),
            vmem_limit_bytes=(46 << 20) if split else VMEM_LIMIT,
        ),
        cost_estimate=pl.CostEstimate(
            flops=steps * (4 * SPANS_STEP * KNB * NLEN * E * width + 2 * tile * width * D),
            bytes_accessed=6 << 20,
            transcendentals=steps * tile * KNB * NLEN * (width // HD),
        ),
        name="decode",
    )(*([blocks] if split else []), own, other, queries, w_key, w_value, w_out, *carried, after)


def body(
    hidden,
    nbr_table,
    nbr_ids,
    w_query,
    w_key,
    w_value,
    w_out,
    enc_query,
    enc_key,
    enc_value,
    enc_out,
):
    store_count = lax.axis_size("store")
    store_rank = lax.axis_index("store")
    seq_count = lax.axis_size("seq")
    seq_rank = lax.axis_index("seq")
    side = math.isqrt(seq_count)
    chips = store_count // 2
    span_count = nbr_ids.shape[0]
    row_requests = span_count * KNB
    per_owner = row_requests // store_count
    blocks_here = nbr_table.shape[0]

    flat_ids = nbr_ids.reshape(-1)
    slot = jnp.arange(row_requests, dtype=jnp.int32)
    rank_key = (flat_ids // blocks_here) * row_requests + slot
    pos = jnp.sum((rank_key[:, None] > rank_key[None, :]).astype(jnp.int32), axis=1)
    by_owner = jnp.sum(jnp.where(pos[None, :] == slot[:, None], slot[None, :], 0), axis=1)
    picked = lax.dynamic_slice_in_dim(by_owner, store_rank * per_owner, per_owner)
    sources = nbr_table[flat_ids[picked] % blocks_here]
    gathered = lax.all_gather(sources, "store", axis=0, tiled=True)
    gathered = pltpu.with_memory_space_constraint(gathered, pltpu.HBM)

    pair_at = jnp.minimum(store_rank, PAIRS - 1) * 128
    weight = jnp.concatenate(
        [
            lax.dynamic_slice_in_dim(enc_key, pair_at, 128, axis=1),
            lax.dynamic_slice_in_dim(enc_value, pair_at, 128, axis=1),
        ],
        axis=1,
    )
    half = weight.shape[0] // 2
    a_four, b_four = stack_fours(
        around(weight[:half], side, False), around(weight[half:], side, True)
    )
    parts = around(a_four, side, True) + around(b_four, side, False)
    rel = jnp.array(REL, jnp.int32)
    y_at, z_at = seq_rank // side, seq_rank % side
    from_rank = jnp.concatenate([(y_at + rel + side) % side, (z_at + rel + side) % side])
    hidden_far = pltpu.with_memory_space_constraint(hidden, pltpu.HBM)
    queries = dot(hidden, w_query).astype(BF16)
    queries = pltpu.with_memory_space_constraint(queries, pltpu.HBM)
    cond = cond_rows(hidden_far, parts, from_rank, queries).reshape(-1, CH, 256)
    own_lane = around_x(cond, chips)
    chip, core = store_rank // 2, store_rank % 2
    lane = 2 * ((chip + rel + chips) % chips)
    pairs = jnp.concatenate([lane + core, lane + 1 - core])

    spans = (jnp.arange(span_count, dtype=jnp.int32) + FIRST) % span_count
    mine = jnp.sum(
        jnp.where(slot[None, :] == (KNB * spans + core)[:, None], pos[None, :], 0), axis=1
    )
    enc_query = pltpu.with_memory_space_constraint(enc_query, pltpu.HBM)
    enc_q = enc_queries(mine, gathered, enc_query)
    own_lane[1:] = hold(own_lane[1:], enc_q)
    conds = own_lane + [swap_cores(block) for block in own_lane]
    part = span_count // 2
    high = encode(0, part, mine, pairs, enc_q, gathered, conds, enc_out, ())
    high_other = swap_cores(high)
    low = encode(part, part, mine, pairs, enc_q, gathered, conds, enc_out, (high,))
    low_other = swap_cores(low)
    carried = tuple(
        lax.ppermute(
            low[:1],
            ("seq", "store"),
            [
                (i * store_count + k, (i + 1) * store_count + (k ^ flip))
                for i in range(seq_count - 1)
                for k in range(store_count)
            ],
        )
        for flip in range(2)
    )
    terms = decode(2, 2, high, high_other, queries, w_key, w_value, w_out, None, (), low)
    weights = (
        queries,
        w_key,
        pltpu.with_memory_space_constraint(w_value, pltpu.HBM),
        pltpu.with_memory_space_constraint(w_out, pltpu.HBM),
    )
    high_out = lax.psum_scatter(terms, "store", scatter_dimension=1, tiled=True)
    kept_1, given_1 = decode(1, 1, low, low_other, *weights, pairs, (), terms)
    taken_1 = swap_cores(given_1)
    kept_0, given_0 = decode(0, 1, low, low_other, *weights, pairs, carried, kept_1)
    taken_0 = swap_cores(given_0)
    sums_1 = core_sums(kept_1, taken_1, (kept_0,))
    got_1 = send_over_x(sums_1, chips)
    sums_0 = core_sums(kept_0, taken_0, sums_1[1:])
    got_0 = send_over_x(sums_0, chips)
    outs = []
    for sums, got in ((sums_0, got_0), (sums_1, got_1)):
        total = sums[0]
        for block in got:
            total = total + block.astype(F32)
        outs.append(total.astype(BF16))
    return jnp.concatenate([*outs, high_out], axis=0)


def solution(mesh):
    in_specs = (
        P("seq", None),
        P("store", None, None),
        P("seq", None),
        P(None, "store"),
        P(None, "store"),
        P(None, "store"),
        P("store", None),
        P(),
        P("seq", None),
        P("seq", None),
        P(),
    )
    out_specs = P("seq", "store")
    return jax.shard_map(body, mesh=mesh, in_specs=in_specs, out_specs=out_specs, check_vma=False)
```

```python
import math

import jax
import jax.numpy as jnp
from jax import lax
from jax.experimental import pallas as pl
from jax.experimental.pallas import tpu as pltpu
from jax.sharding import PartitionSpec as P

D = 4096
HD = 128
E = 896
EHEADS = 14
EHD = 64
CH = 64
NLEN = 128
KNB = 2
PAIRS = E // 128

EPSILON = 1e-06
VMEM_LIMIT = 36 << 20
F32 = jnp.float32
BF16 = jnp.bfloat16
REL = (0, -1, 1, 2)
FIRST = 7


def dot(a, b):
    return jnp.dot(a, b, preferred_element_type=F32)


def grid_route(side, dy, dz):
    return [
        (side * y + z, side * ((y + dy) % side) + (z + dz) % side)
        for y in range(side)
        for z in range(side)
    ]


def around(block, side, along_y):
    got = [block]
    for rel in REL[1:]:
        route = grid_route(side, -rel, 0) if along_y else grid_route(side, 0, -rel)
        got.append(lax.ppermute(block, "seq", route))
    return got


def around_x(block, chips):
    got = [block]
    for rel in REL[1:]:
        route = [
            (2 * x + core, 2 * ((x - rel) % chips) + core) for x in range(chips) for core in range(2)
        ]
        got.append(lax.ppermute(block, "store", route))
    return got


def swap_cores(block):
    count = lax.axis_size("store")
    return lax.ppermute(block, "store", [(i, i ^ 1) for i in range(count)])


def add_kernel(kept_ref, taken_ref, *refs):
    for j, out_ref in enumerate(refs[-4:]):
        total = kept_ref[j].astype(F32) + taken_ref[j].astype(F32)
        out_ref[...] = total.astype(out_ref.dtype)


def core_sums(kept, taken, after):
    vmem = pl.BlockSpec(memory_space=pltpu.VMEM)
    shape = kept.shape[1:]
    return pl.pallas_call(
        add_kernel,
        out_shape=[jax.ShapeDtypeStruct(shape, F32)] + [jax.ShapeDtypeStruct(shape, BF16)] * 3,
        in_specs=[vmem] * 2 + [pl.BlockSpec(memory_space=pl.ANY)] * len(after),
        out_specs=[vmem] * 4,
        compiler_params=pltpu.CompilerParams(vmem_limit_bytes=8 << 20),
        cost_estimate=pl.CostEstimate(flops=1 << 19, bytes_accessed=4 << 20, transcendentals=0),
        name="core_sums",
    )(kept, taken, *after)


def send_over_x(sums, chips):
    got = []
    for j in range(1, 4):
        route = [
            (2 * x + core, 2 * ((x + REL[j]) % chips) + core)
            for x in range(chips)
            for core in range(2)
        ]
        got.append(lax.ppermute(sums[j], "store", route))
    return got


def once(shape):
    return pl.BlockSpec(shape, lambda *_: (0,) * len(shape), pipeline_mode=pl.Buffered(1))


def cond_kernel(src_ref, hidden_ref, *refs):
    a_refs, b_refs, (out_ref, total) = refs[:4], refs[4:8], refs[-2:]
    step = pl.program_id(0)
    for i in range(4):

        @pl.when(step == i)
        def _():
            terms = None if i == 0 else total[...]
            for j in range(4):
                at = pl.multiple_of(src_ref[4 + j] * 256, 256)
                weight = jnp.concatenate([a_refs[i][j], b_refs[j][i]], axis=0)
                term = dot(hidden_ref[:, pl.ds(at, 256)], weight)
                terms = term if terms is None else terms + term
            if i == 3:
                first = FIRST * CH
                out_ref[: terms.shape[0] - first, :] = terms[first:].astype(BF16)
                out_ref[terms.shape[0] - first :, :] = terms[:first].astype(BF16)
            else:
                total[...] = terms


def cond_rows(hidden, parts, sources, after):
    tokens = hidden.shape[0]
    return pl.pallas_call(
        cond_kernel,
        out_shape=jax.ShapeDtypeStruct((tokens, 256), BF16),
        grid_spec=pltpu.PrefetchScalarGridSpec(
            num_scalar_prefetch=1,
            grid=(4,),
            in_specs=[pl.BlockSpec((tokens, D // 4), lambda i, s: (0, s[i]))]
            + [once((4, 128, 256))] * 8
            + [pl.BlockSpec(memory_space=pl.ANY)],
            out_specs=pl.BlockSpec((tokens, 256), lambda i, s: (0, 0)),
            scratch_shapes=[pltpu.VMEM((tokens, 256), F32)],
        ),
        compiler_params=pltpu.CompilerParams(
            dimension_semantics=("arbitrary",), vmem_limit_bytes=VMEM_LIMIT
        ),
        cost_estimate=pl.CostEstimate(
            flops=2 * tokens * D * 256, bytes_accessed=12 << 20, transcendentals=0
        ),
        name="cond_rows",
    )(sources, hidden, *parts, after)


def hold_kernel(*refs):
    count = len(refs) // 2
    for source, target in zip(refs[:count], refs[count + 1 :]):
        target[...] = source[...]


def hold(blocks, after):
    count = len(blocks)
    vmem = pl.BlockSpec(memory_space=pltpu.VMEM)
    return pl.pallas_call(
        hold_kernel,
        out_shape=[jax.ShapeDtypeStruct(block.shape, BF16) for block in blocks],
        in_specs=[vmem] * count + [pl.BlockSpec(memory_space=pl.ANY)],
        out_specs=[vmem] * count,
        compiler_params=pltpu.CompilerParams(vmem_limit_bytes=8 << 20),
        cost_estimate=pl.CostEstimate(flops=0, bytes_accessed=1 << 20, transcendentals=0),
        name="hold",
    )(*blocks, after)


def stack_kernel(*refs):
    for j in range(4):
        refs[8][j] = refs[j][...]
        refs[9][j] = refs[4 + j][...]


def stack_fours(a, b):
    vmem = pl.BlockSpec(memory_space=pltpu.VMEM)
    shape = jax.ShapeDtypeStruct((4, *a[0].shape), BF16)
    return pl.pallas_call(
        stack_kernel,
        out_shape=[shape, shape],
        in_specs=[vmem] * 8,
        out_specs=[vmem] * 2,
        compiler_params=pltpu.CompilerParams(vmem_limit_bytes=8 << 20),
        cost_estimate=pl.CostEstimate(flops=0, bytes_accessed=1 << 20, transcendentals=0),
        name="stack_fours",
    )(*a, *b)


def enc_query_kernel(pos_ref, *refs):
    del pos_ref
    sources, w_ref, out_ref = refs[:4], refs[4], refs[-1]
    rows = []
    for source in sources:
        block = source[0].astype(F32)
        scale = lax.rsqrt(jnp.mean(block * block, axis=-1, keepdims=True) + EPSILON)
        rows.append((block * scale).astype(BF16))
    got = dot(jnp.concatenate(rows, axis=0), w_ref[...]).astype(BF16)
    for n in range(4):
        out_ref[n] = got[n * NLEN : (n + 1) * NLEN]


def enc_queries(pos, gathered, weight):
    count = pos.shape[0]

    def source(n):
        return pl.BlockSpec((1, NLEN, E), lambda i, pos: (pos[4 * i + n], 0, 0))

    return pl.pallas_call(
        enc_query_kernel,
        out_shape=jax.ShapeDtypeStruct((count, NLEN, E), BF16),
        grid_spec=pltpu.PrefetchScalarGridSpec(
            num_scalar_prefetch=1,
            grid=(count // 4,),
            in_specs=[source(n) for n in range(4)] + [once((E, E))],
            out_specs=pl.BlockSpec((4, NLEN, E), lambda i, pos: (i, 0, 0)),
        ),
        compiler_params=pltpu.CompilerParams(
            dimension_semantics=("arbitrary",), vmem_limit_bytes=VMEM_LIMIT
        ),
        cost_estimate=pl.CostEstimate(
            flops=2 * count * NLEN * E * E, bytes_accessed=10 << 20, transcendentals=0
        ),
        name="enc_queries",
    )(pos, *([gathered] * 4), weight)


def encode_kernel(pos_ref, pair_ref, *refs):
    del pos_ref
    sources, conds = refs[:4], refs[4:12]
    query_ref, out_w_ref = refs[12:14]
    out_ref, mixed = refs[-2:]
    row_head = lax.broadcasted_iota(jnp.int32, (128, 128), 0) // EHD
    col_head = lax.broadcasted_iota(jnp.int32, (128, 128), 1) // EHD
    same = row_head == col_head
    zero = jnp.zeros((128, 128), BF16)
    units = [(n, j) for n in range(4) for j in range(8)]

    def two_heads(block):
        return jnp.where(same, jnp.concatenate([block, block], axis=0), zero)

    def score(n, j):
        at = pl.multiple_of(jnp.minimum(pair_ref[j], PAIRS - 1) * 128, 128)
        return lax.dot_general(
            two_heads(conds[j][n, :, :128]),
            query_ref[n, :, pl.ds(at, 128)],
            (((1,), (1,)), ((), ())),
            preferred_element_type=F32,
        ) * (1.0 / math.sqrt(EHD))

    def soften(scores):
        halves = []
        for h in range(2):
            part = scores[h * EHD : (h + 1) * EHD]
            grown = jnp.exp(part - jnp.max(part, axis=0, keepdims=True))
            halves.append((grown * (1.0 / jnp.sum(grown, axis=0, keepdims=True))).astype(BF16))
        return jnp.concatenate(halves, axis=0)

    scores = [score(n, j) for n, j in units]
    weights = [soften(x) for x in scores]
    for weight, (n, j) in zip(weights, units):
        got = lax.dot_general(
            weight,
            two_heads(conds[j][n, :, 128:]),
            (((0,), (0,)), ((), ())),
            preferred_element_type=F32,
        )
        at = pl.multiple_of(pair_ref[j] * 128, 128)
        mixed[n * NLEN : (n + 1) * NLEN, pl.ds(at, 128)] = got.astype(BF16)
    branch = dot(mixed[:, :E], out_w_ref[...])
    for n in range(4):
        rows = branch[n * NLEN : (n + 1) * NLEN]
        out_ref[n] = (sources[n][0].astype(F32) + rows).astype(BF16)


def encode(base, count, pos, pairs, queries, gathered, conds, enc_out, after):
    first = base // 4

    def source(n):
        return pl.BlockSpec((1, NLEN, E), lambda i, pos, pairs: (pos[base + 4 * i + n], 0, 0))

    cond = pl.BlockSpec((4, CH, 256), lambda i, pos, pairs: (first + i, 0, 0))
    return pl.pallas_call(
        encode_kernel,
        out_shape=jax.ShapeDtypeStruct((count, NLEN, E), BF16),
        grid_spec=pltpu.PrefetchScalarGridSpec(
            num_scalar_prefetch=2,
            grid=(count // 4,),
            in_specs=[source(n) for n in range(4)]
            + [cond] * 8
            + [
                pl.BlockSpec((4, NLEN, E), lambda i, pos, pairs: (first + i, 0, 0)),
                once((E, E)),
            ]
            + [pl.BlockSpec(memory_space=pl.ANY)] * len(after),
            out_specs=pl.BlockSpec((4, NLEN, E), lambda i, pos, pairs: (i, 0, 0)),
            scratch_shapes=[pltpu.VMEM((4 * NLEN, 1024), BF16)],
        ),
        compiler_params=pltpu.CompilerParams(
            dimension_semantics=("arbitrary",), vmem_limit_bytes=VMEM_LIMIT
        ),
        cost_estimate=pl.CostEstimate(
            flops=count * NLEN * E * E * 3, bytes_accessed=8 << 20, transcendentals=count << 17
        ),
        name="encode",
    )(pos, pairs, *([gathered] * 4), *conds, queries, enc_out, *after)


SPANS_STEP = 4


def decode_kernel(carries, split, *refs):
    if split:
        block_ref, refs = refs[0], refs[1:]
    own_ref, other_ref, q_ref, wk_ref, wv_ref, wo_ref = refs[:6]
    if split:
        outs, (rows, att, ks, vs, wv_here, wo_here, sems) = refs[-9:-7], refs[-7:]
        load_value = pltpu.make_async_copy(wv_ref, wv_here, sems.at[0])
        load_out = pltpu.make_async_copy(wo_ref, wo_here, sems.at[1])
        load_value.start()
        load_out.start()
        wv_ref, wo_ref = wv_here, wo_here
    else:
        outs, (rows, att, ks, vs) = refs[-5:-4], refs[-4:]
    for j in range(SPANS_STEP):
        for n, ref in enumerate((own_ref, other_ref)):
            at = slice((KNB * j + n) * NLEN, (KNB * j + n + 1) * NLEN)
            rows[at, :] = ref[j]
    if carries:

        @pl.when(pl.program_id(0) == 0)
        def _():
            rows[:NLEN, :] = refs[6][0]
            rows[NLEN : 2 * NLEN, :] = refs[7][0]

    length = KNB * NLEN
    block = rows[...]
    ks[...] = dot(block, wk_ref[...]).astype(BF16)
    units = [(s, p) for s in range(SPANS_STEP) for p in range(q_ref.shape[1] // 256)]
    empty = jnp.zeros((CH, HD), BF16)
    weights = []
    scores = []
    for s, p in units:
        pair = q_ref[s * CH : (s + 1) * CH, p * 256 : (p + 1) * 256]
        both = jnp.concatenate(
            [
                jnp.concatenate([pair[:, :HD], empty], axis=1),
                jnp.concatenate([empty, pair[:, HD:]], axis=1),
            ],
            axis=0,
        )
        scores.append(
            lax.dot_general(
                ks[s * length : (s + 1) * length, p * 256 : (p + 1) * 256],
                both,
                (((1,), (1,)), ((), ())),
                preferred_element_type=F32,
            )
            * (1.0 / math.sqrt(HD))
        )
    for score in scores:
        grown = jnp.exp(score - jnp.max(score, axis=0, keepdims=True))
        weights.append((grown * (1.0 / jnp.sum(grown, axis=0, keepdims=True))).astype(BF16))
    if split:
        load_value.wait()
    vs[...] = dot(block, wv_ref[...]).astype(BF16)
    for weight, (s, p) in zip(weights, units):
        got = lax.dot_general(
            weight,
            vs[s * length : (s + 1) * length, p * 256 : (p + 1) * 256],
            (((0,), (0,)), ((), ())),
            preferred_element_type=F32,
        ).astype(BF16)
        att[s * CH : (s + 1) * CH, p * 256 : p * 256 + HD] = got[:CH, :HD]
        att[s * CH : (s + 1) * CH, p * 256 + HD : (p + 1) * 256] = got[CH:, HD:]
    done = att[...]
    chunk = q_ref.shape[1]

    if split:
        load_out.wait()
        for out_ref, first in ((outs[0], 0), (outs[1], 4)):
            for j in range(4):
                at = pl.multiple_of(block_ref[first + j] * chunk, chunk)
                out_ref[j] = dot(done, wo_ref[:, pl.ds(at, chunk)]).astype(BF16)
    else:
        for j in range(wo_ref.shape[1] // chunk):
            at = slice(j * chunk, (j + 1) * chunk)
            outs[0][:, at] = dot(done, wo_ref[:, at]).astype(BF16)


def decode(first, steps, own, other, queries, w_key, w_value, w_out, blocks, carried, after):
    split = blocks is not None
    width = queries.shape[1]
    tile = SPANS_STEP * CH
    part = first % (own.shape[0] // SPANS_STEP)
    rows = SPANS_STEP * KNB * NLEN
    block = pl.BlockSpec((SPANS_STEP, NLEN, E), lambda i, *_: (part + i, 0, 0))
    far = pl.BlockSpec(memory_space=pltpu.HBM)
    scratch = []
    if split:
        assert steps == 1
        scratch = [
            pltpu.VMEM((E, width), BF16),
            pltpu.VMEM((width, D), BF16),
            pltpu.SemaphoreType.DMA((2,)),
        ]
        out_shape = [jax.ShapeDtypeStruct((4, steps * tile, width), BF16)] * 2
        out_specs = [pl.BlockSpec((4, tile, width), lambda i, *_: (0, i, 0))] * 2
    else:
        out_shape = pltpu.HBM((steps * tile, D), BF16)
        out_specs = pl.BlockSpec((tile, D), lambda i, *_: (i, 0))
    return pl.pallas_call(
        lambda *refs: decode_kernel(len(carried) > 0, split, *refs),
        out_shape=out_shape,
        grid_spec=pltpu.PrefetchScalarGridSpec(
            num_scalar_prefetch=int(split),
            grid=(steps,),
            in_specs=[
                block,
                block,
                pl.BlockSpec((tile, width), lambda i, *_: (first + i, 0)),
                once((E, width)),
                far if split else once((E, width)),
                far if split else once((width, D)),
            ]
            + [once((1, NLEN, E))] * len(carried)
            + [far if split else pl.BlockSpec(memory_space=pl.ANY)],
            out_specs=out_specs,
            scratch_shapes=[
                pltpu.VMEM((rows, E), BF16),
                pltpu.VMEM((tile, width), BF16),
                pltpu.VMEM((rows, width), BF16),
                pltpu.VMEM((rows, width), BF16),
            ]
            + scratch,
        ),
        compiler_params=pltpu.CompilerParams(
            dimension_semantics=("arbitrary",),
            vmem_limit_bytes=(46 << 20) if split else VMEM_LIMIT,
        ),
        cost_estimate=pl.CostEstimate(
            flops=steps * (4 * SPANS_STEP * KNB * NLEN * E * width + 2 * tile * width * D),
            bytes_accessed=6 << 20,
            transcendentals=steps * tile * KNB * NLEN * (width // HD),
        ),
        name="decode",
    )(*([blocks] if split else []), own, other, queries, w_key, w_value, w_out, *carried, after)


def body(
    hidden,
    nbr_table,
    nbr_ids,
    w_query,
    w_key,
    w_value,
    w_out,
    enc_query,
    enc_key,
    enc_value,
    enc_out,
):
    store_count = lax.axis_size("store")
    store_rank = lax.axis_index("store")
    seq_count = lax.axis_size("seq")
    seq_rank = lax.axis_index("seq")
    side = math.isqrt(seq_count)
    chips = store_count // 2
    span_count = nbr_ids.shape[0]
    row_requests = span_count * KNB
    per_owner = row_requests // store_count
    blocks_here = nbr_table.shape[0]

    flat_ids = nbr_ids.reshape(-1)
    slot = jnp.arange(row_requests, dtype=jnp.int32)
    rank_key = (flat_ids // blocks_here) * row_requests + slot
    pos = jnp.sum((rank_key[:, None] > rank_key[None, :]).astype(jnp.int32), axis=1)
    by_owner = jnp.sum(jnp.where(pos[None, :] == slot[:, None], slot[None, :], 0), axis=1)
    picked = lax.dynamic_slice_in_dim(by_owner, store_rank * per_owner, per_owner)
    sources = nbr_table[flat_ids[picked] % blocks_here]
    gathered = lax.all_gather(sources, "store", axis=0, tiled=True)
    gathered = pltpu.with_memory_space_constraint(gathered, pltpu.HBM)

    pair_at = jnp.minimum(store_rank, PAIRS - 1) * 128
    weight = jnp.concatenate(
        [
            lax.dynamic_slice_in_dim(enc_key, pair_at, 128, axis=1),
            lax.dynamic_slice_in_dim(enc_value, pair_at, 128, axis=1),
        ],
        axis=1,
    )
    half = weight.shape[0] // 2
    a_four, b_four = stack_fours(
        around(weight[:half], side, False), around(weight[half:], side, True)
    )
    parts = around(a_four, side, True) + around(b_four, side, False)
    rel = jnp.array(REL, jnp.int32)
    y_at, z_at = seq_rank // side, seq_rank % side
    from_rank = jnp.concatenate([(y_at + rel + side) % side, (z_at + rel + side) % side])
    hidden_far = pltpu.with_memory_space_constraint(hidden, pltpu.HBM)
    queries = dot(hidden, w_query).astype(BF16)
    queries = pltpu.with_memory_space_constraint(queries, pltpu.HBM)
    cond = cond_rows(hidden_far, parts, from_rank, queries).reshape(-1, CH, 256)
    own_lane = around_x(cond, chips)
    chip, core = store_rank // 2, store_rank % 2
    lane = 2 * ((chip + rel + chips) % chips)
    pairs = jnp.concatenate([lane + core, lane + 1 - core])

    spans = (jnp.arange(span_count, dtype=jnp.int32) + FIRST) % span_count
    mine = jnp.sum(
        jnp.where(slot[None, :] == (KNB * spans + core)[:, None], pos[None, :], 0), axis=1
    )
    enc_query = pltpu.with_memory_space_constraint(enc_query, pltpu.HBM)
    enc_q = enc_queries(mine, gathered, enc_query)
    own_lane[1:] = hold(own_lane[1:], enc_q)
    conds = own_lane + [swap_cores(block) for block in own_lane]
    conds[4] = pltpu.with_memory_space_constraint(conds[4], pltpu.HBM)
    part = span_count // 2
    high = encode(0, part, mine, pairs, enc_q, gathered, conds, enc_out, ())
    high_other = swap_cores(high)
    low = encode(part, part, mine, pairs, enc_q, gathered, conds, enc_out, (high,))
    low_other = swap_cores(low)
    carried = tuple(
        lax.ppermute(
            low[:1],
            ("seq", "store"),
            [
                (i * store_count + k, (i + 1) * store_count + (k ^ flip))
                for i in range(seq_count - 1)
                for k in range(store_count)
            ],
        )
        for flip in range(2)
    )
    terms = decode(2, 2, high, high_other, queries, w_key, w_value, w_out, None, (), low)
    weights = (
        queries,
        w_key,
        pltpu.with_memory_space_constraint(w_value, pltpu.HBM),
        pltpu.with_memory_space_constraint(w_out, pltpu.HBM),
    )
    high_out = lax.psum_scatter(terms, "store", scatter_dimension=1, tiled=True)
    kept_1, given_1 = decode(1, 1, low, low_other, *weights, pairs, (), terms)
    taken_1 = swap_cores(given_1)
    kept_0, given_0 = decode(0, 1, low, low_other, *weights, pairs, carried, kept_1)
    taken_0 = swap_cores(given_0)
    sums_1 = core_sums(kept_1, taken_1, (kept_0,))
    got_1 = send_over_x(sums_1, chips)
    sums_0 = core_sums(kept_0, taken_0, sums_1[1:])
    got_0 = send_over_x(sums_0, chips)
    outs = []
    for sums, got in ((sums_0, got_0), (sums_1, got_1)):
        total = sums[0]
        for block in got:
            total = total + block.astype(F32)
        outs.append(total.astype(BF16))
    return jnp.concatenate([*outs, high_out], axis=0)


def solution(mesh):
    in_specs = (
        P("seq", None),
        P("store", None, None),
        P("seq", None),
        P(None, "store"),
        P(None, "store"),
        P(None, "store"),
        P("store", None),
        P(),
        P("seq", None),
        P("seq", None),
        P(),
    )
    out_specs = P("seq", "store")
    return jax.shard_map(body, mesh=mesh, in_specs=in_specs, out_specs=out_specs, check_vma=False)
```

```python
import math

import jax
import jax.numpy as jnp
from jax import lax
from jax.experimental import pallas as pl
from jax.experimental.pallas import tpu as pltpu
from jax.sharding import PartitionSpec as P

D = 4096
HD = 128
E = 896
EHEADS = 14
EHD = 64
CH = 64
NLEN = 128
KNB = 2
PAIRS = E // 128

EPSILON = 1e-06
VMEM_LIMIT = 36 << 20
F32 = jnp.float32
BF16 = jnp.bfloat16
REL = (0, -1, 1, 2)
FIRST = 7


def dot(a, b):
    return jnp.dot(a, b, preferred_element_type=F32)


def grid_route(side, dy, dz):
    return [
        (side * y + z, side * ((y + dy) % side) + (z + dz) % side)
        for y in range(side)
        for z in range(side)
    ]


def around(block, side, along_y):
    got = [block]
    for rel in REL[1:]:
        route = grid_route(side, -rel, 0) if along_y else grid_route(side, 0, -rel)
        got.append(lax.ppermute(block, "seq", route))
    return got


def around_x(block, chips):
    got = [block]
    for rel in REL[1:]:
        route = [
            (2 * x + core, 2 * ((x - rel) % chips) + core) for x in range(chips) for core in range(2)
        ]
        got.append(lax.ppermute(block, "store", route))
    return got


def swap_cores(block):
    count = lax.axis_size("store")
    return lax.ppermute(block, "store", [(i, i ^ 1) for i in range(count)])


def add_kernel(kept_ref, taken_ref, *refs):
    for j, out_ref in enumerate(refs[-4:]):
        total = kept_ref[j].astype(F32) + taken_ref[j].astype(F32)
        out_ref[...] = total.astype(out_ref.dtype)


def core_sums(kept, taken, after):
    vmem = pl.BlockSpec(memory_space=pltpu.VMEM)
    shape = kept.shape[1:]
    return pl.pallas_call(
        add_kernel,
        out_shape=[jax.ShapeDtypeStruct(shape, F32)] + [jax.ShapeDtypeStruct(shape, BF16)] * 3,
        in_specs=[vmem] * 2 + [pl.BlockSpec(memory_space=pl.ANY)] * len(after),
        out_specs=[vmem] * 4,
        compiler_params=pltpu.CompilerParams(vmem_limit_bytes=8 << 20),
        cost_estimate=pl.CostEstimate(flops=1 << 19, bytes_accessed=4 << 20, transcendentals=0),
        name="core_sums",
    )(kept, taken, *after)


def send_over_x(sums, chips):
    got = []
    for j in range(1, 4):
        route = [
            (2 * x + core, 2 * ((x + REL[j]) % chips) + core)
            for x in range(chips)
            for core in range(2)
        ]
        got.append(lax.ppermute(sums[j], "store", route))
    return got


def once(shape):
    return pl.BlockSpec(shape, lambda *_: (0,) * len(shape), pipeline_mode=pl.Buffered(1))


def cond_kernel(src_ref, hidden_ref, *refs):
    a_refs, b_refs, (out_ref, total) = refs[:4], refs[4:8], refs[-2:]
    step = pl.program_id(0)
    for i in range(4):

        @pl.when(step == i)
        def _():
            terms = None if i == 0 else total[...]
            for j in range(4):
                at = pl.multiple_of(src_ref[4 + j] * 256, 256)
                weight = jnp.concatenate([a_refs[i][j], b_refs[j][i]], axis=0)
                term = dot(hidden_ref[:, pl.ds(at, 256)], weight)
                terms = term if terms is None else terms + term
            if i == 3:
                first = FIRST * CH
                out_ref[: terms.shape[0] - first, :] = terms[first:].astype(BF16)
                out_ref[terms.shape[0] - first :, :] = terms[:first].astype(BF16)
            else:
                total[...] = terms


def cond_rows(hidden, parts, sources, after):
    tokens = hidden.shape[0]
    return pl.pallas_call(
        cond_kernel,
        out_shape=jax.ShapeDtypeStruct((tokens, 256), BF16),
        grid_spec=pltpu.PrefetchScalarGridSpec(
            num_scalar_prefetch=1,
            grid=(4,),
            in_specs=[pl.BlockSpec((tokens, D // 4), lambda i, s: (0, s[i]))]
            + [once((4, 128, 256))] * 8
            + [pl.BlockSpec(memory_space=pl.ANY)],
            out_specs=pl.BlockSpec((tokens, 256), lambda i, s: (0, 0)),
            scratch_shapes=[pltpu.VMEM((tokens, 256), F32)],
        ),
        compiler_params=pltpu.CompilerParams(
            dimension_semantics=("arbitrary",), vmem_limit_bytes=VMEM_LIMIT
        ),
        cost_estimate=pl.CostEstimate(
            flops=2 * tokens * D * 256, bytes_accessed=12 << 20, transcendentals=0
        ),
        name="cond_rows",
    )(sources, hidden, *parts, after)


def hold_kernel(*refs):
    count = len(refs) // 2
    for source, target in zip(refs[:count], refs[count + 1 :]):
        target[...] = source[...]


def hold(blocks, after):
    count = len(blocks)
    vmem = pl.BlockSpec(memory_space=pltpu.VMEM)
    return pl.pallas_call(
        hold_kernel,
        out_shape=[jax.ShapeDtypeStruct(block.shape, BF16) for block in blocks],
        in_specs=[vmem] * count + [pl.BlockSpec(memory_space=pl.ANY)],
        out_specs=[vmem] * count,
        compiler_params=pltpu.CompilerParams(vmem_limit_bytes=8 << 20),
        cost_estimate=pl.CostEstimate(flops=0, bytes_accessed=1 << 20, transcendentals=0),
        name="hold",
    )(*blocks, after)


def stack_kernel(*refs):
    for j in range(4):
        refs[8][j] = refs[j][...]
        refs[9][j] = refs[4 + j][...]


def stack_fours(a, b):
    vmem = pl.BlockSpec(memory_space=pltpu.VMEM)
    shape = jax.ShapeDtypeStruct((4, *a[0].shape), BF16)
    return pl.pallas_call(
        stack_kernel,
        out_shape=[shape, shape],
        in_specs=[vmem] * 8,
        out_specs=[vmem] * 2,
        compiler_params=pltpu.CompilerParams(vmem_limit_bytes=8 << 20),
        cost_estimate=pl.CostEstimate(flops=0, bytes_accessed=1 << 20, transcendentals=0),
        name="stack_fours",
    )(*a, *b)


def enc_query_kernel(pos_ref, *refs):
    del pos_ref
    sources, w_ref, out_ref = refs[:4], refs[4], refs[-1]
    scales = []
    for source in sources:
        block = source[0].astype(F32)
        scales.append(lax.rsqrt(jnp.mean(block * block, axis=-1, keepdims=True) + EPSILON))
    got = dot(jnp.concatenate([source[0] for source in sources], axis=0), w_ref[...])
    got = (got * jnp.concatenate(scales, axis=0)).astype(BF16)
    for n in range(4):
        out_ref[n] = got[n * NLEN : (n + 1) * NLEN]


def enc_queries(pos, gathered, weight):
    count = pos.shape[0]

    def source(n):
        return pl.BlockSpec((1, NLEN, E), lambda i, pos: (pos[4 * i + n], 0, 0))

    return pl.pallas_call(
        enc_query_kernel,
        out_shape=jax.ShapeDtypeStruct((count, NLEN, E), BF16),
        grid_spec=pltpu.PrefetchScalarGridSpec(
            num_scalar_prefetch=1,
            grid=(count // 4,),
            in_specs=[source(n) for n in range(4)] + [once((E, E))],
            out_specs=pl.BlockSpec((4, NLEN, E), lambda i, pos: (i, 0, 0)),
        ),
        compiler_params=pltpu.CompilerParams(
            dimension_semantics=("arbitrary",), vmem_limit_bytes=VMEM_LIMIT
        ),
        cost_estimate=pl.CostEstimate(
            flops=2 * count * NLEN * E * E, bytes_accessed=10 << 20, transcendentals=0
        ),
        name="enc_queries",
    )(pos, *([gathered] * 4), weight)


def encode_kernel(pos_ref, pair_ref, *refs):
    del pos_ref
    sources, conds = refs[:4], refs[4:12]
    query_ref, out_w_ref = refs[12:14]
    out_ref, mixed = refs[-2:]
    row_head = lax.broadcasted_iota(jnp.int32, (128, 128), 0) // EHD
    col_head = lax.broadcasted_iota(jnp.int32, (128, 128), 1) // EHD
    same = row_head == col_head
    zero = jnp.zeros((128, 128), BF16)
    units = [(n, j) for n in range(4) for j in range(8)]

    def two_heads(block):
        return jnp.where(same, jnp.concatenate([block, block], axis=0), zero)

    def score(n, j):
        at = pl.multiple_of(jnp.minimum(pair_ref[j], PAIRS - 1) * 128, 128)
        return lax.dot_general(
            two_heads(conds[j][n, :, :128]),
            query_ref[n, :, pl.ds(at, 128)],
            (((1,), (1,)), ((), ())),
            preferred_element_type=F32,
        ) * (1.0 / math.sqrt(EHD))

    def soften(scores):
        halves = []
        for h in range(2):
            part = scores[h * EHD : (h + 1) * EHD]
            grown = jnp.exp(part - jnp.max(part, axis=0, keepdims=True))
            halves.append((grown * (1.0 / jnp.sum(grown, axis=0, keepdims=True))).astype(BF16))
        return jnp.concatenate(halves, axis=0)

    scores = [score(n, j) for n, j in units]
    weights = [soften(x) for x in scores]
    for weight, (n, j) in zip(weights, units):
        got = lax.dot_general(
            weight,
            two_heads(conds[j][n, :, 128:]),
            (((0,), (0,)), ((), ())),
            preferred_element_type=F32,
        )
        at = pl.multiple_of(pair_ref[j] * 128, 128)
        mixed[n * NLEN : (n + 1) * NLEN, pl.ds(at, 128)] = got.astype(BF16)
    branch = dot(mixed[:, :E], out_w_ref[...])
    for n in range(4):
        rows = branch[n * NLEN : (n + 1) * NLEN]
        out_ref[n] = (sources[n][0].astype(F32) + rows).astype(BF16)


def encode(base, count, pos, pairs, queries, gathered, conds, enc_out, after):
    first = base // 4

    def source(n):
        return pl.BlockSpec((1, NLEN, E), lambda i, pos, pairs: (pos[base + 4 * i + n], 0, 0))

    cond = pl.BlockSpec((4, CH, 256), lambda i, pos, pairs: (first + i, 0, 0))
    return pl.pallas_call(
        encode_kernel,
        out_shape=jax.ShapeDtypeStruct((count, NLEN, E), BF16),
        grid_spec=pltpu.PrefetchScalarGridSpec(
            num_scalar_prefetch=2,
            grid=(count // 4,),
            in_specs=[source(n) for n in range(4)]
            + [cond] * 8
            + [
                pl.BlockSpec((4, NLEN, E), lambda i, pos, pairs: (first + i, 0, 0)),
                once((E, E)),
            ]
            + [pl.BlockSpec(memory_space=pl.ANY)] * len(after),
            out_specs=pl.BlockSpec((4, NLEN, E), lambda i, pos, pairs: (i, 0, 0)),
            scratch_shapes=[pltpu.VMEM((4 * NLEN, 1024), BF16)],
        ),
        compiler_params=pltpu.CompilerParams(
            dimension_semantics=("arbitrary",), vmem_limit_bytes=VMEM_LIMIT
        ),
        cost_estimate=pl.CostEstimate(
            flops=count * NLEN * E * E * 3, bytes_accessed=8 << 20, transcendentals=count << 17
        ),
        name="encode",
    )(pos, pairs, *([gathered] * 4), *conds, queries, enc_out, *after)


SPANS_STEP = 4


def decode_kernel(carries, split, *refs):
    if split:
        block_ref, refs = refs[0], refs[1:]
    own_ref, other_ref, q_ref, wk_ref, wv_ref, wo_ref = refs[:6]
    if split:
        outs, (rows, att, ks, vs, wv_here, wo_here, sems) = refs[-9:-7], refs[-7:]
        load_value = pltpu.make_async_copy(wv_ref, wv_here, sems.at[0])
        load_out = pltpu.make_async_copy(wo_ref, wo_here, sems.at[1])
        load_value.start()
        load_out.start()
        wv_ref, wo_ref = wv_here, wo_here
    else:
        outs, (rows, att, ks, vs) = refs[-5:-4], refs[-4:]
    for j in range(SPANS_STEP):
        for n, ref in enumerate((own_ref, other_ref)):
            at = slice((KNB * j + n) * NLEN, (KNB * j + n + 1) * NLEN)
            rows[at, :] = ref[j]
    if carries:

        @pl.when(pl.program_id(0) == 0)
        def _():
            rows[:NLEN, :] = refs[6][0]
            rows[NLEN : 2 * NLEN, :] = refs[7][0]

    length = KNB * NLEN
    block = rows[...]
    ks[...] = dot(block, wk_ref[...]).astype(BF16)
    units = [(s, p) for s in range(SPANS_STEP) for p in range(q_ref.shape[1] // 256)]
    empty = jnp.zeros((CH, HD), BF16)
    weights = []
    scores = []
    for s, p in units:
        pair = q_ref[s * CH : (s + 1) * CH, p * 256 : (p + 1) * 256]
        both = jnp.concatenate(
            [
                jnp.concatenate([pair[:, :HD], empty], axis=1),
                jnp.concatenate([empty, pair[:, HD:]], axis=1),
            ],
            axis=0,
        )
        scores.append(
            lax.dot_general(
                ks[s * length : (s + 1) * length, p * 256 : (p + 1) * 256],
                both,
                (((1,), (1,)), ((), ())),
                preferred_element_type=F32,
            )
            * (1.0 / math.sqrt(HD))
        )
    for score in scores:
        grown = jnp.exp(score - jnp.max(score, axis=0, keepdims=True))
        weights.append((grown * (1.0 / jnp.sum(grown, axis=0, keepdims=True))).astype(BF16))
    if split:
        load_value.wait()
    vs[...] = dot(block, wv_ref[...]).astype(BF16)
    for weight, (s, p) in zip(weights, units):
        got = lax.dot_general(
            weight,
            vs[s * length : (s + 1) * length, p * 256 : (p + 1) * 256],
            (((0,), (0,)), ((), ())),
            preferred_element_type=F32,
        ).astype(BF16)
        att[s * CH : (s + 1) * CH, p * 256 : p * 256 + HD] = got[:CH, :HD]
        att[s * CH : (s + 1) * CH, p * 256 + HD : (p + 1) * 256] = got[CH:, HD:]
    done = att[...]
    chunk = q_ref.shape[1]

    if split:
        load_out.wait()
        for out_ref, first in ((outs[0], 0), (outs[1], 4)):
            for j in range(4):
                at = pl.multiple_of(block_ref[first + j] * chunk, chunk)
                out_ref[j] = dot(done, wo_ref[:, pl.ds(at, chunk)]).astype(BF16)
    else:
        for j in range(wo_ref.shape[1] // chunk):
            at = slice(j * chunk, (j + 1) * chunk)
            outs[0][:, at] = dot(done, wo_ref[:, at]).astype(BF16)


def decode(first, steps, own, other, queries, w_key, w_value, w_out, blocks, carried, after):
    split = blocks is not None
    width = queries.shape[1]
    tile = SPANS_STEP * CH
    part = first % (own.shape[0] // SPANS_STEP)
    rows = SPANS_STEP * KNB * NLEN
    block = pl.BlockSpec((SPANS_STEP, NLEN, E), lambda i, *_: (part + i, 0, 0))
    far = pl.BlockSpec(memory_space=pltpu.HBM)
    scratch = []
    if split:
        assert steps == 1
        scratch = [
            pltpu.VMEM((E, width), BF16),
            pltpu.VMEM((width, D), BF16),
            pltpu.SemaphoreType.DMA((2,)),
        ]
        out_shape = [jax.ShapeDtypeStruct((4, steps * tile, width), BF16)] * 2
        out_specs = [pl.BlockSpec((4, tile, width), lambda i, *_: (0, i, 0))] * 2
    else:
        out_shape = pltpu.HBM((steps * tile, D), BF16)
        out_specs = pl.BlockSpec((tile, D), lambda i, *_: (i, 0))
    return pl.pallas_call(
        lambda *refs: decode_kernel(len(carried) > 0, split, *refs),
        out_shape=out_shape,
        grid_spec=pltpu.PrefetchScalarGridSpec(
            num_scalar_prefetch=int(split),
            grid=(steps,),
            in_specs=[
                block,
                block,
                pl.BlockSpec((tile, width), lambda i, *_: (first + i, 0)),
                once((E, width)),
                far if split else once((E, width)),
                far if split else once((width, D)),
            ]
            + [once((1, NLEN, E))] * len(carried)
            + [far if split else pl.BlockSpec(memory_space=pl.ANY)],
            out_specs=out_specs,
            scratch_shapes=[
                pltpu.VMEM((rows, E), BF16),
                pltpu.VMEM((tile, width), BF16),
                pltpu.VMEM((rows, width), BF16),
                pltpu.VMEM((rows, width), BF16),
            ]
            + scratch,
        ),
        compiler_params=pltpu.CompilerParams(
            dimension_semantics=("arbitrary",),
            vmem_limit_bytes=(46 << 20) if split else VMEM_LIMIT,
        ),
        cost_estimate=pl.CostEstimate(
            flops=steps * (4 * SPANS_STEP * KNB * NLEN * E * width + 2 * tile * width * D),
            bytes_accessed=6 << 20,
            transcendentals=steps * tile * KNB * NLEN * (width // HD),
        ),
        name="decode",
    )(*([blocks] if split else []), own, other, queries, w_key, w_value, w_out, *carried, after)


def body(
    hidden,
    nbr_table,
    nbr_ids,
    w_query,
    w_key,
    w_value,
    w_out,
    enc_query,
    enc_key,
    enc_value,
    enc_out,
):
    store_count = lax.axis_size("store")
    store_rank = lax.axis_index("store")
    seq_count = lax.axis_size("seq")
    seq_rank = lax.axis_index("seq")
    side = math.isqrt(seq_count)
    chips = store_count // 2
    span_count = nbr_ids.shape[0]
    row_requests = span_count * KNB
    per_owner = row_requests // store_count
    blocks_here = nbr_table.shape[0]

    flat_ids = nbr_ids.reshape(-1)
    slot = jnp.arange(row_requests, dtype=jnp.int32)
    rank_key = (flat_ids // blocks_here) * row_requests + slot
    pos = jnp.sum((rank_key[:, None] > rank_key[None, :]).astype(jnp.int32), axis=1)
    by_owner = jnp.sum(jnp.where(pos[None, :] == slot[:, None], slot[None, :], 0), axis=1)
    picked = lax.dynamic_slice_in_dim(by_owner, store_rank * per_owner, per_owner)
    sources = nbr_table[flat_ids[picked] % blocks_here]
    gathered = lax.all_gather(sources, "store", axis=0, tiled=True)
    gathered = pltpu.with_memory_space_constraint(gathered, pltpu.HBM)

    pair_at = jnp.minimum(store_rank, PAIRS - 1) * 128
    weight = jnp.concatenate(
        [
            lax.dynamic_slice_in_dim(enc_key, pair_at, 128, axis=1),
            lax.dynamic_slice_in_dim(enc_value, pair_at, 128, axis=1),
        ],
        axis=1,
    )
    half = weight.shape[0] // 2
    a_four, b_four = stack_fours(
        around(weight[:half], side, False), around(weight[half:], side, True)
    )
    parts = around(a_four, side, True) + around(b_four, side, False)
    rel = jnp.array(REL, jnp.int32)
    y_at, z_at = seq_rank // side, seq_rank % side
    from_rank = jnp.concatenate([(y_at + rel + side) % side, (z_at + rel + side) % side])
    hidden_far = pltpu.with_memory_space_constraint(hidden, pltpu.HBM)
    queries = dot(hidden, w_query).astype(BF16)
    queries = pltpu.with_memory_space_constraint(queries, pltpu.HBM)
    cond = cond_rows(hidden_far, parts, from_rank, queries).reshape(-1, CH, 256)
    own_lane = around_x(cond, chips)
    chip, core = store_rank // 2, store_rank % 2
    lane = 2 * ((chip + rel + chips) % chips)
    pairs = jnp.concatenate([lane + core, lane + 1 - core])

    spans = (jnp.arange(span_count, dtype=jnp.int32) + FIRST) % span_count
    mine = jnp.sum(
        jnp.where(slot[None, :] == (KNB * spans + core)[:, None], pos[None, :], 0), axis=1
    )
    enc_query = pltpu.with_memory_space_constraint(enc_query, pltpu.HBM)
    enc_q = enc_queries(mine, gathered, enc_query)
    own_lane[1:] = hold(own_lane[1:], enc_q)
    conds = own_lane + [swap_cores(block) for block in own_lane]
    conds[4] = pltpu.with_memory_space_constraint(conds[4], pltpu.HBM)
    part = span_count // 2
    high = encode(0, part, mine, pairs, enc_q, gathered, conds, enc_out, ())
    high_other = swap_cores(high)
    low = encode(part, part, mine, pairs, enc_q, gathered, conds, enc_out, (high,))
    low_other = swap_cores(low)
    carried = tuple(
        lax.ppermute(
            low[:1],
            ("seq", "store"),
            [
                (i * store_count + k, (i + 1) * store_count + (k ^ flip))
                for i in range(seq_count - 1)
                for k in range(store_count)
            ],
        )
        for flip in range(2)
    )
    terms = decode(2, 2, high, high_other, queries, w_key, w_value, w_out, None, (), low)
    weights = (
        queries,
        w_key,
        pltpu.with_memory_space_constraint(w_value, pltpu.HBM),
        pltpu.with_memory_space_constraint(w_out, pltpu.HBM),
    )
    high_out = lax.psum_scatter(terms, "store", scatter_dimension=1, tiled=True)
    kept_1, given_1 = decode(1, 1, low, low_other, *weights, pairs, (), terms)
    taken_1 = swap_cores(given_1)
    kept_0, given_0 = decode(0, 1, low, low_other, *weights, pairs, carried, kept_1)
    taken_0 = swap_cores(given_0)
    sums_1 = core_sums(kept_1, taken_1, (kept_0,))
    got_1 = send_over_x(sums_1, chips)
    sums_0 = core_sums(kept_0, taken_0, sums_1[1:])
    got_0 = send_over_x(sums_0, chips)
    outs = []
    for sums, got in ((sums_0, got_0), (sums_1, got_1)):
        total = sums[0]
        for block in got:
            total = total + block.astype(F32)
        outs.append(total.astype(BF16))
    return jnp.concatenate([*outs, high_out], axis=0)


def solution(mesh):
    in_specs = (
        P("seq", None),
        P("store", None, None),
        P("seq", None),
        P(None, "store"),
        P(None, "store"),
        P(None, "store"),
        P("store", None),
        P(),
        P("seq", None),
        P("seq", None),
        P(),
    )
    out_specs = P("seq", "store")
    return jax.shard_map(body, mesh=mesh, in_specs=in_specs, out_specs=out_specs, check_vma=False)
```
